32 devices in a mesh: groups: 2 (over x), seq: 16 (over z, y, core).
Axes of the slice: x: 2, y: 2, z: 4, core: 2. Of those that a mesh axis runs over, the one named last changes fastest.
Arguments:
- x_true: float32 [3, 4096], P(None, ('groups', 'seq')), parts along dimension 1, may hold values from -96 to 96
- noise: float32 [8, 3, 2048], P('groups', None, 'seq'), parts along dimension 0, may hold values from -6 to 6
- noise_level: int32 [8], P('groups'), parts along dimension 0, may hold values from 0 to 199
- atom_single: bfloat16 [4096, 128], P(('groups', 'seq')), parts along dimension 0, may hold values from -6 to 6
- atom_token: int32 [4096], P(('groups', 'seq')), parts along dimension 0, may hold values from 0 to 255, as said below
- window_edges: int32 [128, 2], P(('groups', 'seq')), parts along dimension 0, may hold values from 0 to 2048, as said below
- atom_pair_bias: float32 [128, 4, 32, 128], P(('groups', 'seq')), parts along dimension 0, may hold values from -6 to 300
- token_single: float32 [512, 768], P(('groups', 'seq')), parts along dimension 0, may hold values from -6 to 6
- pair_bias: float32 [32, 256, 256], P('groups', 'seq'), parts along dimension 0, may hold values from -6 to 300
- w_coord: float32 [3, 128], replicated, may hold values from -3.5 to 3.5
- w_atom_qkv: bfloat16 [4, 128, 384], replicated, may hold values from -0.5 to 0.5
- w_atom_out: bfloat16 [4, 128, 128], replicated, may hold values from -0.5 to 0.5
- w_atom_up: bfloat16 [4, 128, 512], replicated, may hold values from -0.5 to 0.5
- w_atom_down: bfloat16 [4, 256, 128], replicated, may hold values from -0.375 to 0.375
- w_pool: bfloat16 [128, 768], replicated, may hold values from -0.5 to 0.5
- w_token_qkv: bfloat16 [768, 2304], replicated, may hold values from -0.21875 to 0.21875
- w_token_out: bfloat16 [768, 768], replicated, may hold values from -0.21875 to 0.21875
- w_back: bfloat16 [768, 128], replicated, may hold values from -0.21875 to 0.21875
- w_final: bfloat16 [3, 128], replicated, may hold values from -0.5 to 0.5
Outputs:
- denoised: float32 [8, 3, 2048], P('groups', None, 'seq'), parts along dimension 0
- token_state: float32 [8, 256, 768], P('groups', 'seq'), parts along dimension 0
The draws below stay inside these ranges and needn't reach their ends.
There are 2 independent parts, one for each index of `groups`. The reference program is written for one: setup_inputs(seed, part) draws one part's arguments, and reference() takes and returns one part's arrays. A program takes and returns all parts, laid end to end along the dimension named above; an argument that names none is the same for every part. Nothing has to cross between parts.
Inputs may be any that keep to these rules, and one draw needn't show every extreme that they name: `atom_token`: never falls along the atoms; every token has one or more atoms; the atoms of token t lie at or after atom 128 * (t // 16) - 48 and before atom 128 * (t // 16) + 128 + 128 * 3 // 8, so the atoms of shard d of the atoms name tokens of token shards d - 1, d and d + 1 only. For block b: max(0, 32 * b - 48) <= window_edges[b, 0] <= max(0, 32 * b - 48 + 48 // 3) and min(2048, 32 * b + 80 - 48 // 3) <= window_edges[b, 1] <= min(2048, 32 * b + 80).
All inputs are finite; a program needn't handle non-finite values.
Results may differ from the reference program's by a relative error of at most 0.008.
Values may be sent and summed in bfloat16 or wider, within the bound.
A program may use at most 128 MiB of HBM per device.

```python
import jax
import jax.numpy as jnp
from jax import lax

ATOM_WIDTH = 128
ATOM_HEADS = 4
TOKEN_WIDTH = 768
HEADS = 16
QUERY_BLOCK = 32
KEY_WINDOW = 128
ENC_LAYERS = 2
LEVELS = 200
SAMPLES = 4
ATOM_DEV = 128
TOK_DEV = 16
ATOMS = 2048
TOKENS = 256
ATOM_BLOCKS = 64
RIM = 48
LAYERS = 4


def draw_atom_token(key, part):
    shard_count = ATOMS // ATOM_DEV
    reach_limit = ATOM_DEV * 3 // 8
    shift_key, weight_key = jax.random.split(jax.random.fold_in(key, 11))
    shifts = jax.random.randint(shift_key, (shard_count,), -reach_limit, reach_limit + 1)
    shifts = jnp.where(jnp.arange(shard_count) == shard_count - 1, 0, shifts)
    earlier = jnp.concatenate([jnp.zeros((1,), jnp.int32), shifts[:-1]])
    totals = ATOM_DEV + shifts - earlier
    weights = jax.random.randint(weight_key, (shard_count, TOK_DEV), 1, 9)
    spare_atoms = totals - TOK_DEV
    counts = 1 + weights * spare_atoms[:, None] // jnp.sum(weights, 1, keepdims=True)
    missing = totals - jnp.sum(counts, 1)
    counts = counts + jnp.where(jnp.arange(TOK_DEV) == TOK_DEV - 1, 1, 0)[None, :] * missing[:, None]
    flat_counts = counts.reshape(-1)
    starts = jnp.cumsum(flat_counts) - flat_counts
    return (jnp.searchsorted(starts, jnp.arange(ATOMS), side='right') - 1).astype(jnp.int32)


def draw_window_edges(key, part):
    lower_key, upper_key = jax.random.split(jax.random.fold_in(key, 23))
    block_start = QUERY_BLOCK * jnp.arange(ATOM_BLOCKS)
    lower = jnp.maximum(block_start - RIM + jax.random.randint(lower_key, (ATOM_BLOCKS,), 0, RIM // 3 + 1), 0)
    upper = jnp.minimum(block_start + QUERY_BLOCK + RIM - jax.random.randint(upper_key, (ATOM_BLOCKS,), 0, RIM // 3 + 1), ATOMS)
    return jnp.stack([lower, upper], 1).astype(jnp.int32)


def biased_rows(key, array_shape):
    base_key = jax.random.fold_in(key, 0)
    return jnp.clip(jax.random.normal(base_key, array_shape, jnp.float32), -6.0, 6.0)


def draw_atom_pair_bias(key, part):
    return biased_rows(jax.random.fold_in(key, 31), (ATOM_BLOCKS, ATOM_HEADS, QUERY_BLOCK, KEY_WINDOW))


def draw_pair_bias(key, part):
    return biased_rows(jax.random.fold_in(key, 37), (HEADS, TOKENS, TOKENS))


def plant(entries, rng, least, top_value):
    longest = entries.shape.index(max(entries.shape))
    spots = []
    for shift in (0, 1):
        where = [jax.random.randint(jax.random.fold_in(rng, axis), (), 0, length) for axis, length in enumerate(entries.shape)]
        where[longest] = (where[longest] + shift) % entries.shape[longest]
        spots.append(tuple(where))
    return entries.at[spots[0]].set(least).at[spots[1]].set(top_value)


def block_scale(rng, extent, pieces, least, top_value):
    gain, own = 1.0, jax.random.fold_in(rng, 6)
    for dim, shards_of in pieces:
        steps = jnp.exp(jax.random.uniform(jax.random.fold_in(own, dim), (shards_of,), jnp.float32, least / len(pieces), top_value / len(pieces)))
        gain = gain * jnp.repeat(steps, extent[dim] // shards_of).reshape([-1 if axis == dim else 1 for axis in range(len(extent))])
    return gain


def scatter_about(rng, extent, scale, most, cuts=(), dtype=jnp.bfloat16):
    array = scale * jax.random.normal(rng, extent, jnp.float32)
    if cuts:
        array = array * block_scale(rng, extent, cuts, -0.22, 0.18)
    return jnp.clip(array, -most, most).astype(dtype)


def setup_inputs(seed: int = 0, part: int = 0) -> dict:
    streams_of = jax.random.split(jax.random.key(seed), 20)
    part_splits = jax.random.split(jax.random.fold_in(streams_of[19], part), 20)
    return {
        "x_true": scatter_about(part_splits[0], (3, ATOMS), 16.0, 96.0, ((1, 16),), jnp.float32),
        "noise": scatter_about(part_splits[1], (SAMPLES, 3, ATOMS), 1.0, 6.0, ((2, 16),), jnp.float32),
        "noise_level": plant(jax.random.randint(part_splits[2], (SAMPLES,), 0, LEVELS), jax.random.fold_in(part_splits[2], 1), 0, LEVELS - 1).astype(jnp.int32),
        "atom_single": scatter_about(part_splits[3], (ATOMS, ATOM_WIDTH), 1.0, 6.0, ((0, 16),)),
        "atom_token": draw_atom_token(jax.random.fold_in(jax.random.fold_in(streams_of[19], part), 71), part),
        "window_edges": draw_window_edges(jax.random.fold_in(jax.random.fold_in(streams_of[19], part), 71), part),
        "atom_pair_bias": draw_atom_pair_bias(jax.random.fold_in(jax.random.fold_in(streams_of[19], part), 71), part),
        "token_single": scatter_about(part_splits[7], (TOKENS, TOKEN_WIDTH), 1.0, 6.0, ((0, 16),), jnp.float32),
        "pair_bias": draw_pair_bias(jax.random.fold_in(jax.random.fold_in(streams_of[19], part), 71), part),
        "w_coord": scatter_about(streams_of[9], (3, ATOM_WIDTH), 3 ** -0.5, 3.5, (), jnp.float32),
        "w_atom_qkv": scatter_about(streams_of[10], (LAYERS, ATOM_WIDTH, 3 * ATOM_WIDTH), ATOM_WIDTH ** -0.5, 0.5),
        "w_atom_out": scatter_about(streams_of[11], (LAYERS, ATOM_WIDTH, ATOM_WIDTH), ATOM_WIDTH ** -0.5, 0.5),
        "w_atom_up": scatter_about(streams_of[12], (LAYERS, ATOM_WIDTH, 4 * ATOM_WIDTH), ATOM_WIDTH ** -0.5, 0.5),
        "w_atom_down": scatter_about(streams_of[13], (LAYERS, 2 * ATOM_WIDTH, ATOM_WIDTH), (2 * ATOM_WIDTH) ** -0.5, 0.375),
        "w_pool": scatter_about(streams_of[14], (ATOM_WIDTH, TOKEN_WIDTH), ATOM_WIDTH ** -0.5, 0.5),
        "w_token_qkv": scatter_about(streams_of[15], (TOKEN_WIDTH, 3 * TOKEN_WIDTH), TOKEN_WIDTH ** -0.5, 0.21875),
        "w_token_out": scatter_about(streams_of[16], (TOKEN_WIDTH, TOKEN_WIDTH), TOKEN_WIDTH ** -0.5, 0.21875),
        "w_back": scatter_about(streams_of[17], (TOKEN_WIDTH, ATOM_WIDTH), TOKEN_WIDTH ** -0.5, 0.21875),
        "w_final": scatter_about(streams_of[18], (3, ATOM_WIDTH), ATOM_WIDTH ** -0.5, 0.5),
    }


EPS = 1e-05
SIGMA_DATA = 16.0
HIGH = lax.Precision.HIGHEST

def normed(values):
    centre = lax.optimization_barrier(jnp.mean(values, -1, keepdims=True))
    centred = values - centre
    spread = lax.optimization_barrier(jnp.mean(centred * centred, -1, keepdims=True))
    return centred * lax.rsqrt(spread + EPS)

def noise_scale(noise_level):
    upper_root = 160.0 ** (1.0 / 7.0)
    lower_root = 0.0004 ** (1.0 / 7.0)
    fraction = noise_level.astype(jnp.float32) / (LEVELS - 1)
    return SIGMA_DATA * (upper_root + fraction * (lower_root - upper_root)) ** 7

def atom_layer(stream, layer_index, w_atom_qkv, w_atom_out, w_atom_up, w_atom_down, atom_pair_bias, window_edges):
    channels = stream.shape[-1]
    head_count = atom_pair_bias.shape[1]
    head_size = channels // head_count
    block_count = stream.shape[0] // QUERY_BLOCK
    normal_in = normed(stream).astype(jnp.bfloat16)
    projected = jnp.dot(normal_in, w_atom_qkv[layer_index], preferred_element_type=jnp.float32)
    queries = projected[:, :channels].astype(jnp.bfloat16)
    key_rows = jnp.pad(projected[:, channels:2 * channels].astype(jnp.bfloat16), ((RIM, RIM), (0, 0)))
    value_rows = jnp.pad(projected[:, 2 * channels:].astype(jnp.bfloat16), ((RIM, RIM), (0, 0)))
    window = QUERY_BLOCK * jnp.arange(block_count)[:, None] + jnp.arange(KEY_WINDOW)[None, :]
    key_win = key_rows[window].reshape(block_count, KEY_WINDOW, head_count, head_size).astype(jnp.float32)
    value_win = value_rows[window].reshape(block_count, KEY_WINDOW, head_count, head_size).astype(jnp.float32)
    query_blocks = queries.reshape(block_count, QUERY_BLOCK, head_count, head_size).astype(jnp.float32)
    scores = jnp.einsum('bqhd,bkhd->bhqk', query_blocks, key_win) * head_size ** (-0.5) + atom_pair_bias
    position = window - RIM
    allowed = (position >= window_edges[:, 0:1]) & (position < window_edges[:, 1:2])
    allowed_mask = allowed[:, None, None, :]
    row_max = lax.optimization_barrier(jnp.max(jnp.where(allowed_mask, scores, -jnp.inf), -1, keepdims=True))
    expo = jnp.where(allowed_mask, jnp.exp(scores - row_max), 0.0)
    attend = (expo / lax.optimization_barrier(jnp.sum(expo, -1, keepdims=True))).astype(jnp.bfloat16)
    mixed = jnp.einsum('bhqk,bkhd->bqhd', attend.astype(jnp.float32), value_win)
    mixed = mixed.reshape(stream.shape[0], channels).astype(jnp.bfloat16)
    stream = stream + jnp.dot(mixed, w_atom_out[layer_index], preferred_element_type=jnp.float32)
    normal_mid = normed(stream).astype(jnp.bfloat16)
    gated = jnp.dot(normal_mid, w_atom_up[layer_index], preferred_element_type=jnp.float32)
    hidden = (jax.nn.silu(gated[:, :2 * channels]) * gated[:, 2 * channels:]).astype(jnp.bfloat16)
    return stream + jnp.dot(hidden, w_atom_down[layer_index], preferred_element_type=jnp.float32)

def reference(x_true, noise, noise_level, atom_single, atom_token, window_edges, atom_pair_bias, token_single, pair_bias, w_coord, w_atom_qkv, w_atom_out, w_atom_up, w_atom_down, w_pool, w_token_qkv, w_token_out, w_back, w_final):
    sigma_all = noise_scale(noise_level)
    channels = token_single.shape[1]
    head_count = pair_bias.shape[0]
    head_size = channels // head_count
    token_count = token_single.shape[0]

    def one_sample(inputs):
        noise_one, sigma = inputs
        total = sigma * sigma + SIGMA_DATA * SIGMA_DATA
        noisy = x_true + sigma * noise_one
        scaled = noisy * lax.rsqrt(total)
        stream = atom_single.astype(jnp.float32) + scaled[0][:, None] * w_coord[0] + scaled[1][:, None] * w_coord[1] + scaled[2][:, None] * w_coord[2]
        for layer_index in range(ENC_LAYERS):
            stream = atom_layer(stream, layer_index, w_atom_qkv, w_atom_out, w_atom_up, w_atom_down, atom_pair_bias, window_edges)
        encoded = stream
        pooled_atoms = jax.nn.relu(jnp.dot(normed(encoded).astype(jnp.bfloat16), w_pool, preferred_element_type=jnp.float32))
        token_sums = jax.ops.segment_sum(pooled_atoms, atom_token, num_segments=token_count)
        token_counts = jax.ops.segment_sum(jnp.ones(atom_token.shape, jnp.float32), atom_token, num_segments=token_count)
        token_in = token_sums / token_counts[:, None] + token_single
        normal_tok = normed(token_in).astype(jnp.bfloat16)
        projected = jnp.dot(normal_tok, w_token_qkv, preferred_element_type=jnp.float32).astype(jnp.bfloat16)
        queries = projected[:, :channels].reshape(token_count, head_count, head_size).astype(jnp.float32)
        key_rows = projected[:, channels:2 * channels].reshape(token_count, head_count, head_size).astype(jnp.float32)
        value_rows = projected[:, 2 * channels:].reshape(token_count, head_count, head_size).astype(jnp.float32)
        scores = jnp.einsum('qhd,khd->hqk', queries, key_rows) * head_size ** (-0.5) + pair_bias
        row_max = lax.optimization_barrier(jnp.max(scores, -1, keepdims=True))
        expo = jnp.exp(scores - row_max)
        attend = expo / lax.optimization_barrier(jnp.sum(expo, -1, keepdims=True))
        mixed = jnp.einsum('hqk,khd->qhd', attend, value_rows, precision=HIGH)
        mixed = mixed.reshape(token_count, channels).astype(jnp.bfloat16)
        token_state = token_in + jnp.dot(mixed, w_token_out, preferred_element_type=jnp.float32)
        back_proj = jnp.dot(normed(token_state).astype(jnp.bfloat16), w_back, preferred_element_type=jnp.float32)
        stream = encoded + back_proj[atom_token]
        for layer_index in range(ENC_LAYERS, LAYERS):
            stream = atom_layer(stream, layer_index, w_atom_qkv, w_atom_out, w_atom_up, w_atom_down, atom_pair_bias, window_edges)
        update = jnp.dot(normed(stream).astype(jnp.bfloat16), w_final.T, preferred_element_type=jnp.float32).T
        denoised = (SIGMA_DATA * SIGMA_DATA / total * noisy + sigma * SIGMA_DATA * lax.rsqrt(total) * update) / SIGMA_DATA
        return (denoised, token_state)
    denoised, token_state = lax.map(one_sample, (noise, sigma_all))
    return (denoised, token_state)
```

```python
import functools

import jax
import jax.numpy as jnp
from jax import lax
from jax.experimental import pallas as pl
from jax.experimental.pallas import tpu as pltpu
from jax.sharding import PartitionSpec as P

QUERY_BLOCK = 32
KEY_WINDOW = 128
ENC_LAYERS = 2
LEVELS = 200
RIM = 48
LAYERS = 4
GROUPS = 2

EPS = 1e-05
SIGMA_DATA = 16.0
MESH = pl.DeviceIdType.MESH
F32 = jnp.float32
BF16 = jnp.bfloat16
LAST = (((1,), (1,)), ((), ()))
FIRST = (((0,), (0,)), ((), ()))


def normed(values):
    centred = values - jnp.mean(values, -1, keepdims=True)
    spread = jnp.mean(centred * centred, -1, keepdims=True)
    return centred * lax.rsqrt(spread + EPS)


def dot(a, b):
    return jnp.dot(a, b, preferred_element_type=F32)


def remote(src, dst, send, recv, target):
    return pltpu.make_async_remote_copy(
        src_ref=src,
        dst_ref=dst,
        send_sem=send,
        recv_sem=recv,
        device_id={"seq": target},
        device_id_type=MESH,
    )


def plan(n, heads, samples):
    per = heads * samples // n
    gs = samples // GROUPS
    pack = 2 if per % 2 == 0 else 1
    waves = GROUPS if per == samples and gs == pack else 1
    return per, pack, waves, per // pack // waves


def kernel(
    n,
    level_ref,
    edges_ref,
    x_true_ref,
    noise_ref,
    single_ref,
    atom_token_ref,
    bias_hbm,
    token_single_hbm,
    pair_hbm,
    w_coord_ref,
    w_qkv_hbm,
    w_out_hbm,
    w_up_hbm,
    w_down_hbm,
    w_pool_hbm,
    w_tqkv_hbm,
    w_tout_hbm,
    w_back_hbm,
    w_final_ref,
    denoised_ref,
    state_ref,
    stream,
    kv,
    queries,
    masked_bias,
    counts,
    own_sum,
    psend,
    precv,
    token_in,
    items,
    got,
    pair_buf,
    outs,
    returned,
    back,
    w_tqkv,
    w_tout,
    bias_ref,
    token_single_ref,
    w_qkv_ref,
    w_out_ref,
    w_up_ref,
    w_down_ref,
    w_pool_ref,
    w_back_ref,
    w_sem,
    late_sem,
    halo_send,
    halo_recv,
    count_send,
    count_recv,
    pool_send,
    pool_recv,
    pair_send,
    pair_recv,
    item_send,
    item_recv,
    out_send,
    out_recv,
    back_send,
    back_recv,
):
    samples = noise_ref.shape[1]
    atom_rows, width = single_ref.shape
    token_rows, channels = token_single_ref.shape
    blocks, atom_heads = bias_ref.shape[:2]
    atom_head = width // atom_heads
    heads = pair_hbm.shape[0]
    head_size = channels // heads
    tokens = n * token_rows
    gs = samples // GROUPS
    per, pack, waves, units = plan(n, heads, samples)
    wave_samples = samples // waves
    wave_rows = wave_samples * token_rows

    me = lax.axis_index("seq")
    right = lax.rem(me + 1, n)
    left = lax.rem(me + n - 1, n)
    has_left = me > 0
    has_right = me < n - 1

    barrier = pltpu.get_barrier_semaphore()

    def greet(k, c):
        pl.semaphore_signal(
            barrier, inc=1, device_id={"seq": lax.rem(me + k, n)}, device_id_type=MESH
        )
        return c

    lax.fori_loop(1, n, greet, 0)
    load_tqkv = pltpu.make_async_copy(w_tqkv_hbm, w_tqkv, w_sem.at[0])
    load_tout = pltpu.make_async_copy(w_tout_hbm, w_tout, w_sem.at[1])
    late = {}
    for slot, (name, src, dst) in enumerate(
        (
            ("qkv", w_qkv_hbm, w_qkv_ref),
            ("bias", bias_hbm, bias_ref),
            ("out", w_out_hbm, w_out_ref),
            ("up", w_up_hbm, w_up_ref),
            ("down", w_down_hbm, w_down_ref),
            ("pool", w_pool_hbm, w_pool_ref),
            ("single", token_single_hbm, token_single_ref),
            ("back", w_back_hbm, w_back_ref),
        )
    ):
        late[name] = pltpu.make_async_copy(src, dst, late_sem.at[slot])
        late[name].start()
    load_tqkv.start()
    load_tout.start()
    own_head = (me * per) // samples
    own_pair = pltpu.make_async_copy(pair_hbm.at[own_head], pair_buf.at[me], w_sem.at[2])
    own_pair.start()

    upper_root = 160.0 ** (1.0 / 7.0)
    lower_root = 0.0004 ** (1.0 / 7.0)

    def sigma_of(s):
        level = jnp.full((1, atom_rows), level_ref[s], jnp.int32).astype(F32)
        base = upper_root + level / (LEVELS - 1) * (lower_root - upper_root)
        square = base * base
        sigma = SIGMA_DATA * (square * square * square * base)
        return sigma, sigma * sigma + SIGMA_DATA * SIGMA_DATA

    def noisy_of(s, sigma):
        noise = jnp.concatenate([noise_ref[c, pl.ds(s, 1), :] for c in range(3)], axis=0)
        return x_true_ref[...] + sigma * noise

    scaled = []
    for s in range(samples):
        sigma, total = sigma_of(s)
        scaled.append(noisy_of(s, sigma) * lax.rsqrt(total))
    spare = atom_rows - 3 * samples
    columns = jnp.transpose(
        jnp.concatenate(scaled + [jnp.zeros((spare, atom_rows), F32)], axis=0)
    )
    single = single_ref[...].astype(F32)
    for s in range(samples):
        value = single
        for c in range(3):
            at = 3 * s + c
            value = value + columns[:, at : at + 1] * w_coord_ref[c : c + 1, :]
        stream[s // gs, pl.ds((s % gs) * atom_rows, atom_rows), :] = value

    relative = atom_token_ref[...] - (me - 1) * token_rows
    selector = (
        lax.broadcasted_iota(jnp.int32, (3 * token_rows, atom_rows), 0) == relative
    ).astype(F32)
    sel = selector.astype(BF16)
    counted = jnp.broadcast_to(jnp.sum(selector, 1, keepdims=True), (3 * token_rows, 128))
    for j in range(3):
        counts[j] = counted[j * token_rows : (j + 1) * token_rows].astype(BF16)

    def exchange(to_right, to_left, begin):
        if begin:

            @pl.when(has_right)
            def _():
                to_right.start()

            @pl.when(has_left)
            def _():
                to_left.start()

        else:

            @pl.when(has_left)
            def _():
                to_right.wait_recv()
                to_left.wait_send()

            @pl.when(has_right)
            def _():
                to_left.wait_recv()
                to_right.wait_send()

    def halo(layer, g):
        return (
            remote(
                kv.at[layer, g, :, pl.ds(atom_rows, RIM), :],
                kv.at[layer, g, :, pl.ds(0, RIM), :],
                halo_send.at[layer, g, 0],
                halo_recv.at[layer, g, 0],
                right,
            ),
            remote(
                kv.at[layer, g, :, pl.ds(RIM, RIM), :],
                kv.at[layer, g, :, pl.ds(RIM + atom_rows, RIM), :],
                halo_send.at[layer, g, 1],
                halo_recv.at[layer, g, 1],
                left,
            ),
        )

    def project(layer, g):
        normal_in = normed(stream[g]).astype(BF16)
        key_value = dot(normal_in, w_qkv_ref[layer, :, width:]).astype(BF16)
        for i in range(gs):
            kv[layer, g, i, RIM : RIM + atom_rows, :] = key_value[
                i * atom_rows : (i + 1) * atom_rows
            ]
        queries[g] = dot(normal_in, w_qkv_ref[layer, :, :width]).astype(BF16)

    def send_halo(layer, g):
        exchange(*halo(layer, g), True)

    stacked = atom_heads * QUERY_BLOCK
    row_head = lax.broadcasted_iota(jnp.int32, (stacked, width), 0) // QUERY_BLOCK
    lane_head = lax.broadcasted_iota(jnp.int32, (stacked, width), 1) // atom_head
    own_lanes = row_head == lane_head
    few_lanes = lane_head[:QUERY_BLOCK]
    scale = atom_head ** (-0.5)
    ones = jnp.ones((KEY_WINDOW, width), BF16)

    def attend(layer, g):
        exchange(*halo(layer, g), False)
        mixed = []
        pairs = [(i, b) for i in range(gs) for b in range(blocks)]
        for start in range(0, len(pairs), 8):
            part = pairs[start : start + 8]
            scores = []
            for i, b in part:
                q = queries[g, pl.ds(i * atom_rows + b * QUERY_BLOCK, QUERY_BLOCK), :]
                q = jnp.concatenate([q] * atom_heads, axis=0)
                q = jnp.where(own_lanes, q, jnp.zeros_like(q))
                key_win = kv[layer, g, i, QUERY_BLOCK * b : QUERY_BLOCK * b + KEY_WINDOW, :width]
                score = lax.dot_general(q, key_win, LAST, preferred_element_type=F32)
                scores.append(score * scale + masked_bias[b])
            tops = [jnp.max(score, -1, keepdims=True) for score in scores]
            expos = [jnp.exp(score - top).astype(BF16) for score, top in zip(scores, tops)]
            sums = []
            for (i, b), expo in zip(part, expos):
                value_win = kv[layer, g, i, QUERY_BLOCK * b : QUERY_BLOCK * b + KEY_WINDOW, width:]
                sums.append(dot(expo, jnp.concatenate([value_win, ones], axis=1)))
            for both in sums:
                picked = both[:QUERY_BLOCK]
                number, below = picked[:, :width], picked[:, width:]
                for h in range(1, atom_heads):
                    rows = both[h * QUERY_BLOCK : (h + 1) * QUERY_BLOCK]
                    number = jnp.where(few_lanes == h, rows[:, :width], number)
                    below = jnp.where(few_lanes == h, rows[:, width:], below)
                mixed.append((number / below).astype(BF16))
        mixed = jnp.concatenate(mixed, axis=0)
        value = stream[g] + dot(mixed, w_out_ref[layer])
        normal_mid = normed(value).astype(BF16)
        gated = dot(normal_mid, w_up_ref[layer])
        gate = gated[:, : 2 * width]
        hidden = (gate / (1.0 + jnp.exp(-gate)) * gated[:, 2 * width :]).astype(BF16)
        value = value + dot(hidden, w_down_ref[layer])
        stream[g] = value
        return value

    def pool_copy(g):
        return (
            remote(
                psend.at[g, 1], precv.at[g, 0], pool_send.at[g, 0], pool_recv.at[g, 0], right
            ),
            remote(psend.at[g, 0], precv.at[g, 1], pool_send.at[g, 1], pool_recv.at[g, 1], left),
        )

    def count_copy():
        return (
            remote(counts.at[2], counts.at[3], count_send.at[0], count_recv.at[0], right),
            remote(counts.at[0], counts.at[4], count_send.at[1], count_recv.at[1], left),
        )

    def back_copy(t):
        return (
            remote(back.at[t, 1], back.at[t, 0], back_send.at[t, 0], back_recv.at[t, 0], right),
            remote(back.at[t, 1], back.at[t, 2], back_send.at[t, 1], back_recv.at[t, 1], left),
        )

    def run_pair(first, finish):
        def step(g, c):
            attend(first, g)
            project(first + 1, g)
            send_halo(first + 1, g)
            return c

        lax.fori_loop(0, GROUPS, step, 0)

        def last(g, c):
            finish(g, attend(first + 1, g))
            return c

        lax.fori_loop(0, GROUPS, last, 0)

    late["qkv"].wait()
    project(0, 0)
    pl.semaphore_wait(barrier, n - 1)
    send_halo(0, 0)
    exchange(*count_copy(), True)
    project(0, 1)
    send_halo(0, 1)

    def pair_copy(target, slot):
        return remote(
            pair_hbm.at[(target * per) // samples],
            pair_buf.at[slot],
            pair_send.at[target],
            pair_recv.at[slot],
            target,
        )

    def pair_start(k, c):
        pair_copy(lax.rem(me + k, n), me).start()
        return c

    lax.fori_loop(1, n, pair_start, 0)

    def pool(g, value):
        pooled = jnp.maximum(dot(normed(value).astype(BF16), w_pool_ref[...]), 0.0)
        high = pooled.astype(BF16)
        low = (pooled - high.astype(F32)).astype(BF16)
        for i in range(gs):
            at = slice(i * atom_rows, (i + 1) * atom_rows)
            part = dot(sel, high[at]) + dot(sel, low[at])
            psend[g, 0, i] = part[:token_rows].astype(BF16)
            own_sum[g, i] = part[token_rows : 2 * token_rows]
            psend[g, 1, i] = part[2 * token_rows :].astype(BF16)
        exchange(*pool_copy(g), True)

    late["bias"].wait()
    place = lax.broadcasted_iota(jnp.int32, (1, KEY_WINDOW), 1)
    for b in range(blocks):
        position = me * atom_rows - RIM + QUERY_BLOCK * b + place
        allowed = (position >= edges_ref[0, b]) & (position < edges_ref[1, b])
        masked_bias[b] = jnp.where(
            allowed, bias_ref[b].reshape(atom_heads * QUERY_BLOCK, KEY_WINDOW), -1e30
        )

    @pl.when(jnp.logical_not(has_left))
    def _():
        for layer in range(LAYERS):
            for g in range(GROUPS):
                kv[layer, g, :, 0:RIM, :] = jnp.zeros((gs, RIM, 2 * width), BF16)
        for g in range(GROUPS):
            precv[g, 0] = jnp.zeros(precv.shape[2:], BF16)
        for t in range(waves):
            back[t, 0] = jnp.zeros(back.shape[2:], BF16)
        counts[3] = jnp.zeros(counts.shape[1:], BF16)

    @pl.when(jnp.logical_not(has_right))
    def _():
        for layer in range(LAYERS):
            for g in range(GROUPS):
                kv[layer, g, :, RIM + atom_rows :, :] = jnp.zeros((gs, RIM, 2 * width), BF16)
        for g in range(GROUPS):
            precv[g, 1] = jnp.zeros(precv.shape[2:], BF16)
        for t in range(waves):
            back[t, 2] = jnp.zeros(back.shape[2:], BF16)
        counts[4] = jnp.zeros(counts.shape[1:], BF16)

    for name in ("out", "up", "down", "pool"):
        late[name].wait()
    run_pair(0, pool)
    late["single"].wait()
    late["back"].wait()

    exchange(*count_copy(), False)
    number_of = (
        counts[1].astype(F32)[:, :1] + counts[3].astype(F32)[:, :1] + counts[4].astype(F32)[:, :1]
    )
    lanes = 128
    half = lanes // 2
    lane = lax.broadcasted_iota(jnp.int32, (token_rows, lanes), 1)

    def moved(block, start, to):
        tile, off = start // lanes, start % lanes
        shift = (to - off) % lanes

        def turned(t):
            part = block[:, t * lanes : (t + 1) * lanes]
            return part if shift == 0 else pltpu.roll(part, shift, 1)

        if off + head_size <= lanes:
            return turned(tile)
        return jnp.where(lane < to + lanes - off, turned(tile), turned(tile + 1))

    def spread(copy_of, begin):
        def step(k, c):
            other = lax.rem(me + k, n)
            if begin:
                copy_of(other, me).start()
            else:
                copy = copy_of(other, other)
                copy.wait_send()
                copy.wait_recv()
            return c

        lax.fori_loop(1, n, step, 0)

    def item_copy(t):
        return lambda target, slot: remote(
            items.at[t, target],
            got.at[t, slot],
            item_send.at[t, target],
            item_recv.at[t, slot],
            target,
        )

    def out_copy(t):
        return lambda target, slot: remote(
            outs.at[t, target],
            returned.at[t, slot],
            out_send.at[t, target],
            out_recv.at[t, slot],
            target,
        )

    def token_project(t):
        for g in range(GROUPS) if waves == 1 else (t,):
            exchange(*pool_copy(g), False)
        for a in range(wave_samples):
            s = t * wave_samples + a
            g, i = s // gs, s % gs
            sums = own_sum[g, i] + precv[g, 0, i].astype(F32) + precv[g, 1, i].astype(F32)
            token_in[s * token_rows : (s + 1) * token_rows, :] = (
                sums / number_of + token_single_ref[...]
            )
        normal_tok = normed(token_in[t * wave_rows : (t + 1) * wave_rows, :]).astype(BF16)
        parts = [
            dot(normal_tok, w_tqkv[:, j * channels : (j + 1) * channels]) for j in range(3)
        ]
        for h in range(heads):
            start = h * head_size
            for a in range(0, wave_samples, pack):
                keys = []
                for p in range(pack):
                    item = h * samples + t * wave_samples + a + p
                    owner, unit = item // per, item % per // pack - t * units
                    at = slice((a + p) * token_rows, (a + p + 1) * token_rows)
                    v = moved(parts[2][at], start, half * p)
                    q = moved(parts[0][at], start, half * (1 - p))
                    keys.append(moved(parts[1][at], start, half * (1 - p)))
                    low, high = (v, q) if p == 0 else (q, v)
                    tile = jnp.where(lane < head_size, low, jnp.where(lane < half, 1.0, high))
                    items[t, owner, unit, p * token_rows : (p + 1) * token_rows, :] = tile.astype(
                        BF16
                    )
                key = keys[0] if pack == 1 else jnp.where(lane < half, keys[1], keys[0])
                items[t, owner, unit, pack * token_rows :, :] = key.astype(BF16)
        spread(item_copy(t), True)
        got[t, me] = items[t, me]

    token_scale = head_size ** (-0.5)
    tile = 16
    key_lane = lax.broadcasted_iota(jnp.int32, (tokens, lanes), 1)
    out_lane = lax.broadcasted_iota(jnp.int32, (tile * token_rows, lanes), 1)

    def token_attend(t):
        spread(item_copy(t), False)
        for unit in range(units):
            packed = got[t, :, unit, pack * token_rows :, :].reshape(tokens, lanes)

            def one(block, c):
                span = pl.ds(block * tile, tile)
                ratios = []
                for p in range(pack):
                    at = slice(p * token_rows, (p + 1) * token_rows)
                    mine = key_lane < head_size
                    if p == 0:
                        mine = (key_lane >= half) & (key_lane < half + head_size)
                    keys = jnp.where(mine, packed, jnp.zeros_like(packed))
                    values = got[t, :, unit, at, :].reshape(tokens, lanes)
                    q = got[t, span, unit, at, :].reshape(tile * token_rows, lanes)
                    scores = lax.dot_general(q, keys, LAST, preferred_element_type=F32)
                    scores = scores * token_scale + pair_buf[span].reshape(
                        tile * token_rows, tokens
                    )
                    expo = jnp.exp(scores - jnp.max(scores, -1, keepdims=True)).astype(BF16)
                    both = dot(expo, values)
                    ratios.append(both / both[:, head_size : head_size + 1])
                ratio = ratios[0] if pack == 1 else jnp.where(out_lane < half, *ratios)
                outs[t, span, unit, :, :] = ratio.astype(BF16).reshape(tile, token_rows, lanes)
                return c

            if n == tile:
                one(0, 0)
            else:
                lax.fori_loop(0, n // tile, one, 0)
        spread(out_copy(t), True)
        returned[t, me] = outs[t, me]

    def token_finish(t):
        spread(out_copy(t), False)
        state = token_in[t * wave_rows : (t + 1) * wave_rows, :]
        for h in range(heads):
            mix = []
            for a in range(wave_samples):
                item = h * samples + t * wave_samples + a
                owner, unit, p = item // per, item % per // pack - t * units, item % per % pack
                block = returned[t, owner, unit]
                if p == 1:
                    block = pltpu.roll(block.astype(F32), half, 1).astype(BF16)
                mix.append(block[:, :head_size])
            state = state + dot(
                jnp.concatenate(mix, axis=0), w_tout[h * head_size : (h + 1) * head_size, :]
            )
        for a in range(wave_samples):
            state_ref[t * wave_samples + a] = state[a * token_rows : (a + 1) * token_rows]
        back[t, 1] = dot(normed(state).astype(BF16), w_back_ref[...]).astype(BF16)
        exchange(*back_copy(t), True)

    load_tqkv.wait()
    for t in range(waves):
        token_project(t)
    own_pair.wait()
    spread(pair_copy, False)
    for t in range(waves):
        token_attend(t)
    load_tout.wait()
    for t in range(waves):
        token_finish(t)
    first = ENC_LAYERS
    for g in range(GROUPS):
        for t in range(waves):
            if g * waves // GROUPS == t and (waves == GROUPS or g == 0):
                exchange(*back_copy(t), False)
        for i in range(gs):
            s = g * gs + i
            t, at = s // wave_samples, s % wave_samples * token_rows
            near = jnp.concatenate([back[t, j, at : at + token_rows, :] for j in range(3)], axis=0)
            picked = lax.dot_general(sel, near, FIRST, preferred_element_type=F32)
            stream[g, i * atom_rows : (i + 1) * atom_rows, :] += picked
        project(first, g)
        send_halo(first, g)

    def finish(g, value):
        normal = normed(value).astype(BF16)
        for i in range(gs):
            s = g * gs + i
            update = lax.dot_general(
                w_final_ref[...],
                normal[i * atom_rows : (i + 1) * atom_rows],
                LAST,
                preferred_element_type=F32,
            )
            sigma, total = sigma_of(s)
            result = (
                SIGMA_DATA * SIGMA_DATA / total * noisy_of(s, sigma)
                + sigma * SIGMA_DATA * lax.rsqrt(total) * update
            ) / SIGMA_DATA
            for c in range(3):
                denoised_ref[c, pl.ds(s, 1), :] = result[c : c + 1]

    run_pair(first, finish)


def store(denoised_ref, state_ref, denoised_out, state_out, sem):
    copies = (
        pltpu.make_async_copy(state_ref, state_out, sem.at[0]),
        pltpu.make_async_copy(denoised_ref, denoised_out, sem.at[1]),
    )
    for copy in copies:
        copy.start()
    for copy in copies:
        copy.wait()


def shards(
    n,
    x_true,
    noise,
    noise_level,
    atom_single,
    atom_token,
    window_edges,
    atom_pair_bias,
    token_single,
    pair_bias,
    w_coord,
    w_atom_qkv,
    w_atom_out,
    w_atom_up,
    w_atom_down,
    w_pool,
    w_token_qkv,
    w_token_out,
    w_back,
    w_final,
):
    samples = noise.shape[0]
    atom_rows, width = atom_single.shape
    token_rows, channels = token_single.shape
    blocks, atom_heads = atom_pair_bias.shape[:2]
    heads = pair_bias.shape[0]
    gs = samples // GROUPS
    per, pack, waves, units = plan(n, heads, samples)
    vmem = pl.BlockSpec(memory_space=pltpu.VMEM)
    smem = pl.BlockSpec(memory_space=pltpu.SMEM)
    anywhere = pl.BlockSpec(memory_space=pl.ANY)
    dma = pltpu.SemaphoreType.DMA
    held = pl.pallas_call(
        functools.partial(kernel, n),
        name="denoise",
        out_shape=(
            pltpu.VMEM((3, samples, atom_rows), F32),
            pltpu.VMEM((samples, token_rows, channels), F32),
        ),
        in_specs=[smem, smem]
        + [vmem] * 4
        + [anywhere] * 3
        + [vmem]
        + [anywhere] * 8
        + [vmem],
        out_specs=(vmem, vmem),
        scratch_shapes=[
            pltpu.VMEM((GROUPS, gs * atom_rows, width), F32),
            pltpu.VMEM((LAYERS, GROUPS, gs, atom_rows + 2 * RIM, 2 * width), BF16),
            pltpu.VMEM((GROUPS, gs * atom_rows, width), BF16),
            pltpu.VMEM((blocks, atom_heads * QUERY_BLOCK, KEY_WINDOW), F32),
            pltpu.VMEM((5, token_rows, 128), BF16),
            pltpu.VMEM((GROUPS, gs, token_rows, channels), F32),
            pltpu.VMEM((GROUPS, 2, gs, token_rows, channels), BF16),
            pltpu.VMEM((GROUPS, 2, gs, token_rows, channels), BF16),
            pltpu.VMEM((samples * token_rows, channels), F32),
            pltpu.VMEM((waves, n, units, (pack + 1) * token_rows, 128), BF16),
            pltpu.VMEM((waves, n, units, (pack + 1) * token_rows, 128), BF16),
            pltpu.VMEM((n, token_rows, n * token_rows), F32),
            pltpu.VMEM((waves, n, units, token_rows, 128), BF16),
            pltpu.VMEM((waves, n, units, token_rows, 128), BF16),
            pltpu.VMEM((waves, 3, samples // waves * token_rows, width), BF16),
            pltpu.VMEM(w_token_qkv.shape, BF16),
            pltpu.VMEM(w_token_out.shape, BF16),
            pltpu.VMEM(atom_pair_bias.shape, F32),
            pltpu.VMEM(token_single.shape, F32),
            pltpu.VMEM(w_atom_qkv.shape, BF16),
            pltpu.VMEM(w_atom_out.shape, BF16),
            pltpu.VMEM(w_atom_up.shape, BF16),
            pltpu.VMEM(w_atom_down.shape, BF16),
            pltpu.VMEM(w_pool.shape, BF16),
            pltpu.VMEM(w_back.shape, BF16),
            dma((3,)),
            dma((8,)),
            dma((LAYERS, GROUPS, 2)),
            dma((LAYERS, GROUPS, 2)),
            dma((2,)),
            dma((2,)),
            dma((GROUPS, 2)),
            dma((GROUPS, 2)),
            dma((n,)),
            dma((n,)),
            dma((waves, n)),
            dma((waves, n)),
            dma((waves, n)),
            dma((waves, n)),
            dma((waves, 2)),
            dma((waves, 2)),
        ],
        compiler_params=pltpu.CompilerParams(
            collective_id=0, has_side_effects=True, vmem_limit_bytes=56 * 1024 * 1024
        ),
    )(
        noise_level,
        window_edges.T,
        x_true,
        noise.transpose(1, 0, 2),
        atom_single,
        atom_token.reshape(1, atom_rows),
        atom_pair_bias,
        token_single,
        pair_bias,
        w_coord,
        w_atom_qkv,
        w_atom_out,
        w_atom_up,
        w_atom_down,
        w_pool,
        w_token_qkv,
        w_token_out,
        w_back,
        w_final,
    )
    denoised, state = pl.pallas_call(
        store,
        name="store",
        out_shape=(
            jax.ShapeDtypeStruct((3, samples, atom_rows), F32),
            jax.ShapeDtypeStruct((samples, token_rows, channels), F32),
        ),
        in_specs=[vmem] * 2,
        out_specs=(anywhere, anywhere),
        scratch_shapes=[dma((2,))],
    )(*[pltpu.with_memory_space_constraint(x, pltpu.VMEM) for x in held])
    return denoised.transpose(1, 0, 2), state


def solution(mesh):
    in_specs = (
        P(None, ("groups", "seq")),
        P("groups", None, "seq"),
        P("groups"),
        P(("groups", "seq"), None),
        P(("groups", "seq")),
        P(("groups", "seq"), None),
        P(("groups", "seq"), None, None, None),
        P(("groups", "seq"), None),
        P("groups", "seq", None),
    ) + (P(),) * 10
    out_specs = (P("groups", None, "seq"), P("groups", "seq", None))
    return jax.shard_map(
        functools.partial(shards, mesh.shape["seq"]),
        mesh=mesh,
        in_specs=in_specs,
        out_specs=out_specs,
        check_vma=False,
    )
```

```python
import functools

import jax
import jax.numpy as jnp
from jax import lax
from jax.experimental import pallas as pl
from jax.experimental.pallas import tpu as pltpu
from jax.sharding import PartitionSpec as P

QUERY_BLOCK = 32
KEY_WINDOW = 128
ENC_LAYERS = 2
LEVELS = 200
RIM = 48
LAYERS = 4
GROUPS = 2

EPS = 1e-05
SIGMA_DATA = 16.0
MESH = pl.DeviceIdType.MESH
F32 = jnp.float32
BF16 = jnp.bfloat16
LAST = (((1,), (1,)), ((), ()))
FIRST = (((0,), (0,)), ((), ()))


def normed(values):
    centred = values - jnp.mean(values, -1, keepdims=True)
    spread = jnp.mean(centred * centred, -1, keepdims=True)
    return centred * lax.rsqrt(spread + EPS)


def dot(a, b):
    return jnp.dot(a, b, preferred_element_type=F32)


def remote(src, dst, send, recv, target):
    return pltpu.make_async_remote_copy(
        src_ref=src,
        dst_ref=dst,
        send_sem=send,
        recv_sem=recv,
        device_id={"seq": target},
        device_id_type=MESH,
    )


def plan(n, heads, samples):
    per = heads * samples // n
    gs = samples // GROUPS
    pack = 2 if per % 2 == 0 else 1
    waves = GROUPS if per == samples and gs == pack else 1
    return per, pack, waves, per // pack // waves


def kernel(
    n,
    level_hbm,
    edges_hbm,
    x_true_hbm,
    noise_hbm,
    single_hbm,
    atom_token_hbm,
    bias_hbm,
    token_single_hbm,
    pair_hbm,
    w_coord_hbm,
    w_qkv_hbm,
    w_out_hbm,
    w_up_hbm,
    w_down_hbm,
    w_pool_hbm,
    w_tqkv_hbm,
    w_tout_hbm,
    w_back_hbm,
    w_final_hbm,
    denoised_ref,
    state_ref,
    level_ref,
    edges_ref,
    x_true_ref,
    noise_ref,
    single_ref,
    atom_token_ref,
    w_coord_ref,
    w_final_ref,
    stream,
    kv,
    queries,
    masked_bias,
    counts,
    own_sum,
    psend,
    precv,
    token_in,
    items,
    got,
    pair_buf,
    outs,
    returned,
    back,
    w_tqkv,
    w_tout,
    bias_ref,
    token_single_ref,
    w_qkv_ref,
    w_out_ref,
    w_up_ref,
    w_down_ref,
    w_pool_ref,
    w_back_ref,
    load_sem,
    halo_send,
    halo_recv,
    count_send,
    count_recv,
    pool_send,
    pool_recv,
    pair_send,
    pair_recv,
    item_send,
    item_recv,
    out_send,
    out_recv,
    back_send,
    back_recv,
):
    samples = noise_ref.shape[1]
    atom_rows, width = single_ref.shape
    token_rows, channels = token_single_ref.shape
    blocks, atom_heads = bias_ref.shape[:2]
    atom_head = width // atom_heads
    heads = pair_hbm.shape[0]
    head_size = channels // heads
    tokens = n * token_rows
    gs = samples // GROUPS
    per, pack, waves, units = plan(n, heads, samples)
    wave_samples = samples // waves
    wave_rows = wave_samples * token_rows

    me = lax.axis_index("seq")
    right = lax.rem(me + 1, n)
    left = lax.rem(me + n - 1, n)
    has_left = me > 0
    has_right = me < n - 1

    barrier = pltpu.get_barrier_semaphore()

    def greet(k, c):
        pl.semaphore_signal(
            barrier, inc=1, device_id={"seq": lax.rem(me + k, n)}, device_id_type=MESH
        )
        return c

    own_head = (me * per) // samples
    loads = {}
    for slot, (name, src, dst) in enumerate(
        (
            ("level", level_hbm, level_ref),
            ("x_true", x_true_hbm, x_true_ref),
            ("noise", noise_hbm, noise_ref),
            ("atoms", single_hbm, single_ref),
            ("coord", w_coord_hbm, w_coord_ref),
            ("qkv", w_qkv_hbm, w_qkv_ref),
            ("atom_token", atom_token_hbm, atom_token_ref),
            ("edges", edges_hbm, edges_ref),
            ("bias", bias_hbm, bias_ref),
            ("out", w_out_hbm, w_out_ref),
            ("up", w_up_hbm, w_up_ref),
            ("down", w_down_hbm, w_down_ref),
            ("pool", w_pool_hbm, w_pool_ref),
            ("single", token_single_hbm, token_single_ref),
            ("tqkv", w_tqkv_hbm, w_tqkv),
            ("back", w_back_hbm, w_back_ref),
            ("tout", w_tout_hbm, w_tout),
            ("final", w_final_hbm, w_final_ref),
            ("own_pair", pair_hbm.at[own_head], pair_buf.at[me]),
        )
    ):
        loads[name] = pltpu.make_async_copy(src, dst, load_sem.at[slot])
        loads[name].start()
        if name == "qkv":
            lax.fori_loop(1, n, greet, 0)

    upper_root = 160.0 ** (1.0 / 7.0)
    lower_root = 0.0004 ** (1.0 / 7.0)

    def sigma_of(s):
        level = jnp.full((1, atom_rows), level_ref[s], jnp.int32).astype(F32)
        base = upper_root + level / (LEVELS - 1) * (lower_root - upper_root)
        square = base * base
        sigma = SIGMA_DATA * (square * square * square * base)
        return sigma, sigma * sigma + SIGMA_DATA * SIGMA_DATA

    def noisy_of(s, sigma):
        noise = jnp.concatenate([noise_ref[c, pl.ds(s, 1), :] for c in range(3)], axis=0)
        return x_true_ref[...] + sigma * noise

    for name in ("level", "x_true", "noise"):
        loads[name].wait()
    scaled = []
    for s in range(samples):
        sigma, total = sigma_of(s)
        scaled.append(noisy_of(s, sigma) * lax.rsqrt(total))
    spare = atom_rows - 3 * samples
    columns = jnp.transpose(
        jnp.concatenate(scaled + [jnp.zeros((spare, atom_rows), F32)], axis=0)
    )
    loads["atoms"].wait()
    loads["coord"].wait()
    single = single_ref[...].astype(F32)
    for s in range(samples):
        value = single
        for c in range(3):
            at = 3 * s + c
            value = value + columns[:, at : at + 1] * w_coord_ref[c : c + 1, :]
        stream[s // gs, pl.ds((s % gs) * atom_rows, atom_rows), :] = value

    def exchange(to_right, to_left, begin):
        if begin:

            @pl.when(has_right)
            def _():
                to_right.start()

            @pl.when(has_left)
            def _():
                to_left.start()

        else:

            @pl.when(has_left)
            def _():
                to_right.wait_recv()

            @pl.when(has_right)
            def _():
                to_left.wait_recv()

    def sent(to_right, to_left):
        @pl.when(has_right)
        def _():
            to_right.wait_send()

        @pl.when(has_left)
        def _():
            to_left.wait_send()

    def halo(layer, g):
        return (
            remote(
                kv.at[layer, g, :, pl.ds(atom_rows, RIM), :],
                kv.at[layer, g, :, pl.ds(0, RIM), :],
                halo_send.at[0],
                halo_recv.at[layer, g, 0],
                right,
            ),
            remote(
                kv.at[layer, g, :, pl.ds(RIM, RIM), :],
                kv.at[layer, g, :, pl.ds(RIM + atom_rows, RIM), :],
                halo_send.at[1],
                halo_recv.at[layer, g, 1],
                left,
            ),
        )

    def project(layer, g):
        normal_in = normed(stream[g]).astype(BF16)
        key_value = dot(normal_in, w_qkv_ref[layer, :, width:]).astype(BF16)
        for i in range(gs):
            kv[layer, g, i, RIM : RIM + atom_rows, :] = key_value[
                i * atom_rows : (i + 1) * atom_rows
            ]
        queries[g] = dot(normal_in, w_qkv_ref[layer, :, :width]).astype(BF16)

    def send_halo(layer, g):
        exchange(*halo(layer, g), True)

    stacked = atom_heads * QUERY_BLOCK
    row_head = lax.broadcasted_iota(jnp.int32, (stacked, width), 0) // QUERY_BLOCK
    lane_head = lax.broadcasted_iota(jnp.int32, (stacked, width), 1) // atom_head
    own_lanes = row_head == lane_head
    few_lanes = lane_head[:QUERY_BLOCK]
    scale = atom_head ** (-0.5)
    ones = jnp.ones((KEY_WINDOW, width), BF16)

    def attend(layer, g):
        exchange(*halo(layer, g), False)
        mixed = []
        pairs = [(i, b) for i in range(gs) for b in range(blocks)]
        for start in range(0, len(pairs), 8):
            part = pairs[start : start + 8]
            scores = []
            for i, b in part:
                q = queries[g, pl.ds(i * atom_rows + b * QUERY_BLOCK, QUERY_BLOCK), :]
                q = jnp.concatenate([q] * atom_heads, axis=0)
                q = jnp.where(own_lanes, q, jnp.zeros_like(q))
                key_win = kv[layer, g, i, QUERY_BLOCK * b : QUERY_BLOCK * b + KEY_WINDOW, :width]
                score = lax.dot_general(q, key_win, LAST, preferred_element_type=F32)
                scores.append(score * scale + masked_bias[b])
            tops = [jnp.max(score, -1, keepdims=True) for score in scores]
            expos = [jnp.exp(score - top).astype(BF16) for score, top in zip(scores, tops)]
            sums = []
            for (i, b), expo in zip(part, expos):
                value_win = kv[layer, g, i, QUERY_BLOCK * b : QUERY_BLOCK * b + KEY_WINDOW, width:]
                sums.append(dot(expo, jnp.concatenate([value_win, ones], axis=1)))
            for both in sums:
                picked = both[:QUERY_BLOCK]
                number, below = picked[:, :width], picked[:, width:]
                for h in range(1, atom_heads):
                    rows = both[h * QUERY_BLOCK : (h + 1) * QUERY_BLOCK]
                    number = jnp.where(few_lanes == h, rows[:, :width], number)
                    below = jnp.where(few_lanes == h, rows[:, width:], below)
                mixed.append((number / below).astype(BF16))
        mixed = jnp.concatenate(mixed, axis=0)
        value = stream[g] + dot(mixed, w_out_ref[layer])
        normal_mid = normed(value).astype(BF16)
        gated = dot(normal_mid, w_up_ref[layer])
        gate = gated[:, : 2 * width]
        hidden = (gate / (1.0 + jnp.exp(-gate)) * gated[:, 2 * width :]).astype(BF16)
        value = value + dot(hidden, w_down_ref[layer])
        stream[g] = value
        return value

    def pool_copy(g):
        return (
            remote(
                psend.at[g, 1], precv.at[g, 0], pool_send.at[0], pool_recv.at[g, 0], right
            ),
            remote(psend.at[g, 0], precv.at[g, 1], pool_send.at[1], pool_recv.at[g, 1], left),
        )

    def count_copy():
        return (
            remote(counts.at[2], counts.at[3], count_send.at[0], count_recv.at[0], right),
            remote(counts.at[0], counts.at[4], count_send.at[1], count_recv.at[1], left),
        )

    def back_copy(t):
        return (
            remote(back.at[t, 1], back.at[t, 0], back_send.at[0], back_recv.at[t, 0], right),
            remote(back.at[t, 1], back.at[t, 2], back_send.at[1], back_recv.at[t, 1], left),
        )

    def run_pair(first, finish):
        def step(g, c):
            attend(first, g)
            project(first + 1, g)
            send_halo(first + 1, g)
            return c

        lax.fori_loop(0, GROUPS, step, 0)

        def last(g, c):
            finish(g, attend(first + 1, g))
            return c

        lax.fori_loop(0, GROUPS, last, 0)

    loads["qkv"].wait()
    project(0, 0)
    pl.semaphore_wait(barrier, n - 1)
    send_halo(0, 0)
    project(0, 1)
    send_halo(0, 1)
    loads["atom_token"].wait()
    relative = atom_token_ref[...] - (me - 1) * token_rows
    selector = (
        lax.broadcasted_iota(jnp.int32, (3 * token_rows, atom_rows), 0) == relative
    ).astype(F32)
    sel = selector.astype(BF16)
    counted = jnp.broadcast_to(jnp.sum(selector, 1, keepdims=True), (3 * token_rows, 128))
    for j in range(3):
        counts[j] = counted[j * token_rows : (j + 1) * token_rows].astype(BF16)

    exchange(*count_copy(), True)

    def pair_copy(target, slot):
        return remote(
            pair_hbm.at[(target * per) // samples],
            pair_buf.at[slot],
            pair_send,
            pair_recv,
            target,
        )

    def pair_start(k, c):
        pair_copy(lax.rem(me + k, n), me).start()
        return c

    lax.fori_loop(1, n, pair_start, 0)

    def pool(g, value):
        pooled = jnp.maximum(dot(normed(value).astype(BF16), w_pool_ref[...]), 0.0)
        high = pooled.astype(BF16)
        low = (pooled - high.astype(F32)).astype(BF16)
        for i in range(gs):
            at = slice(i * atom_rows, (i + 1) * atom_rows)
            part = dot(sel, high[at]) + dot(sel, low[at])
            psend[g, 0, i] = part[:token_rows].astype(BF16)
            own_sum[g, i] = part[token_rows : 2 * token_rows]
            psend[g, 1, i] = part[2 * token_rows :].astype(BF16)
        exchange(*pool_copy(g), True)

    loads["bias"].wait()
    loads["edges"].wait()
    place = lax.broadcasted_iota(jnp.int32, (1, KEY_WINDOW), 1)
    for b in range(blocks):
        position = me * atom_rows - RIM + QUERY_BLOCK * b + place
        allowed = (position >= edges_ref[0, b]) & (position < edges_ref[1, b])
        masked_bias[b] = jnp.where(
            allowed, bias_ref[b].reshape(atom_heads * QUERY_BLOCK, KEY_WINDOW), -1e30
        )

    @pl.when(jnp.logical_not(has_left))
    def _():
        for layer in range(LAYERS):
            for g in range(GROUPS):
                kv[layer, g, :, 0:RIM, :] = jnp.zeros((gs, RIM, 2 * width), BF16)
        for g in range(GROUPS):
            precv[g, 0] = jnp.zeros(precv.shape[2:], BF16)
        for t in range(waves):
            back[t, 0] = jnp.zeros(back.shape[2:], BF16)
        counts[3] = jnp.zeros(counts.shape[1:], BF16)

    @pl.when(jnp.logical_not(has_right))
    def _():
        for layer in range(LAYERS):
            for g in range(GROUPS):
                kv[layer, g, :, RIM + atom_rows :, :] = jnp.zeros((gs, RIM, 2 * width), BF16)
        for g in range(GROUPS):
            precv[g, 1] = jnp.zeros(precv.shape[2:], BF16)
        for t in range(waves):
            back[t, 2] = jnp.zeros(back.shape[2:], BF16)
        counts[4] = jnp.zeros(counts.shape[1:], BF16)

    for name in ("out", "up", "down", "pool"):
        loads[name].wait()
    run_pair(0, pool)
    loads["single"].wait()
    loads["back"].wait()

    exchange(*count_copy(), False)
    number_of = (
        counts[1].astype(F32)[:, :1] + counts[3].astype(F32)[:, :1] + counts[4].astype(F32)[:, :1]
    )
    lanes = 128
    half = lanes // 2
    lane = lax.broadcasted_iota(jnp.int32, (token_rows, lanes), 1)

    def moved(block, start, to):
        tile, off = start // lanes, start % lanes
        shift = (to - off) % lanes

        def turned(t):
            part = block[:, t * lanes : (t + 1) * lanes]
            return part if shift == 0 else pltpu.roll(part, shift, 1)

        if off + head_size <= lanes:
            return turned(tile)
        return jnp.where(lane < to + lanes - off, turned(tile), turned(tile + 1))

    def spread(copy_of):
        def step(k, c):
            copy_of(lax.rem(me + k, n), me).start()
            return c

        lax.fori_loop(1, n, step, 0)

    others = pl.ds(0, n - 1)

    def every_pair():
        return remote(
            pair_buf.at[others], pair_buf.at[others], pair_send, pair_recv, right
        )

    def item_copy(t):
        return lambda target, slot: remote(
            items.at[t, target], got.at[t, slot], item_send, item_recv.at[t], target
        )

    def every_item(t):
        return remote(
            items.at[t, others], got.at[t, others], item_send, item_recv.at[t], right
        )

    def out_copy(t):
        return lambda target, slot: remote(
            outs.at[t, target], returned.at[t, slot], out_send, out_recv.at[t], target
        )

    def every_out(t):
        return remote(
            outs.at[t, others], returned.at[t, others], out_send, out_recv.at[t], right
        )

    def token_project(t):
        for g in range(GROUPS) if waves == 1 else (t,):
            exchange(*pool_copy(g), False)
        for a in range(wave_samples):
            s = t * wave_samples + a
            g, i = s // gs, s % gs
            sums = own_sum[g, i] + precv[g, 0, i].astype(F32) + precv[g, 1, i].astype(F32)
            token_in[s * token_rows : (s + 1) * token_rows, :] = (
                sums / number_of + token_single_ref[...]
            )
        normal_tok = normed(token_in[t * wave_rows : (t + 1) * wave_rows, :]).astype(BF16)
        parts = [
            dot(normal_tok, w_tqkv[:, j * channels : (j + 1) * channels]) for j in range(3)
        ]
        for h in range(heads):
            start = h * head_size
            for a in range(0, wave_samples, pack):
                keys = []
                for p in range(pack):
                    item = h * samples + t * wave_samples + a + p
                    owner, unit = item // per, item % per // pack - t * units
                    at = slice((a + p) * token_rows, (a + p + 1) * token_rows)
                    v = moved(parts[2][at], start, half * p)
                    q = moved(parts[0][at], start, half * (1 - p))
                    keys.append(moved(parts[1][at], start, half * (1 - p)))
                    low, high = (v, q) if p == 0 else (q, v)
                    tile = jnp.where(lane < head_size, low, jnp.where(lane < half, 1.0, high))
                    items[t, owner, unit, p * token_rows : (p + 1) * token_rows, :] = tile.astype(
                        BF16
                    )
                key = keys[0] if pack == 1 else jnp.where(lane < half, keys[1], keys[0])
                items[t, owner, unit, pack * token_rows :, :] = key.astype(BF16)
        spread(item_copy(t))
        got[t, me] = items[t, me]

    token_scale = head_size ** (-0.5)
    tile = 16
    key_lane = lax.broadcasted_iota(jnp.int32, (tokens, lanes), 1)
    out_lane = lax.broadcasted_iota(jnp.int32, (tile * token_rows, lanes), 1)

    def token_attend(t):
        every_item(t).wait_recv()
        for unit in range(units):
            packed = got[t, :, unit, pack * token_rows :, :].reshape(tokens, lanes)

            def one(block, c):
                span = pl.ds(block * tile, tile)
                ratios = []
                for p in range(pack):
                    at = slice(p * token_rows, (p + 1) * token_rows)
                    mine = key_lane < head_size
                    if p == 0:
                        mine = (key_lane >= half) & (key_lane < half + head_size)
                    keys = jnp.where(mine, packed, jnp.zeros_like(packed))
                    values = got[t, :, unit, at, :].reshape(tokens, lanes)
                    q = got[t, span, unit, at, :].reshape(tile * token_rows, lanes)
                    scores = lax.dot_general(q, keys, LAST, preferred_element_type=F32)
                    scores = scores * token_scale + pair_buf[span].reshape(
                        tile * token_rows, tokens
                    )
                    expo = jnp.exp(scores - jnp.max(scores, -1, keepdims=True)).astype(BF16)
                    both = dot(expo, values)
                    ratios.append(both / both[:, head_size : head_size + 1])
                ratio = ratios[0] if pack == 1 else jnp.where(out_lane < half, *ratios)
                outs[t, span, unit, :, :] = ratio.astype(BF16).reshape(tile, token_rows, lanes)
                return c

            if n == tile:
                one(0, 0)
            else:
                lax.fori_loop(0, n // tile, one, 0)
        spread(out_copy(t))
        returned[t, me] = outs[t, me]

    def token_finish(t):
        every_out(t).wait_recv()
        state = token_in[t * wave_rows : (t + 1) * wave_rows, :]
        for h in range(heads):
            mix = []
            for a in range(wave_samples):
                item = h * samples + t * wave_samples + a
                owner, unit, p = item // per, item % per // pack - t * units, item % per % pack
                block = returned[t, owner, unit]
                if p == 1:
                    block = pltpu.roll(block.astype(F32), half, 1).astype(BF16)
                mix.append(block[:, :head_size])
            state = state + dot(
                jnp.concatenate(mix, axis=0), w_tout[h * head_size : (h + 1) * head_size, :]
            )
        for a in range(wave_samples):
            state_ref[t * wave_samples + a] = state[a * token_rows : (a + 1) * token_rows]
        back[t, 1] = dot(normed(state).astype(BF16), w_back_ref[...]).astype(BF16)
        exchange(*back_copy(t), True)

    loads["tqkv"].wait()
    for t in range(waves):
        token_project(t)
    loads["own_pair"].wait()
    every_pair().wait_recv()
    for t in range(waves):
        token_attend(t)
    loads["tout"].wait()
    for t in range(waves):
        token_finish(t)
    first = ENC_LAYERS
    for g in range(GROUPS):
        for t in range(waves):
            if g * waves // GROUPS == t and (waves == GROUPS or g == 0):
                exchange(*back_copy(t), False)
        for i in range(gs):
            s = g * gs + i
            t, at = s // wave_samples, s % wave_samples * token_rows
            near = jnp.concatenate([back[t, j, at : at + token_rows, :] for j in range(3)], axis=0)
            picked = lax.dot_general(sel, near, FIRST, preferred_element_type=F32)
            stream[g, i * atom_rows : (i + 1) * atom_rows, :] += picked
        project(first, g)
        send_halo(first, g)

    def finish(g, value):
        normal = normed(value).astype(BF16)
        for i in range(gs):
            s = g * gs + i
            update = lax.dot_general(
                w_final_ref[...],
                normal[i * atom_rows : (i + 1) * atom_rows],
                LAST,
                preferred_element_type=F32,
            )
            sigma, total = sigma_of(s)
            result = (
                SIGMA_DATA * SIGMA_DATA / total * noisy_of(s, sigma)
                + sigma * SIGMA_DATA * lax.rsqrt(total) * update
            ) / SIGMA_DATA
            for c in range(3):
                denoised_ref[c, pl.ds(s, 1), :] = result[c : c + 1]

    loads["final"].wait()
    run_pair(first, finish)

    sent(
        remote(
            kv.at[:, :, :, pl.ds(0, RIM), :],
            kv.at[:, :, :, pl.ds(0, RIM), :],
            halo_send.at[0],
            halo_recv.at[0, 0, 0],
            right,
        ),
        remote(
            kv.at[:, :, :, pl.ds(0, RIM), :],
            kv.at[:, :, :, pl.ds(0, RIM), :],
            halo_send.at[1],
            halo_recv.at[0, 0, 1],
            left,
        ),
    )
    sent(*count_copy())
    sent(
        remote(psend.at[:, 1], precv.at[:, 0], pool_send.at[0], pool_recv.at[0, 0], right),
        remote(psend.at[:, 0], precv.at[:, 1], pool_send.at[1], pool_recv.at[0, 1], left),
    )
    sent(
        remote(back.at[:, 1], back.at[:, 0], back_send.at[0], back_recv.at[0, 0], right),
        remote(back.at[:, 1], back.at[:, 2], back_send.at[1], back_recv.at[0, 1], left),
    )
    every_pair().wait_send()
    for t in range(waves):
        every_item(t).wait_send()
        every_out(t).wait_send()


def store(denoised_ref, state_ref, denoised_out, state_out, sem):
    copies = (
        pltpu.make_async_copy(state_ref, state_out, sem.at[0]),
        pltpu.make_async_copy(denoised_ref, denoised_out, sem.at[1]),
    )
    for copy in copies:
        copy.start()
    for copy in copies:
        copy.wait()


def shards(
    n,
    x_true,
    noise,
    noise_level,
    atom_single,
    atom_token,
    window_edges,
    atom_pair_bias,
    token_single,
    pair_bias,
    w_coord,
    w_atom_qkv,
    w_atom_out,
    w_atom_up,
    w_atom_down,
    w_pool,
    w_token_qkv,
    w_token_out,
    w_back,
    w_final,
):
    samples = noise.shape[0]
    atom_rows, width = atom_single.shape
    token_rows, channels = token_single.shape
    blocks, atom_heads = atom_pair_bias.shape[:2]
    heads = pair_bias.shape[0]
    gs = samples // GROUPS
    per, pack, waves, units = plan(n, heads, samples)
    vmem = pl.BlockSpec(memory_space=pltpu.VMEM)
    anywhere = pl.BlockSpec(memory_space=pl.ANY)
    dma = pltpu.SemaphoreType.DMA
    held = pl.pallas_call(
        functools.partial(kernel, n),
        name="denoise",
        out_shape=(
            pltpu.VMEM((3, samples, atom_rows), F32),
            pltpu.VMEM((samples, token_rows, channels), F32),
        ),
        in_specs=[anywhere] * 19,
        out_specs=(vmem, vmem),
        scratch_shapes=[
            pltpu.SMEM((samples,), jnp.int32),
            pltpu.SMEM((2, blocks), jnp.int32),
            pltpu.VMEM(x_true.shape, F32),
            pltpu.VMEM((3, samples, atom_rows), F32),
            pltpu.VMEM(atom_single.shape, BF16),
            pltpu.VMEM((1, atom_rows), jnp.int32),
            pltpu.VMEM(w_coord.shape, F32),
            pltpu.VMEM(w_final.shape, BF16),
            pltpu.VMEM((GROUPS, gs * atom_rows, width), F32),
            pltpu.VMEM((LAYERS, GROUPS, gs, atom_rows + 2 * RIM, 2 * width), BF16),
            pltpu.VMEM((GROUPS, gs * atom_rows, width), BF16),
            pltpu.VMEM((blocks, atom_heads * QUERY_BLOCK, KEY_WINDOW), F32),
            pltpu.VMEM((5, token_rows, 128), BF16),
            pltpu.VMEM((GROUPS, gs, token_rows, channels), F32),
            pltpu.VMEM((GROUPS, 2, gs, token_rows, channels), BF16),
            pltpu.VMEM((GROUPS, 2, gs, token_rows, channels), BF16),
            pltpu.VMEM((samples * token_rows, channels), F32),
            pltpu.VMEM((waves, n, units, (pack + 1) * token_rows, 128), BF16),
            pltpu.VMEM((waves, n, units, (pack + 1) * token_rows, 128), BF16),
            pltpu.VMEM((n, token_rows, n * token_rows), F32),
            pltpu.VMEM((waves, n, units, token_rows, 128), BF16),
            pltpu.VMEM((waves, n, units, token_rows, 128), BF16),
            pltpu.VMEM((waves, 3, samples // waves * token_rows, width), BF16),
            pltpu.VMEM(w_token_qkv.shape, BF16),
            pltpu.VMEM(w_token_out.shape, BF16),
            pltpu.VMEM(atom_pair_bias.shape, F32),
            pltpu.VMEM(token_single.shape, F32),
            pltpu.VMEM(w_atom_qkv.shape, BF16),
            pltpu.VMEM(w_atom_out.shape, BF16),
            pltpu.VMEM(w_atom_up.shape, BF16),
            pltpu.VMEM(w_atom_down.shape, BF16),
            pltpu.VMEM(w_pool.shape, BF16),
            pltpu.VMEM(w_back.shape, BF16),
            dma((19,)),
            dma((2,)),
            dma((LAYERS, GROUPS, 2)),
            dma((2,)),
            dma((2,)),
            dma((2,)),
            dma((GROUPS, 2)),
            dma(()),
            dma(()),
            dma(()),
            dma((waves,)),
            dma(()),
            dma((waves,)),
            dma((2,)),
            dma((waves, 2)),
        ],
        compiler_params=pltpu.CompilerParams(
            collective_id=0, has_side_effects=True, vmem_limit_bytes=56 * 1024 * 1024
        ),
    )(
        noise_level,
        window_edges.T,
        x_true,
        noise.transpose(1, 0, 2),
        atom_single,
        atom_token.reshape(1, atom_rows),
        atom_pair_bias,
        token_single,
        pair_bias,
        w_coord,
        w_atom_qkv,
        w_atom_out,
        w_atom_up,
        w_atom_down,
        w_pool,
        w_token_qkv,
        w_token_out,
        w_back,
        w_final,
    )
    denoised, state = pl.pallas_call(
        store,
        name="store",
        out_shape=(
            jax.ShapeDtypeStruct((3, samples, atom_rows), F32),
            jax.ShapeDtypeStruct((samples, token_rows, channels), F32),
        ),
        in_specs=[vmem] * 2,
        out_specs=(anywhere, anywhere),
        scratch_shapes=[dma((2,))],
    )(*[pltpu.with_memory_space_constraint(x, pltpu.VMEM) for x in held])
    return denoised.transpose(1, 0, 2), state


def solution(mesh):
    in_specs = (
        P(None, ("groups", "seq")),
        P("groups", None, "seq"),
        P("groups"),
        P(("groups", "seq"), None),
        P(("groups", "seq")),
        P(("groups", "seq"), None),
        P(("groups", "seq"), None, None, None),
        P(("groups", "seq"), None),
        P("groups", "seq", None),
    ) + (P(),) * 10
    out_specs = (P("groups", None, "seq"), P("groups", "seq", None))
    return jax.shard_map(
        functools.partial(shards, mesh.shape["seq"]),
        mesh=mesh,
        in_specs=in_specs,
        out_specs=out_specs,
        check_vma=False,
    )
```

```python
import functools

import jax
import jax.numpy as jnp
from jax import lax
from jax.experimental import pallas as pl
from jax.experimental.pallas import tpu as pltpu
from jax.sharding import PartitionSpec as P

QUERY_BLOCK = 32
KEY_WINDOW = 128
ENC_LAYERS = 2
LEVELS = 200
RIM = 48
LAYERS = 4
GROUPS = 2

EPS = 1e-05
SIGMA_DATA = 16.0
MESH = pl.DeviceIdType.MESH
F32 = jnp.float32
BF16 = jnp.bfloat16
LAST = (((1,), (1,)), ((), ()))
FIRST = (((0,), (0,)), ((), ()))


def normed(values):
    centred = values - jnp.mean(values, -1, keepdims=True)
    spread = jnp.mean(centred * centred, -1, keepdims=True)
    return centred * lax.rsqrt(spread + EPS)


def dot(a, b):
    return jnp.dot(a, b, preferred_element_type=F32)


def remote(src, dst, send, recv, target):
    return pltpu.make_async_remote_copy(
        src_ref=src,
        dst_ref=dst,
        send_sem=send,
        recv_sem=recv,
        device_id={"seq": target},
        device_id_type=MESH,
    )


def plan(n, heads, samples):
    per = heads * samples // n
    gs = samples // GROUPS
    pack = 2 if per % 2 == 0 else 1
    waves = GROUPS if per == samples and gs == pack else 1
    return per, pack, waves, per // pack // waves


def item_rows(token_rows, pack, waves):
    if waves == 1:
        return ((pack + 1) * token_rows,)
    return 2 * token_rows, 2 * token_rows + token_rows // 2


def kernel(
    n,
    level_hbm,
    edges_hbm,
    x_true_hbm,
    noise_hbm,
    single_hbm,
    atom_token_hbm,
    bias_hbm,
    token_single_hbm,
    pair_hbm,
    w_coord_hbm,
    w_qkv_hbm,
    w_out_hbm,
    w_up_hbm,
    w_down_hbm,
    w_pool_hbm,
    w_tqkv_hbm,
    w_tout_hbm,
    w_back_hbm,
    w_final_hbm,
    denoised_ref,
    state_ref,
    level_ref,
    edges_ref,
    x_true_ref,
    noise_ref,
    single_ref,
    atom_token_ref,
    w_coord_ref,
    w_final_ref,
    stream,
    kv,
    queries,
    masked_bias,
    counts,
    own_sum,
    psend,
    precv,
    token_in,
    items,
    got,
    held,
    weights,
    pair_buf,
    outs,
    returned,
    back,
    w_tqkv,
    w_tout,
    bias_ref,
    token_single_ref,
    w_qkv_ref,
    w_out_ref,
    w_up_ref,
    w_down_ref,
    w_pool_ref,
    w_back_ref,
    load_sem,
    halo_send,
    halo_recv,
    count_send,
    count_recv,
    pool_send,
    pool_recv,
    pair_send,
    pair_recv,
    item_send,
    item_recv,
    out_send,
    out_recv,
    back_send,
    back_recv,
):
    samples = noise_ref.shape[1]
    atom_rows, width = single_ref.shape
    token_rows, channels = token_single_ref.shape
    blocks, atom_heads = bias_ref.shape[:2]
    atom_head = width // atom_heads
    heads = pair_hbm.shape[0]
    head_size = channels // heads
    tokens = n * token_rows
    gs = samples // GROUPS
    per, pack, waves, units = plan(n, heads, samples)
    wave_samples = samples // waves
    wave_rows = wave_samples * token_rows

    me = lax.axis_index("seq")
    right = lax.rem(me + 1, n)
    left = lax.rem(me + n - 1, n)
    has_left = me > 0
    has_right = me < n - 1

    barrier = pltpu.get_barrier_semaphore()

    def greet(k, c):
        pl.semaphore_signal(
            barrier, inc=1, device_id={"seq": lax.rem(me + k, n)}, device_id_type=MESH
        )
        return c

    own_head = (me * per) // samples
    loads = {}
    for slot, (name, src, dst) in enumerate(
        (
            ("level", level_hbm, level_ref),
            ("x_true", x_true_hbm, x_true_ref),
            ("noise", noise_hbm, noise_ref),
            ("atoms", single_hbm, single_ref),
            ("coord", w_coord_hbm, w_coord_ref),
            ("qkv", w_qkv_hbm, w_qkv_ref),
            ("atom_token", atom_token_hbm, atom_token_ref),
            ("edges", edges_hbm, edges_ref),
            ("bias", bias_hbm, bias_ref),
            ("out", w_out_hbm, w_out_ref),
            ("up", w_up_hbm, w_up_ref),
            ("down", w_down_hbm, w_down_ref),
            ("pool", w_pool_hbm, w_pool_ref),
            ("single", token_single_hbm, token_single_ref),
            ("tqkv", w_tqkv_hbm, w_tqkv),
            ("back", w_back_hbm, w_back_ref),
            ("tout", w_tout_hbm, w_tout),
            ("final", w_final_hbm, w_final_ref),
            ("own_pair", pair_hbm.at[own_head], pair_buf.at[me]),
        )
    ):
        loads[name] = pltpu.make_async_copy(src, dst, load_sem.at[slot])
        loads[name].start()
        if name == "qkv":
            lax.fori_loop(1, n, greet, 0)

    upper_root = 160.0 ** (1.0 / 7.0)
    lower_root = 0.0004 ** (1.0 / 7.0)

    def sigma_of(s):
        level = jnp.full((1, atom_rows), level_ref[s], jnp.int32).astype(F32)
        base = upper_root + level / (LEVELS - 1) * (lower_root - upper_root)
        square = base * base
        sigma = SIGMA_DATA * (square * square * square * base)
        return sigma, sigma * sigma + SIGMA_DATA * SIGMA_DATA

    def noisy_of(s, sigma):
        noise = jnp.concatenate([noise_ref[c, pl.ds(s, 1), :] for c in range(3)], axis=0)
        return x_true_ref[...] + sigma * noise

    for name in ("level", "x_true", "noise"):
        loads[name].wait()
    scaled = []
    for s in range(samples):
        sigma, total = sigma_of(s)
        scaled.append(noisy_of(s, sigma) * lax.rsqrt(total))
    spare = atom_rows - 3 * samples
    columns = jnp.transpose(
        jnp.concatenate(scaled + [jnp.zeros((spare, atom_rows), F32)], axis=0)
    )
    loads["atoms"].wait()
    loads["coord"].wait()
    single = single_ref[...].astype(F32)
    for s in range(samples):
        value = single
        for c in range(3):
            at = 3 * s + c
            value = value + columns[:, at : at + 1] * w_coord_ref[c : c + 1, :]
        stream[s // gs, pl.ds((s % gs) * atom_rows, atom_rows), :] = value

    def exchange(to_right, to_left, begin):
        if begin:

            @pl.when(has_right)
            def _():
                to_right.start()

            @pl.when(has_left)
            def _():
                to_left.start()

        else:

            @pl.when(has_left)
            def _():
                to_right.wait_recv()

            @pl.when(has_right)
            def _():
                to_left.wait_recv()

    def sent(to_right, to_left):
        @pl.when(has_right)
        def _():
            to_right.wait_send()

        @pl.when(has_left)
        def _():
            to_left.wait_send()

    def halo(layer, g):
        return (
            remote(
                kv.at[layer, g, :, pl.ds(atom_rows, RIM), :],
                kv.at[layer, g, :, pl.ds(0, RIM), :],
                halo_send.at[0],
                halo_recv.at[layer, g, 0],
                right,
            ),
            remote(
                kv.at[layer, g, :, pl.ds(RIM, RIM), :],
                kv.at[layer, g, :, pl.ds(RIM + atom_rows, RIM), :],
                halo_send.at[1],
                halo_recv.at[layer, g, 1],
                left,
            ),
        )

    def project(layer, g):
        normal_in = normed(stream[g]).astype(BF16)
        key_value = dot(normal_in, w_qkv_ref[layer, :, width:]).astype(BF16)
        for i in range(gs):
            kv[layer, g, i, RIM : RIM + atom_rows, :] = key_value[
                i * atom_rows : (i + 1) * atom_rows
            ]
        queries[g] = dot(normal_in, w_qkv_ref[layer, :, :width]).astype(BF16)

    def send_halo(layer, g):
        exchange(*halo(layer, g), True)

    stacked = atom_heads * QUERY_BLOCK
    row_head = lax.broadcasted_iota(jnp.int32, (stacked, width), 0) // QUERY_BLOCK
    lane_head = lax.broadcasted_iota(jnp.int32, (stacked, width), 1) // atom_head
    own_lanes = row_head == lane_head
    few_lanes = lane_head[:QUERY_BLOCK]
    scale = atom_head ** (-0.5)
    ones = jnp.ones((KEY_WINDOW, width), BF16)

    def attend(layer, g):
        exchange(*halo(layer, g), False)
        mixed = []
        pairs = [(i, b) for i in range(gs) for b in range(blocks)]
        for start in range(0, len(pairs), 8):
            part = pairs[start : start + 8]
            scores = []
            for i, b in part:
                q = queries[g, pl.ds(i * atom_rows + b * QUERY_BLOCK, QUERY_BLOCK), :]
                q = jnp.concatenate([q] * atom_heads, axis=0)
                q = jnp.where(own_lanes, q, jnp.zeros_like(q))
                key_win = kv[layer, g, i, QUERY_BLOCK * b : QUERY_BLOCK * b + KEY_WINDOW, :width]
                score = lax.dot_general(q, key_win, LAST, preferred_element_type=F32)
                scores.append(score * scale + masked_bias[b])
            tops = [jnp.max(score, -1, keepdims=True) for score in scores]
            expos = [jnp.exp(score - top).astype(BF16) for score, top in zip(scores, tops)]
            sums = []
            for (i, b), expo in zip(part, expos):
                value_win = kv[layer, g, i, QUERY_BLOCK * b : QUERY_BLOCK * b + KEY_WINDOW, width:]
                sums.append(dot(expo, jnp.concatenate([value_win, ones], axis=1)))
            for both in sums:
                picked = both[:QUERY_BLOCK]
                number, below = picked[:, :width], picked[:, width:]
                for h in range(1, atom_heads):
                    rows = both[h * QUERY_BLOCK : (h + 1) * QUERY_BLOCK]
                    number = jnp.where(few_lanes == h, rows[:, :width], number)
                    below = jnp.where(few_lanes == h, rows[:, width:], below)
                mixed.append((number / below).astype(BF16))
        mixed = jnp.concatenate(mixed, axis=0)
        value = stream[g] + dot(mixed, w_out_ref[layer])
        normal_mid = normed(value).astype(BF16)
        gated = dot(normal_mid, w_up_ref[layer])
        gate = gated[:, : 2 * width]
        hidden = (gate / (1.0 + jnp.exp(-gate)) * gated[:, 2 * width :]).astype(BF16)
        value = value + dot(hidden, w_down_ref[layer])
        stream[g] = value
        return value

    def pool_copy(g):
        return (
            remote(
                psend.at[g, 1], precv.at[g, 0], pool_send.at[0], pool_recv.at[g, 0], right
            ),
            remote(psend.at[g, 0], precv.at[g, 1], pool_send.at[1], pool_recv.at[g, 1], left),
        )

    def count_copy():
        return (
            remote(counts.at[2], counts.at[3], count_send.at[0], count_recv.at[0], right),
            remote(counts.at[0], counts.at[4], count_send.at[1], count_recv.at[1], left),
        )

    def back_copy(t):
        return (
            remote(back.at[t, 1], back.at[t, 0], back_send.at[0], back_recv.at[t, 0], right),
            remote(back.at[t, 1], back.at[t, 2], back_send.at[1], back_recv.at[t, 1], left),
        )

    def run_pair(first, finish):
        def step(g, c):
            attend(first, g)
            project(first + 1, g)
            send_halo(first + 1, g)
            if first == 0:
                pair_batch(g)
            return c

        lax.fori_loop(0, GROUPS, step, 0)

        def last(g, c):
            finish(g, attend(first + 1, g))
            if first == 0:

                @pl.when(g == 0)
                def _():
                    pair_batch(2)

            return c

        lax.fori_loop(0, GROUPS, last, 0)

    loads["qkv"].wait()
    project(0, 0)
    pl.semaphore_wait(barrier, n - 1)
    send_halo(0, 0)
    project(0, 1)
    send_halo(0, 1)
    loads["atom_token"].wait()
    relative = atom_token_ref[...] - (me - 1) * token_rows
    selector = (
        lax.broadcasted_iota(jnp.int32, (3 * token_rows, atom_rows), 0) == relative
    ).astype(F32)
    sel = selector.astype(BF16)
    counted = jnp.broadcast_to(jnp.sum(selector, 1, keepdims=True), (3 * token_rows, 128))
    for j in range(3):
        counts[j] = counted[j * token_rows : (j + 1) * token_rows].astype(BF16)

    exchange(*count_copy(), True)

    def pair_copy(target, slot):
        return remote(
            pair_hbm.at[(target * per) // samples],
            pair_buf.at[slot],
            pair_send,
            pair_recv,
            target,
        )

    def pair_start(k, c):
        pair_copy(lax.rem(me + k, n), me).start()
        return c

    third = (n - 1) // 3

    def pair_batch(number):
        low = 1 + number * third
        high = jnp.where(number == 2, n, low + third)
        lax.fori_loop(low, high, pair_start, 0)

    def pool(g, value):
        pooled = jnp.maximum(dot(normed(value).astype(BF16), w_pool_ref[...]), 0.0)
        high = pooled.astype(BF16)
        low = (pooled - high.astype(F32)).astype(BF16)
        for i in range(gs):
            at = slice(i * atom_rows, (i + 1) * atom_rows)
            part = dot(sel, high[at]) + dot(sel, low[at])
            psend[g, 0, i] = part[:token_rows].astype(BF16)
            own_sum[g, i] = part[token_rows : 2 * token_rows]
            psend[g, 1, i] = part[2 * token_rows :].astype(BF16)
        exchange(*pool_copy(g), True)

    loads["bias"].wait()
    loads["edges"].wait()
    place = lax.broadcasted_iota(jnp.int32, (1, KEY_WINDOW), 1)
    for b in range(blocks):
        position = me * atom_rows - RIM + QUERY_BLOCK * b + place
        allowed = (position >= edges_ref[0, b]) & (position < edges_ref[1, b])
        masked_bias[b] = jnp.where(
            allowed, bias_ref[b].reshape(atom_heads * QUERY_BLOCK, KEY_WINDOW), -1e30
        )

    @pl.when(jnp.logical_not(has_left))
    def _():
        for layer in range(LAYERS):
            for g in range(GROUPS):
                kv[layer, g, :, 0:RIM, :] = jnp.zeros((gs, RIM, 2 * width), BF16)
        for g in range(GROUPS):
            precv[g, 0] = jnp.zeros(precv.shape[2:], BF16)
        for t in range(waves):
            back[t, 0] = jnp.zeros(back.shape[2:], BF16)
        counts[3] = jnp.zeros(counts.shape[1:], BF16)

    @pl.when(jnp.logical_not(has_right))
    def _():
        for layer in range(LAYERS):
            for g in range(GROUPS):
                kv[layer, g, :, RIM + atom_rows :, :] = jnp.zeros((gs, RIM, 2 * width), BF16)
        for g in range(GROUPS):
            precv[g, 1] = jnp.zeros(precv.shape[2:], BF16)
        for t in range(waves):
            back[t, 2] = jnp.zeros(back.shape[2:], BF16)
        counts[4] = jnp.zeros(counts.shape[1:], BF16)

    for name in ("out", "up", "down", "pool"):
        loads[name].wait()
    run_pair(0, pool)
    loads["single"].wait()
    loads["back"].wait()

    exchange(*count_copy(), False)
    number_of = (
        counts[1].astype(F32)[:, :1] + counts[3].astype(F32)[:, :1] + counts[4].astype(F32)[:, :1]
    )
    lanes = 128
    half = lanes // 2
    main = lanes - 2 * head_size
    rest = head_size - main
    lane = lax.broadcasted_iota(jnp.int32, (token_rows, lanes), 1)

    def moved(block, start, to, size=head_size):
        tile, off = start // lanes, start % lanes
        shift = (to - off) % lanes

        def turned(t):
            part = block[:, t * lanes : (t + 1) * lanes]
            return part if shift == 0 else pltpu.roll(part, shift, 1)

        if off + size <= lanes:
            return turned(tile)
        return jnp.where(lane < to + lanes - off, turned(tile), turned(tile + 1))

    def spread(copy_of):
        def step(k, c):
            copy_of(lax.rem(me + k, n), me).start()
            return c

        lax.fori_loop(1, n, step, 0)

    others = pl.ds(0, n - 1)

    def every_pair():
        return remote(
            pair_buf.at[others], pair_buf.at[others], pair_send, pair_recv, right
        )

    rows_of = item_rows(token_rows, pack, waves)
    starts = (0, rows_of[0])

    def item_copy(t):
        span = pl.ds(starts[t], rows_of[t])
        return lambda target, slot: remote(
            items.at[target, :, span], got.at[slot, :, span], item_send, item_recv.at[t], target
        )

    def every_item(t):
        span = pl.ds(starts[t], rows_of[t])
        return remote(
            items.at[others, :, span], got.at[others, :, span], item_send, item_recv.at[t], right
        )

    def out_copy(t):
        return lambda target, slot: remote(
            outs.at[t, target], returned.at[t, slot], out_send, out_recv.at[t], target
        )

    def every_out(t):
        return remote(
            outs.at[t, others], returned.at[t, others], out_send, out_recv.at[t], right
        )

    def token_project(t):
        for g in range(GROUPS) if waves == 1 else (t,):
            exchange(*pool_copy(g), False)
        for a in range(wave_samples):
            s = t * wave_samples + a
            g, i = s // gs, s % gs
            sums = own_sum[g, i] + precv[g, 0, i].astype(F32) + precv[g, 1, i].astype(F32)
            token_in[s * token_rows : (s + 1) * token_rows, :] = (
                sums / number_of + token_single_ref[...]
            )
        normal_tok = normed(token_in[t * wave_rows : (t + 1) * wave_rows, :]).astype(BF16)
        parts = [
            dot(normal_tok, w_tqkv[:, j * channels : (j + 1) * channels]) for j in range(3)
        ]
        for h in range(heads) if waves == 1 else ():
            start = h * head_size
            for a in range(0, wave_samples, pack):
                keys = []
                for p in range(pack):
                    item = h * samples + a + p
                    owner, unit = item // per, item % per // pack
                    at = slice((a + p) * token_rows, (a + p + 1) * token_rows)
                    v = moved(parts[2][at], start, half * p)
                    q = moved(parts[0][at], start, half * (1 - p))
                    keys.append(moved(parts[1][at], start, half * (1 - p)))
                    low, high = (v, q) if p == 0 else (q, v)
                    tile = jnp.where(lane < head_size, low, jnp.where(lane < half, 1.0, high))
                    items[owner, unit, p * token_rows : (p + 1) * token_rows, :] = tile.astype(
                        BF16
                    )
                key = keys[0] if pack == 1 else jnp.where(lane < half, keys[1], keys[0])
                items[owner, unit, pack * token_rows :, :] = key.astype(BF16)
        if waves == 2:
            if t == 0:
                held[...] = parts[2]
            one, two = slice(0, token_rows), slice(token_rows, 2 * token_rows)
            for h in range(heads):
                start = h * head_size
                mixed = []
                for upper, lower, at in ((0, 1, one), (1, 0, two)):
                    low = moved(parts[upper][one], start, 0)
                    mid = moved(parts[lower][two], start, head_size)
                    high = moved(parts[2][at], start, 2 * head_size, main)
                    tile = jnp.where(lane < head_size, low, jnp.where(lane < 2 * head_size, mid, high))
                    mixed.append(tile)
                at = starts[t]
                items[h, 0, at : at + 2 * token_rows, :] = jnp.concatenate(mixed, axis=0).astype(BF16)
                if t == 1:
                    tails = [
                        moved(values[at], start + main, rest * i, rest)
                        for i, (values, at) in enumerate(
                            ((held[...], one), (held[...], two), (parts[2], one), (parts[2], two))
                        )
                    ]
                    tail = tails[3]
                    for i in (2, 1, 0):
                        tail = jnp.where(lane < rest * (i + 1), tails[i], tail)
                    near, far = tail[: token_rows // 2], tail[token_rows // 2 :]
                    tail = jnp.where(lane[: token_rows // 2] < half, near, pltpu.roll(far, half, 1))
                    items[h, 0, at + 2 * token_rows :, :] = tail.astype(BF16)
        spread(item_copy(t))
        span = pl.ds(starts[t], rows_of[t])
        got[me, :, span] = items[me, :, span]

    token_scale = head_size ** (-0.5)
    tile = 16
    key_lane = lax.broadcasted_iota(jnp.int32, (tokens, lanes), 1)
    out_lane = lax.broadcasted_iota(jnp.int32, (tile * token_rows, lanes), 1)

    def token_attend(t):
        every_item(t).wait_recv()
        for unit in range(units):
            packed = got[:, unit, pack * token_rows :, :].reshape(tokens, lanes)

            def one(block, c):
                span = pl.ds(block * tile, tile)
                ratios = []
                for p in range(pack):
                    at = slice(p * token_rows, (p + 1) * token_rows)
                    mine = key_lane < head_size
                    if p == 0:
                        mine = (key_lane >= half) & (key_lane < half + head_size)
                    keys = jnp.where(mine, packed, jnp.zeros_like(packed))
                    values = got[:, unit, at, :].reshape(tokens, lanes)
                    q = got[span, unit, at, :].reshape(tile * token_rows, lanes)
                    scores = lax.dot_general(q, keys, LAST, preferred_element_type=F32)
                    scores = scores * token_scale + pair_buf[span].reshape(
                        tile * token_rows, tokens
                    )
                    expo = jnp.exp(scores - jnp.max(scores, -1, keepdims=True)).astype(BF16)
                    both = dot(expo, values)
                    ratios.append(both / both[:, head_size : head_size + 1])
                ratio = ratios[0] if pack == 1 else jnp.where(out_lane < half, *ratios)
                outs[t, span, unit, :, :] = ratio.astype(BF16).reshape(tile, token_rows, lanes)
                return c

            if n == tile:
                one(0, 0)
            else:
                lax.fori_loop(0, n // tile, one, 0)
        spread(out_copy(t))
        returned[t, me] = outs[t, me]

    all_lane = lax.broadcasted_iota(jnp.int32, (tokens, lanes), 1)

    def token_weights(t):
        at = starts[t]
        one = got[:, 0, at : at + token_rows, :].reshape(tokens, lanes)
        two = got[:, 0, at + token_rows : at + 2 * token_rows, :].reshape(tokens, lanes)
        bias = pair_buf[...].reshape(tokens, tokens)
        for a, (q, k) in enumerate(((one, two), (two, one))):
            mine = (all_lane >= a * head_size) & (all_lane < (a + 1) * head_size)
            keys = jnp.where(mine, k, jnp.zeros_like(k))
            scores = lax.dot_general(q, keys, LAST, preferred_element_type=F32)
            scores = scores * token_scale + bias
            expo = jnp.exp(scores - jnp.max(scores, -1, keepdims=True))
            weights[t, a] = expo.astype(BF16)

    def token_mix(t):
        end = starts[1] + 2 * token_rows
        tail = got[:, 0, end:, :].astype(F32)
        flat = tail.reshape(n * token_rows // 2, lanes)
        tail = jnp.concatenate(
            [tail, pltpu.roll(flat, half, 1).reshape(tail.shape)], axis=1
        ).reshape(tokens, lanes)
        tail = jnp.where(all_lane < half, tail, 1.0).astype(BF16)
        ratios = []
        for a in range(2):
            at = starts[t] + a * token_rows
            values = got[:, 0, at : at + token_rows, :].reshape(tokens, lanes)
            both = dot(weights[t, a], jnp.concatenate([values, tail], axis=1))
            ratios.append(both / both[:, lanes + half : lanes + half + 1])
        first, second = ratios
        edge = rest * (2 * t + 1)
        out = jnp.where(
            all_lane >= 2 * head_size,
            first[:, :lanes],
            jnp.where(
                all_lane >= half,
                pltpu.roll(second[:, :lanes], lanes - main, 1),
                jnp.where(all_lane < edge, first[:, lanes:], second[:, lanes:]),
            ),
        )
        outs[t, :, 0, :, :] = out.astype(BF16).reshape(n, token_rows, lanes)
        spread(out_copy(t))
        returned[t, me] = outs[t, me]

    def token_finish(t):
        every_out(t).wait_recv()
        state = token_in[t * wave_rows : (t + 1) * wave_rows, :]
        for h in range(heads):
            mix = []
            for a in range(wave_samples):
                item = h * samples + t * wave_samples + a
                owner, unit, p = item // per, item % per // pack - t * units, item % per % pack
                block = returned[t, owner, unit]
                if waves == 2:
                    block = block.astype(F32)
                    to_main = pltpu.roll(block, (1 + a) * main, 1)
                    shift = (main - rest * (2 * t + a)) % lanes
                    to_rest = pltpu.roll(block, shift, 1) if shift else block
                    block = jnp.where(lane < main, to_main, to_rest).astype(BF16)
                elif p == 1:
                    block = pltpu.roll(block.astype(F32), half, 1).astype(BF16)
                mix.append(block[:, :head_size])
            state = state + dot(
                jnp.concatenate(mix, axis=0), w_tout[h * head_size : (h + 1) * head_size, :]
            )
        for a in range(wave_samples):
            state_ref[t * wave_samples + a] = state[a * token_rows : (a + 1) * token_rows]
        back[t, 1] = dot(normed(state).astype(BF16), w_back_ref[...]).astype(BF16)
        exchange(*back_copy(t), True)

    loads["tqkv"].wait()
    for t in range(waves):
        token_project(t)
    loads["own_pair"].wait()
    every_pair().wait_recv()
    if waves == 1:
        token_attend(0)
    else:
        for t in range(waves):
            every_item(t).wait_recv()
            token_weights(t)
            if t == 0:
                continue
            for u in range(waves):
                token_mix(u)
    loads["tout"].wait()
    for t in range(waves):
        token_finish(t)
    first = ENC_LAYERS
    for g in range(GROUPS):
        for t in range(waves):
            if g * waves // GROUPS == t and (waves == GROUPS or g == 0):
                exchange(*back_copy(t), False)
        for i in range(gs):
            s = g * gs + i
            t, at = s // wave_samples, s % wave_samples * token_rows
            near = jnp.concatenate([back[t, j, at : at + token_rows, :] for j in range(3)], axis=0)
            picked = lax.dot_general(sel, near, FIRST, preferred_element_type=F32)
            stream[g, i * atom_rows : (i + 1) * atom_rows, :] += picked
        project(first, g)
        send_halo(first, g)

    def finish(g, value):
        normal = normed(value).astype(BF16)
        for i in range(gs):
            s = g * gs + i
            update = lax.dot_general(
                w_final_ref[...],
                normal[i * atom_rows : (i + 1) * atom_rows],
                LAST,
                preferred_element_type=F32,
            )
            sigma, total = sigma_of(s)
            result = (
                SIGMA_DATA * SIGMA_DATA / total * noisy_of(s, sigma)
                + sigma * SIGMA_DATA * lax.rsqrt(total) * update
            ) / SIGMA_DATA
            for c in range(3):
                denoised_ref[c, pl.ds(s, 1), :] = result[c : c + 1]

    loads["final"].wait()
    run_pair(first, finish)

    sent(
        remote(
            kv.at[:, :, :, pl.ds(0, RIM), :],
            kv.at[:, :, :, pl.ds(0, RIM), :],
            halo_send.at[0],
            halo_recv.at[0, 0, 0],
            right,
        ),
        remote(
            kv.at[:, :, :, pl.ds(0, RIM), :],
            kv.at[:, :, :, pl.ds(0, RIM), :],
            halo_send.at[1],
            halo_recv.at[0, 0, 1],
            left,
        ),
    )
    sent(*count_copy())
    sent(
        remote(psend.at[:, 1], precv.at[:, 0], pool_send.at[0], pool_recv.at[0, 0], right),
        remote(psend.at[:, 0], precv.at[:, 1], pool_send.at[1], pool_recv.at[0, 1], left),
    )
    sent(
        remote(back.at[:, 1], back.at[:, 0], back_send.at[0], back_recv.at[0, 0], right),
        remote(back.at[:, 1], back.at[:, 2], back_send.at[1], back_recv.at[0, 1], left),
    )
    every_pair().wait_send()
    for t in range(waves):
        every_item(t).wait_send()
        every_out(t).wait_send()


def store(denoised_ref, state_ref, denoised_out, state_out, sem):
    copies = (
        pltpu.make_async_copy(state_ref, state_out, sem.at[0]),
        pltpu.make_async_copy(denoised_ref, denoised_out, sem.at[1]),
    )
    for copy in copies:
        copy.start()
    for copy in copies:
        copy.wait()


def shards(
    n,
    x_true,
    noise,
    noise_level,
    atom_single,
    atom_token,
    window_edges,
    atom_pair_bias,
    token_single,
    pair_bias,
    w_coord,
    w_atom_qkv,
    w_atom_out,
    w_atom_up,
    w_atom_down,
    w_pool,
    w_token_qkv,
    w_token_out,
    w_back,
    w_final,
):
    samples = noise.shape[0]
    atom_rows, width = atom_single.shape
    token_rows, channels = token_single.shape
    blocks, atom_heads = atom_pair_bias.shape[:2]
    heads = pair_bias.shape[0]
    gs = samples // GROUPS
    per, pack, waves, units = plan(n, heads, samples)
    vmem = pl.BlockSpec(memory_space=pltpu.VMEM)
    anywhere = pl.BlockSpec(memory_space=pl.ANY)
    dma = pltpu.SemaphoreType.DMA
    held = pl.pallas_call(
        functools.partial(kernel, n),
        name="denoise",
        out_shape=(
            pltpu.VMEM((3, samples, atom_rows), F32),
            pltpu.VMEM((samples, token_rows, channels), F32),
        ),
        in_specs=[anywhere] * 19,
        out_specs=(vmem, vmem),
        scratch_shapes=[
            pltpu.SMEM((samples,), jnp.int32),
            pltpu.SMEM((2, blocks), jnp.int32),
            pltpu.VMEM(x_true.shape, F32),
            pltpu.VMEM((3, samples, atom_rows), F32),
            pltpu.VMEM(atom_single.shape, BF16),
            pltpu.VMEM((1, atom_rows), jnp.int32),
            pltpu.VMEM(w_coord.shape, F32),
            pltpu.VMEM(w_final.shape, BF16),
            pltpu.VMEM((GROUPS, gs * atom_rows, width), F32),
            pltpu.VMEM((LAYERS, GROUPS, gs, atom_rows + 2 * RIM, 2 * width), BF16),
            pltpu.VMEM((GROUPS, gs * atom_rows, width), BF16),
            pltpu.VMEM((blocks, atom_heads * QUERY_BLOCK, KEY_WINDOW), F32),
            pltpu.VMEM((5, token_rows, 128), BF16),
            pltpu.VMEM((GROUPS, gs, token_rows, channels), F32),
            pltpu.VMEM((GROUPS, 2, gs, token_rows, channels), BF16),
            pltpu.VMEM((GROUPS, 2, gs, token_rows, channels), BF16),
            pltpu.VMEM((samples * token_rows, channels), F32),
            pltpu.VMEM((n, units, sum(item_rows(token_rows, pack, waves)), 128), BF16),
            pltpu.VMEM((n, units, sum(item_rows(token_rows, pack, waves)), 128), BF16),
            pltpu.VMEM((2 * token_rows, channels), F32),
            pltpu.VMEM((waves, 2, n * token_rows, n * token_rows), BF16),
            pltpu.VMEM((n, token_rows, n * token_rows), F32),
            pltpu.VMEM((waves, n, units, token_rows, 128), BF16),
            pltpu.VMEM((waves, n, units, token_rows, 128), BF16),
            pltpu.VMEM((waves, 3, samples // waves * token_rows, width), BF16),
            pltpu.VMEM(w_token_qkv.shape, BF16),
            pltpu.VMEM(w_token_out.shape, BF16),
            pltpu.VMEM(atom_pair_bias.shape, F32),
            pltpu.VMEM(token_single.shape, F32),
            pltpu.VMEM(w_atom_qkv.shape, BF16),
            pltpu.VMEM(w_atom_out.shape, BF16),
            pltpu.VMEM(w_atom_up.shape, BF16),
            pltpu.VMEM(w_atom_down.shape, BF16),
            pltpu.VMEM(w_pool.shape, BF16),
            pltpu.VMEM(w_back.shape, BF16),
            dma((19,)),
            dma((2,)),
            dma((LAYERS, GROUPS, 2)),
            dma((2,)),
            dma((2,)),
            dma((2,)),
            dma((GROUPS, 2)),
            dma(()),
            dma(()),
            dma(()),
            dma((waves,)),
            dma(()),
            dma((waves,)),
            dma((2,)),
            dma((waves, 2)),
        ],
        compiler_params=pltpu.CompilerParams(
            collective_id=0, has_side_effects=True, vmem_limit_bytes=56 * 1024 * 1024
        ),
    )(
        noise_level,
        window_edges.T,
        x_true,
        noise.transpose(1, 0, 2),
        atom_single,
        atom_token.reshape(1, atom_rows),
        atom_pair_bias,
        token_single,
        pair_bias,
        w_coord,
        w_atom_qkv,
        w_atom_out,
        w_atom_up,
        w_atom_down,
        w_pool,
        w_token_qkv,
        w_token_out,
        w_back,
        w_final,
    )
    denoised, state = pl.pallas_call(
        store,
        name="store",
        out_shape=(
            jax.ShapeDtypeStruct((3, samples, atom_rows), F32),
            jax.ShapeDtypeStruct((samples, token_rows, channels), F32),
        ),
        in_specs=[vmem] * 2,
        out_specs=(anywhere, anywhere),
        scratch_shapes=[dma((2,))],
    )(*[pltpu.with_memory_space_constraint(x, pltpu.VMEM) for x in held])
    return denoised.transpose(1, 0, 2), state


def solution(mesh):
    in_specs = (
        P(None, ("groups", "seq")),
        P("groups", None, "seq"),
        P("groups"),
        P(("groups", "seq"), None),
        P(("groups", "seq")),
        P(("groups", "seq"), None),
        P(("groups", "seq"), None, None, None),
        P(("groups", "seq"), None),
        P("groups", "seq", None),
    ) + (P(),) * 10
    out_specs = (P("groups", None, "seq"), P("groups", "seq", None))
    return jax.shard_map(
        functools.partial(shards, mesh.shape["seq"]),
        mesh=mesh,
        in_specs=in_specs,
        out_specs=out_specs,
        check_vma=False,
    )
```

```python
import functools

import jax
import jax.numpy as jnp
from jax import lax
from jax.experimental import pallas as pl
from jax.experimental.pallas import tpu as pltpu
from jax.sharding import PartitionSpec as P

QUERY_BLOCK = 32
KEY_WINDOW = 128
ENC_LAYERS = 2
LEVELS = 200
RIM = 48
LAYERS = 4
GROUPS = 2

EPS = 1e-05
SIGMA_DATA = 16.0
MESH = pl.DeviceIdType.MESH
F32 = jnp.float32
BF16 = jnp.bfloat16
LAST = (((1,), (1,)), ((), ()))
FIRST = (((0,), (0,)), ((), ()))


def normed(values):
    centred = values - jnp.mean(values, -1, keepdims=True)
    spread = jnp.mean(centred * centred, -1, keepdims=True)
    return centred * lax.rsqrt(spread + EPS)


def dot(a, b):
    return jnp.dot(a, b, preferred_element_type=F32)


def remote(src, dst, send, recv, target):
    return pltpu.make_async_remote_copy(
        src_ref=src,
        dst_ref=dst,
        send_sem=send,
        recv_sem=recv,
        device_id={"seq": target},
        device_id_type=MESH,
    )


def plan(n, heads, samples):
    per = heads * samples // n
    gs = samples // GROUPS
    pack = 2 if per % 2 == 0 else 1
    waves = GROUPS if per == samples and gs == pack else 1
    return per, pack, waves, per // pack // waves


def item_rows(token_rows, pack, waves):
    if waves == 1:
        return ((pack + 1) * token_rows,)
    return (2 * token_rows + token_rows // 2,) * 2


def kernel(
    n,
    level_hbm,
    edges_hbm,
    x_true_hbm,
    noise_hbm,
    single_hbm,
    atom_token_hbm,
    bias_hbm,
    token_single_hbm,
    pair_hbm,
    w_coord_hbm,
    w_qkv_hbm,
    w_out_hbm,
    w_up_hbm,
    w_down_hbm,
    w_pool_hbm,
    w_tqkv_hbm,
    w_tout_hbm,
    w_back_hbm,
    w_final_hbm,
    denoised_ref,
    state_ref,
    level_ref,
    edges_ref,
    x_true_ref,
    noise_ref,
    single_ref,
    atom_token_ref,
    w_coord_ref,
    w_final_ref,
    stream,
    kv,
    queries,
    masked_bias,
    counts,
    own_sum,
    psend,
    precv,
    token_in,
    items,
    got,
    pair_own,
    pair_out,
    pair_buf,
    outs,
    returned,
    back,
    w_tqkv,
    w_tout,
    bias_ref,
    token_single_ref,
    w_qkv_ref,
    w_out_ref,
    w_up_ref,
    w_down_ref,
    w_pool_ref,
    w_back_ref,
    load_sem,
    halo_send,
    halo_recv,
    count_send,
    count_recv,
    pool_send,
    pool_recv,
    pair_send,
    pair_recv,
    item_send,
    item_recv,
    out_send,
    out_recv,
    back_send,
    back_recv,
):
    samples = noise_ref.shape[1]
    atom_rows, width = single_ref.shape
    token_rows, channels = token_single_ref.shape
    blocks, atom_heads = bias_ref.shape[:2]
    atom_head = width // atom_heads
    heads = pair_hbm.shape[0]
    head_size = channels // heads
    tokens = n * token_rows
    gs = samples // GROUPS
    per, pack, waves, units = plan(n, heads, samples)
    wave_samples = samples // waves
    wave_rows = wave_samples * token_rows

    me = lax.axis_index("seq")
    right = lax.rem(me + 1, n)
    left = lax.rem(me + n - 1, n)
    has_left = me > 0
    has_right = me < n - 1

    barrier = pltpu.get_barrier_semaphore()

    def greet(k, c):
        pl.semaphore_signal(
            barrier, inc=1, device_id={"seq": lax.rem(me + k, n)}, device_id_type=MESH
        )
        return c

    own_head = (me * per) // samples
    loads = {}
    for slot, (name, src, dst) in enumerate(
        (
            ("level", level_hbm, level_ref),
            ("x_true", x_true_hbm, x_true_ref),
            ("noise", noise_hbm, noise_ref),
            ("atoms", single_hbm, single_ref),
            ("coord", w_coord_hbm, w_coord_ref),
            ("qkv", w_qkv_hbm, w_qkv_ref),
            ("pair", pair_hbm, pair_own),
            ("atom_token", atom_token_hbm, atom_token_ref),
            ("edges", edges_hbm, edges_ref),
            ("bias", bias_hbm, bias_ref),
            ("out", w_out_hbm, w_out_ref),
            ("up", w_up_hbm, w_up_ref),
            ("down", w_down_hbm, w_down_ref),
            ("pool", w_pool_hbm, w_pool_ref),
            ("single", token_single_hbm, token_single_ref),
            ("tqkv", w_tqkv_hbm, w_tqkv),
            ("back", w_back_hbm, w_back_ref),
            ("tout", w_tout_hbm, w_tout),
            ("final", w_final_hbm, w_final_ref),
        )
    ):
        loads[name] = pltpu.make_async_copy(src, dst, load_sem.at[slot])
        loads[name].start()
        if name == "qkv":
            lax.fori_loop(1, n, greet, 0)

    upper_root = 160.0 ** (1.0 / 7.0)
    lower_root = 0.0004 ** (1.0 / 7.0)

    def sigma_of(s):
        level = jnp.full((1, atom_rows), level_ref[s], jnp.int32).astype(F32)
        base = upper_root + level / (LEVELS - 1) * (lower_root - upper_root)
        square = base * base
        sigma = SIGMA_DATA * (square * square * square * base)
        return sigma, sigma * sigma + SIGMA_DATA * SIGMA_DATA

    def noisy_of(s, sigma):
        noise = jnp.concatenate([noise_ref[c, pl.ds(s, 1), :] for c in range(3)], axis=0)
        return x_true_ref[...] + sigma * noise

    for name in ("level", "x_true", "noise"):
        loads[name].wait()
    scaled = []
    for s in range(samples):
        sigma, total = sigma_of(s)
        scaled.append(noisy_of(s, sigma) * lax.rsqrt(total))
    spare = atom_rows - 3 * samples
    columns = jnp.transpose(
        jnp.concatenate(scaled + [jnp.zeros((spare, atom_rows), F32)], axis=0)
    )
    loads["atoms"].wait()
    loads["coord"].wait()
    single = single_ref[...].astype(F32)
    for s in range(samples):
        value = single
        for c in range(3):
            at = 3 * s + c
            value = value + columns[:, at : at + 1] * w_coord_ref[c : c + 1, :]
        stream[s // gs, pl.ds((s % gs) * atom_rows, atom_rows), :] = value

    def exchange(to_right, to_left, begin):
        if begin:

            @pl.when(has_right)
            def _():
                to_right.start()

            @pl.when(has_left)
            def _():
                to_left.start()

        else:

            @pl.when(has_left)
            def _():
                to_right.wait_recv()

            @pl.when(has_right)
            def _():
                to_left.wait_recv()

    def sent(to_right, to_left):
        @pl.when(has_right)
        def _():
            to_right.wait_send()

        @pl.when(has_left)
        def _():
            to_left.wait_send()

    def halo(layer, g):
        return (
            remote(
                kv.at[layer, g, :, pl.ds(atom_rows, RIM), :],
                kv.at[layer, g, :, pl.ds(0, RIM), :],
                halo_send.at[0],
                halo_recv.at[layer, g, 0],
                right,
            ),
            remote(
                kv.at[layer, g, :, pl.ds(RIM, RIM), :],
                kv.at[layer, g, :, pl.ds(RIM + atom_rows, RIM), :],
                halo_send.at[1],
                halo_recv.at[layer, g, 1],
                left,
            ),
        )

    def project(layer, g):
        normal_in = normed(stream[g]).astype(BF16)
        key_value = dot(normal_in, w_qkv_ref[layer, :, width:]).astype(BF16)
        for i in range(gs):
            kv[layer, g, i, RIM : RIM + atom_rows, :] = key_value[
                i * atom_rows : (i + 1) * atom_rows
            ]
        queries[g] = dot(normal_in, w_qkv_ref[layer, :, :width]).astype(BF16)

    def send_halo(layer, g):
        exchange(*halo(layer, g), True)

    stacked = atom_heads * QUERY_BLOCK
    row_head = lax.broadcasted_iota(jnp.int32, (stacked, width), 0) // QUERY_BLOCK
    lane_head = lax.broadcasted_iota(jnp.int32, (stacked, width), 1) // atom_head
    own_lanes = row_head == lane_head
    few_lanes = lane_head[:QUERY_BLOCK]
    scale = atom_head ** (-0.5)
    ones = jnp.ones((KEY_WINDOW, width), BF16)

    def attend(layer, g):
        exchange(*halo(layer, g), False)
        mixed = []
        pairs = [(i, b) for i in range(gs) for b in range(blocks)]
        for start in range(0, len(pairs), 8):
            part = pairs[start : start + 8]
            scores = []
            for i, b in part:
                q = queries[g, pl.ds(i * atom_rows + b * QUERY_BLOCK, QUERY_BLOCK), :]
                q = jnp.concatenate([q] * atom_heads, axis=0)
                q = jnp.where(own_lanes, q, jnp.zeros_like(q))
                key_win = kv[layer, g, i, QUERY_BLOCK * b : QUERY_BLOCK * b + KEY_WINDOW, :width]
                score = lax.dot_general(q, key_win, LAST, preferred_element_type=F32)
                scores.append(score * scale + masked_bias[b])
            tops = [jnp.max(score, -1, keepdims=True) for score in scores]
            expos = [jnp.exp(score - top).astype(BF16) for score, top in zip(scores, tops)]
            sums = []
            for (i, b), expo in zip(part, expos):
                value_win = kv[layer, g, i, QUERY_BLOCK * b : QUERY_BLOCK * b + KEY_WINDOW, width:]
                sums.append(dot(expo, jnp.concatenate([value_win, ones], axis=1)))
            for both in sums:
                picked = both[:QUERY_BLOCK]
                number, below = picked[:, :width], picked[:, width:]
                for h in range(1, atom_heads):
                    rows = both[h * QUERY_BLOCK : (h + 1) * QUERY_BLOCK]
                    number = jnp.where(few_lanes == h, rows[:, :width], number)
                    below = jnp.where(few_lanes == h, rows[:, width:], below)
                mixed.append((number / below).astype(BF16))
        mixed = jnp.concatenate(mixed, axis=0)
        value = stream[g] + dot(mixed, w_out_ref[layer])
        normal_mid = normed(value).astype(BF16)
        gated = dot(normal_mid, w_up_ref[layer])
        gate = gated[:, : 2 * width]
        hidden = (gate / (1.0 + jnp.exp(-gate)) * gated[:, 2 * width :]).astype(BF16)
        value = value + dot(hidden, w_down_ref[layer])
        stream[g] = value
        return value

    def pool_copy(g):
        return (
            remote(
                psend.at[g, 1], precv.at[g, 0], pool_send.at[0], pool_recv.at[g, 0], right
            ),
            remote(psend.at[g, 0], precv.at[g, 1], pool_send.at[1], pool_recv.at[g, 1], left),
        )

    def count_copy():
        return (
            remote(counts.at[2], counts.at[3], count_send.at[0], count_recv.at[0], right),
            remote(counts.at[0], counts.at[4], count_send.at[1], count_recv.at[1], left),
        )

    def back_copy(t):
        return (
            remote(back.at[t, 1], back.at[t, 0], back_send.at[0], back_recv.at[t, 0], right),
            remote(back.at[t, 1], back.at[t, 2], back_send.at[1], back_recv.at[t, 1], left),
        )

    def run_pair(first, finish):
        def step(g, c):
            attend(first, g)
            project(first + 1, g)
            send_halo(first + 1, g)
            return c

        lax.fori_loop(0, GROUPS, step, 0)
        if first == 0:
            lax.fori_loop(1, n, pair_start, 0)

        def last(g, c):
            finish(g, attend(first + 1, g))
            return c

        lax.fori_loop(0, GROUPS, last, 0)

    loads["qkv"].wait()
    project(0, 0)
    pl.semaphore_wait(barrier, n - 1)
    send_halo(0, 0)
    project(0, 1)
    send_halo(0, 1)
    loads["atom_token"].wait()
    relative = atom_token_ref[...] - (me - 1) * token_rows
    selector = (
        lax.broadcasted_iota(jnp.int32, (3 * token_rows, atom_rows), 0) == relative
    ).astype(F32)
    sel = selector.astype(BF16)
    counted = jnp.broadcast_to(jnp.sum(selector, 1, keepdims=True), (3 * token_rows, 128))
    for j in range(3):
        counts[j] = counted[j * token_rows : (j + 1) * token_rows].astype(BF16)

    exchange(*count_copy(), True)

    def pair_copy(target, slot):
        return remote(
            pair_out.at[(target * per) // samples],
            pair_buf.at[slot],
            pair_send,
            pair_recv,
            target,
        )

    def pair_start(k, c):
        pair_copy(lax.rem(me + k, n), me).start()
        return c

    loads["pair"].wait()
    rows = pair_own[...]
    pair_out[...] = (rows - jnp.max(rows, -1, keepdims=True)).astype(BF16)
    pair_buf[me] = pair_out[own_head]

    def pool(g, value):
        pooled = jnp.maximum(dot(normed(value).astype(BF16), w_pool_ref[...]), 0.0)
        high = pooled.astype(BF16)
        low = (pooled - high.astype(F32)).astype(BF16)
        for i in range(gs):
            at = slice(i * atom_rows, (i + 1) * atom_rows)
            part = dot(sel, high[at]) + dot(sel, low[at])
            psend[g, 0, i] = part[:token_rows].astype(BF16)
            own_sum[g, i] = part[token_rows : 2 * token_rows]
            psend[g, 1, i] = part[2 * token_rows :].astype(BF16)
        exchange(*pool_copy(g), True)

    loads["bias"].wait()
    loads["edges"].wait()
    place = lax.broadcasted_iota(jnp.int32, (1, KEY_WINDOW), 1)
    for b in range(blocks):
        position = me * atom_rows - RIM + QUERY_BLOCK * b + place
        allowed = (position >= edges_ref[0, b]) & (position < edges_ref[1, b])
        masked_bias[b] = jnp.where(
            allowed, bias_ref[b].reshape(atom_heads * QUERY_BLOCK, KEY_WINDOW), -1e30
        )

    @pl.when(jnp.logical_not(has_left))
    def _():
        for layer in range(LAYERS):
            for g in range(GROUPS):
                kv[layer, g, :, 0:RIM, :] = jnp.zeros((gs, RIM, 2 * width), BF16)
        for g in range(GROUPS):
            precv[g, 0] = jnp.zeros(precv.shape[2:], BF16)
        for t in range(waves):
            back[t, 0] = jnp.zeros(back.shape[2:], BF16)
        counts[3] = jnp.zeros(counts.shape[1:], BF16)

    @pl.when(jnp.logical_not(has_right))
    def _():
        for layer in range(LAYERS):
            for g in range(GROUPS):
                kv[layer, g, :, RIM + atom_rows :, :] = jnp.zeros((gs, RIM, 2 * width), BF16)
        for g in range(GROUPS):
            precv[g, 1] = jnp.zeros(precv.shape[2:], BF16)
        for t in range(waves):
            back[t, 2] = jnp.zeros(back.shape[2:], BF16)
        counts[4] = jnp.zeros(counts.shape[1:], BF16)

    for name in ("out", "up", "down", "pool"):
        loads[name].wait()
    run_pair(0, pool)
    loads["single"].wait()
    loads["back"].wait()

    exchange(*count_copy(), False)
    number_of = (
        counts[1].astype(F32)[:, :1] + counts[3].astype(F32)[:, :1] + counts[4].astype(F32)[:, :1]
    )
    lanes = 128
    half = lanes // 2
    main = lanes - 2 * head_size
    rest = head_size - main
    lane = lax.broadcasted_iota(jnp.int32, (token_rows, lanes), 1)

    def moved(block, start, to, size=head_size):
        tile, off = start // lanes, start % lanes
        shift = (to - off) % lanes

        def turned(t):
            part = block[:, t * lanes : (t + 1) * lanes]
            return part if shift == 0 else pltpu.roll(part, shift, 1)

        if off + size <= lanes:
            return turned(tile)
        return jnp.where(lane < to + lanes - off, turned(tile), turned(tile + 1))

    def spread(copy_of):
        def step(k, c):
            copy_of(lax.rem(me + k, n), me).start()
            return c

        lax.fori_loop(1, n, step, 0)

    others = pl.ds(0, n - 1)

    def every_pair():
        return remote(
            pair_buf.at[others], pair_buf.at[others], pair_send, pair_recv, right
        )

    rows_of = item_rows(token_rows, pack, waves)
    starts = (0, rows_of[0])

    def item_copy(t):
        span = pl.ds(starts[t], rows_of[t])
        return lambda target, slot: remote(
            items.at[target, :, span], got.at[slot, :, span], item_send, item_recv.at[t], target
        )

    def every_item(t):
        span = pl.ds(starts[t], rows_of[t])
        return remote(
            items.at[others, :, span], got.at[others, :, span], item_send, item_recv.at[t], right
        )

    def out_copy(t):
        return lambda target, slot: remote(
            outs.at[t, target], returned.at[t, slot], out_send, out_recv.at[t], target
        )

    def every_out(t):
        return remote(
            outs.at[t, others], returned.at[t, others], out_send, out_recv.at[t], right
        )

    def token_project(t):
        for g in range(GROUPS) if waves == 1 else (t,):
            exchange(*pool_copy(g), False)
        for a in range(wave_samples):
            s = t * wave_samples + a
            g, i = s // gs, s % gs
            sums = own_sum[g, i] + precv[g, 0, i].astype(F32) + precv[g, 1, i].astype(F32)
            token_in[s * token_rows : (s + 1) * token_rows, :] = (
                sums / number_of + token_single_ref[...]
            )
        normal_tok = normed(token_in[t * wave_rows : (t + 1) * wave_rows, :]).astype(BF16)
        parts = [
            dot(normal_tok, w_tqkv[:, j * channels : (j + 1) * channels]) for j in range(3)
        ]
        for h in range(heads) if waves == 1 else ():
            start = h * head_size
            for a in range(0, wave_samples, pack):
                keys = []
                for p in range(pack):
                    item = h * samples + a + p
                    owner, unit = item // per, item % per // pack
                    at = slice((a + p) * token_rows, (a + p + 1) * token_rows)
                    v = moved(parts[2][at], start, half * p)
                    q = moved(parts[0][at], start, half * (1 - p))
                    keys.append(moved(parts[1][at], start, half * (1 - p)))
                    low, high = (v, q) if p == 0 else (q, v)
                    tile = jnp.where(lane < head_size, low, jnp.where(lane < half, 1.0, high))
                    items[owner, unit, p * token_rows : (p + 1) * token_rows, :] = tile.astype(
                        BF16
                    )
                key = keys[0] if pack == 1 else jnp.where(lane < half, keys[1], keys[0])
                items[owner, unit, pack * token_rows :, :] = key.astype(BF16)
        if waves == 2:
            one, two = slice(0, token_rows), slice(token_rows, 2 * token_rows)
            for h in range(heads):
                start = h * head_size
                mixed = []
                for upper, lower, at in ((0, 1, one), (1, 0, two)):
                    low = moved(parts[upper][one], start, 0)
                    mid = moved(parts[lower][two], start, head_size)
                    high = moved(parts[2][at], start, 2 * head_size, main)
                    tile = jnp.where(lane < head_size, low, jnp.where(lane < 2 * head_size, mid, high))
                    mixed.append(tile)
                at = starts[t]
                items[h, 0, at : at + 2 * token_rows, :] = jnp.concatenate(mixed, axis=0).astype(BF16)
                tail = jnp.where(
                    lane < rest,
                    moved(parts[2][one], start + main, 0, rest),
                    moved(parts[2][two], start + main, half - rest, rest),
                )
                near, far = tail[: token_rows // 2], tail[token_rows // 2 :]
                tail = jnp.where(lane[: token_rows // 2] < half, near, pltpu.roll(far, half, 1))
                items[h, 0, at + 2 * token_rows : at + rows_of[t], :] = tail.astype(BF16)
        spread(item_copy(t))
        span = pl.ds(starts[t], rows_of[t])
        got[me, :, span] = items[me, :, span]

    token_scale = head_size ** (-0.5)
    tile = 16
    key_lane = lax.broadcasted_iota(jnp.int32, (tokens, lanes), 1)
    out_lane = lax.broadcasted_iota(jnp.int32, (tile * token_rows, lanes), 1)

    def token_attend(t):
        every_item(t).wait_recv()
        for unit in range(units):
            packed = got[:, unit, pack * token_rows :, :].reshape(tokens, lanes)

            def one(block, c):
                span = pl.ds(block * tile, tile)
                ratios = []
                for p in range(pack):
                    at = slice(p * token_rows, (p + 1) * token_rows)
                    mine = key_lane < head_size
                    if p == 0:
                        mine = (key_lane >= half) & (key_lane < half + head_size)
                    keys = jnp.where(mine, packed, jnp.zeros_like(packed))
                    values = got[:, unit, at, :].reshape(tokens, lanes)
                    q = got[span, unit, at, :].reshape(tile * token_rows, lanes)
                    scores = lax.dot_general(q, keys, LAST, preferred_element_type=F32)
                    scores = scores * token_scale + pair_buf[span].astype(F32).reshape(
                        tile * token_rows, tokens
                    )
                    expo = jnp.exp(scores - jnp.max(scores, -1, keepdims=True)).astype(BF16)
                    both = dot(expo, values)
                    ratios.append(both / both[:, head_size : head_size + 1])
                ratio = ratios[0] if pack == 1 else jnp.where(out_lane < half, *ratios)
                outs[t, span, unit, :, :] = ratio.astype(BF16).reshape(tile, token_rows, lanes)
                return c

            if n == tile:
                one(0, 0)
            else:
                lax.fori_loop(0, n // tile, one, 0)
        spread(out_copy(t))
        returned[t, me] = outs[t, me]

    all_lane = lax.broadcasted_iota(jnp.int32, (tokens, lanes), 1)

    def token_pair(t):
        every_item(t).wait_recv()
        at = starts[t]
        one = got[:, 0, at : at + token_rows, :].reshape(tokens, lanes)
        two = got[:, 0, at + token_rows : at + 2 * token_rows, :].reshape(tokens, lanes)
        tail = got[:, 0, at + 2 * token_rows : at + rows_of[t], :].astype(F32)
        flat = tail.reshape(n * token_rows // 2, lanes)
        tail = jnp.concatenate(
            [tail, pltpu.roll(flat, half, 1).reshape(tail.shape)], axis=1
        ).reshape(tokens, lanes)
        tail = jnp.where(all_lane < half, tail, 1.0).astype(BF16)
        bias = pair_buf[...].astype(F32).reshape(tokens, tokens)
        ratios = []
        for a, (q, k) in enumerate(((one, two), (two, one))):
            mine = (all_lane >= a * head_size) & (all_lane < (a + 1) * head_size)
            keys = jnp.where(mine, k, jnp.zeros_like(k))
            scores = lax.dot_general(q, keys, LAST, preferred_element_type=F32)
            scores = scores * token_scale + bias
            expo = jnp.exp(scores - jnp.max(scores, -1, keepdims=True)).astype(BF16)
            both = dot(expo, jnp.concatenate([q, tail], axis=1))
            ratios.append(both / both[:, lanes + half : lanes + half + 1])
        first, second = ratios
        out = jnp.where(
            all_lane >= lanes - main,
            first[:, :lanes],
            jnp.where(
                all_lane < rest,
                first[:, lanes:],
                jnp.where(
                    all_lane < half - rest,
                    pltpu.roll(second[:, :lanes], half - rest, 1),
                    second[:, lanes:],
                ),
            ),
        )
        outs[t, :, 0, :, :] = out.astype(BF16).reshape(n, token_rows, lanes)
        spread(out_copy(t))
        returned[t, me] = outs[t, me]

    def token_finish(t):
        every_out(t).wait_recv()
        state = token_in[t * wave_rows : (t + 1) * wave_rows, :]
        for h in range(heads):
            mix = []
            for a in range(wave_samples):
                item = h * samples + t * wave_samples + a
                owner, unit, p = item // per, item % per // pack - t * units, item % per % pack
                block = returned[t, owner, unit]
                if waves == 2:
                    shift = lanes - rest if a else main
                    block = pltpu.roll(block.astype(F32), shift, 1).astype(BF16)
                elif p == 1:
                    block = pltpu.roll(block.astype(F32), half, 1).astype(BF16)
                mix.append(block[:, :head_size])
            state = state + dot(
                jnp.concatenate(mix, axis=0), w_tout[h * head_size : (h + 1) * head_size, :]
            )
        for a in range(wave_samples):
            state_ref[t * wave_samples + a] = state[a * token_rows : (a + 1) * token_rows]
        back[t, 1] = dot(normed(state).astype(BF16), w_back_ref[...]).astype(BF16)
        exchange(*back_copy(t), True)

    loads["tqkv"].wait()
    for t in range(waves):
        token_project(t)
    every_pair().wait_recv()
    if waves == 1:
        token_attend(0)
    else:
        for t in range(waves):
            token_pair(t)
    loads["tout"].wait()
    for t in range(waves):
        token_finish(t)
    first = ENC_LAYERS
    for g in range(GROUPS):
        for t in range(waves):
            if g * waves // GROUPS == t and (waves == GROUPS or g == 0):
                exchange(*back_copy(t), False)
        for i in range(gs):
            s = g * gs + i
            t, at = s // wave_samples, s % wave_samples * token_rows
            near = jnp.concatenate([back[t, j, at : at + token_rows, :] for j in range(3)], axis=0)
            picked = lax.dot_general(sel, near, FIRST, preferred_element_type=F32)
            stream[g, i * atom_rows : (i + 1) * atom_rows, :] += picked
        project(first, g)
        send_halo(first, g)

    def finish(g, value):
        normal = normed(value).astype(BF16)
        for i in range(gs):
            s = g * gs + i
            update = lax.dot_general(
                w_final_ref[...],
                normal[i * atom_rows : (i + 1) * atom_rows],
                LAST,
                preferred_element_type=F32,
            )
            sigma, total = sigma_of(s)
            result = (
                SIGMA_DATA * SIGMA_DATA / total * noisy_of(s, sigma)
                + sigma * SIGMA_DATA * lax.rsqrt(total) * update
            ) / SIGMA_DATA
            for c in range(3):
                denoised_ref[c, pl.ds(s, 1), :] = result[c : c + 1]

    loads["final"].wait()
    run_pair(first, finish)

    sent(
        remote(
            kv.at[:, :, :, pl.ds(0, RIM), :],
            kv.at[:, :, :, pl.ds(0, RIM), :],
            halo_send.at[0],
            halo_recv.at[0, 0, 0],
            right,
        ),
        remote(
            kv.at[:, :, :, pl.ds(0, RIM), :],
            kv.at[:, :, :, pl.ds(0, RIM), :],
            halo_send.at[1],
            halo_recv.at[0, 0, 1],
            left,
        ),
    )
    sent(*count_copy())
    sent(
        remote(psend.at[:, 1], precv.at[:, 0], pool_send.at[0], pool_recv.at[0, 0], right),
        remote(psend.at[:, 0], precv.at[:, 1], pool_send.at[1], pool_recv.at[0, 1], left),
    )
    sent(
        remote(back.at[:, 1], back.at[:, 0], back_send.at[0], back_recv.at[0, 0], right),
        remote(back.at[:, 1], back.at[:, 2], back_send.at[1], back_recv.at[0, 1], left),
    )
    every_pair().wait_send()
    for t in range(waves):
        every_item(t).wait_send()
        every_out(t).wait_send()


def store(denoised_ref, state_ref, denoised_out, state_out, sem):
    copies = (
        pltpu.make_async_copy(state_ref, state_out, sem.at[0]),
        pltpu.make_async_copy(denoised_ref, denoised_out, sem.at[1]),
    )
    for copy in copies:
        copy.start()
    for copy in copies:
        copy.wait()


def shards(
    n,
    x_true,
    noise,
    noise_level,
    atom_single,
    atom_token,
    window_edges,
    atom_pair_bias,
    token_single,
    pair_bias,
    w_coord,
    w_atom_qkv,
    w_atom_out,
    w_atom_up,
    w_atom_down,
    w_pool,
    w_token_qkv,
    w_token_out,
    w_back,
    w_final,
):
    samples = noise.shape[0]
    atom_rows, width = atom_single.shape
    token_rows, channels = token_single.shape
    blocks, atom_heads = atom_pair_bias.shape[:2]
    heads = pair_bias.shape[0]
    gs = samples // GROUPS
    per, pack, waves, units = plan(n, heads, samples)
    vmem = pl.BlockSpec(memory_space=pltpu.VMEM)
    anywhere = pl.BlockSpec(memory_space=pl.ANY)
    dma = pltpu.SemaphoreType.DMA
    held = pl.pallas_call(
        functools.partial(kernel, n),
        name="denoise",
        out_shape=(
            pltpu.VMEM((3, samples, atom_rows), F32),
            pltpu.VMEM((samples, token_rows, channels), F32),
        ),
        in_specs=[anywhere] * 19,
        out_specs=(vmem, vmem),
        scratch_shapes=[
            pltpu.SMEM((samples,), jnp.int32),
            pltpu.SMEM((2, blocks), jnp.int32),
            pltpu.VMEM(x_true.shape, F32),
            pltpu.VMEM((3, samples, atom_rows), F32),
            pltpu.VMEM(atom_single.shape, BF16),
            pltpu.VMEM((1, atom_rows), jnp.int32),
            pltpu.VMEM(w_coord.shape, F32),
            pltpu.VMEM(w_final.shape, BF16),
            pltpu.VMEM((GROUPS, gs * atom_rows, width), F32),
            pltpu.VMEM((LAYERS, GROUPS, gs, atom_rows + 2 * RIM, 2 * width), BF16),
            pltpu.VMEM((GROUPS, gs * atom_rows, width), BF16),
            pltpu.VMEM((blocks, atom_heads * QUERY_BLOCK, KEY_WINDOW), F32),
            pltpu.VMEM((5, token_rows, 128), BF16),
            pltpu.VMEM((GROUPS, gs, token_rows, channels), F32),
            pltpu.VMEM((GROUPS, 2, gs, token_rows, channels), BF16),
            pltpu.VMEM((GROUPS, 2, gs, token_rows, channels), BF16),
            pltpu.VMEM((samples * token_rows, channels), F32),
            pltpu.VMEM((n, units, sum(item_rows(token_rows, pack, waves)), 128), BF16),
            pltpu.VMEM((n, units, sum(item_rows(token_rows, pack, waves)), 128), BF16),
            pltpu.VMEM(pair_bias.shape, F32),
            pltpu.VMEM(pair_bias.shape, BF16),
            pltpu.VMEM((n, token_rows, n * token_rows), BF16),
            pltpu.VMEM((waves, n, units, token_rows, 128), BF16),
            pltpu.VMEM((waves, n, units, token_rows, 128), BF16),
            pltpu.VMEM((waves, 3, samples // waves * token_rows, width), BF16),
            pltpu.VMEM(w_token_qkv.shape, BF16),
            pltpu.VMEM(w_token_out.shape, BF16),
            pltpu.VMEM(atom_pair_bias.shape, F32),
            pltpu.VMEM(token_single.shape, F32),
            pltpu.VMEM(w_atom_qkv.shape, BF16),
            pltpu.VMEM(w_atom_out.shape, BF16),
            pltpu.VMEM(w_atom_up.shape, BF16),
            pltpu.VMEM(w_atom_down.shape, BF16),
            pltpu.VMEM(w_pool.shape, BF16),
            pltpu.VMEM(w_back.shape, BF16),
            dma((19,)),
            dma((2,)),
            dma((LAYERS, GROUPS, 2)),
            dma((2,)),
            dma((2,)),
            dma((2,)),
            dma((GROUPS, 2)),
            dma(()),
            dma(()),
            dma(()),
            dma((waves,)),
            dma(()),
            dma((waves,)),
            dma((2,)),
            dma((waves, 2)),
        ],
        compiler_params=pltpu.CompilerParams(
            collective_id=0, has_side_effects=True, vmem_limit_bytes=56 * 1024 * 1024
        ),
    )(
        noise_level,
        window_edges.T,
        x_true,
        noise.transpose(1, 0, 2),
        atom_single,
        atom_token.reshape(1, atom_rows),
        atom_pair_bias,
        token_single,
        pair_bias,
        w_coord,
        w_atom_qkv,
        w_atom_out,
        w_atom_up,
        w_atom_down,
        w_pool,
        w_token_qkv,
        w_token_out,
        w_back,
        w_final,
    )
    denoised, state = pl.pallas_call(
        store,
        name="store",
        out_shape=(
            jax.ShapeDtypeStruct((3, samples, atom_rows), F32),
            jax.ShapeDtypeStruct((samples, token_rows, channels), F32),
        ),
        in_specs=[vmem] * 2,
        out_specs=(anywhere, anywhere),
        scratch_shapes=[dma((2,))],
    )(*[pltpu.with_memory_space_constraint(x, pltpu.VMEM) for x in held])
    return denoised.transpose(1, 0, 2), state


def solution(mesh):
    in_specs = (
        P(None, ("groups", "seq")),
        P("groups", None, "seq"),
        P("groups"),
        P(("groups", "seq"), None),
        P(("groups", "seq")),
        P(("groups", "seq"), None),
        P(("groups", "seq"), None, None, None),
        P(("groups", "seq"), None),
        P("groups", "seq", None),
    ) + (P(),) * 10
    out_specs = (P("groups", None, "seq"), P("groups", "seq", None))
    return jax.shard_map(
        functools.partial(shards, mesh.shape["seq"]),
        mesh=mesh,
        in_specs=in_specs,
        out_specs=out_specs,
        check_vma=False,
    )
```

```python
import functools

import jax
import jax.numpy as jnp
from jax import lax
from jax.experimental import pallas as pl
from jax.experimental.pallas import tpu as pltpu
from jax.sharding import PartitionSpec as P

QUERY_BLOCK = 32
KEY_WINDOW = 128
ENC_LAYERS = 2
LEVELS = 200
RIM = 48
LAYERS = 4
GROUPS = 2

EPS = 1e-05
SIGMA_DATA = 16.0
MESH = pl.DeviceIdType.MESH
F32 = jnp.float32
BF16 = jnp.bfloat16
LAST = (((1,), (1,)), ((), ()))
FIRST = (((0,), (0,)), ((), ()))


def normed(values):
    centred = values - jnp.mean(values, -1, keepdims=True)
    spread = jnp.mean(centred * centred, -1, keepdims=True)
    return centred * lax.rsqrt(spread + EPS)


def dot(a, b):
    return jnp.dot(a, b, preferred_element_type=F32)


def remote(src, dst, send, recv, target):
    return pltpu.make_async_remote_copy(
        src_ref=src,
        dst_ref=dst,
        send_sem=send,
        recv_sem=recv,
        device_id={"seq": target},
        device_id_type=MESH,
    )


def plan(n, heads, samples):
    per = heads * samples // n
    gs = samples // GROUPS
    pack = 2 if per % 2 == 0 else 1
    waves = GROUPS if per == samples and gs == pack else 1
    return per, pack, waves, per // pack // waves


def reach_rounds(n):
    rounds, known = 0, 1
    while known < n - 1:
        rounds, known = rounds + 1, 2 * known
    return rounds


def item_rows(token_rows, pack, waves):
    if waves == 1:
        return ((pack + 1) * token_rows,)
    return (2 * token_rows + token_rows // 2,) * 2


def kernel(
    n,
    level_hbm,
    edges_hbm,
    x_true_hbm,
    noise_hbm,
    single_hbm,
    atom_token_hbm,
    bias_hbm,
    token_single_hbm,
    pair_hbm,
    w_coord_hbm,
    w_qkv_hbm,
    w_out_hbm,
    w_up_hbm,
    w_down_hbm,
    w_pool_hbm,
    w_tqkv_hbm,
    w_tout_hbm,
    w_back_hbm,
    w_final_hbm,
    denoised_ref,
    state_ref,
    level_ref,
    edges_ref,
    x_true_ref,
    noise_ref,
    single_ref,
    atom_token_ref,
    w_coord_ref,
    w_final_ref,
    stream,
    edge,
    near_token,
    kv,
    queries,
    masked_bias,
    counts,
    own_sum,
    psend,
    precv,
    token_in,
    items,
    got,
    pair_own,
    pair_out,
    pair_buf,
    outs,
    returned,
    back,
    w_tqkv,
    w_tout,
    bias_ref,
    token_single_ref,
    w_qkv_ref,
    w_out_ref,
    w_up_ref,
    w_down_ref,
    w_pool_ref,
    w_back_ref,
    load_sem,
    ready,
    halo_send,
    halo_recv,
    count_send,
    count_recv,
    pool_send,
    pool_recv,
    pair_send,
    pair_recv,
    item_send,
    item_recv,
    out_send,
    out_recv,
    back_send,
    back_recv,
    edge_send,
    edge_recv,
    token_send,
    token_recv,
):
    samples = noise_ref.shape[1]
    atom_rows, width = single_ref.shape
    token_rows, channels = token_single_ref.shape
    blocks, atom_heads = bias_ref.shape[:2]
    atom_head = width // atom_heads
    heads = pair_hbm.shape[0]
    head_size = channels // heads
    tokens = n * token_rows
    gs = samples // GROUPS
    per, pack, waves, units = plan(n, heads, samples)
    wave_samples = samples // waves
    wave_rows = wave_samples * token_rows

    me = lax.axis_index("seq")
    right = lax.rem(me + 1, n)
    left = lax.rem(me + n - 1, n)
    has_left = me > 0
    has_right = me < n - 1

    barrier = pltpu.get_barrier_semaphore()

    def signal(semaphore, reach):
        for there, target in ((me >= reach, me - reach), (me + reach < n, me + reach)):

            @pl.when(there)
            def _():
                pl.semaphore_signal(
                    semaphore, inc=1, device_id={"seq": target}, device_id_type=MESH
                )

    def await_signals(semaphore, reach):
        count = (me >= reach).astype(jnp.int32) + (me + reach < n).astype(jnp.int32)
        pl.semaphore_wait(semaphore, count)

    rounds = reach_rounds(n)

    def met(number):
        if number < rounds:
            await_signals(ready.at[number], 2**number)
        if number + 1 < rounds:
            signal(ready.at[number + 1], 2 ** (number + 1))

    own_head = (me * per) // samples
    loads = {}
    for slot, (name, src, dst) in enumerate(
        (
            ("level", level_hbm, level_ref),
            ("x_true", x_true_hbm, x_true_ref),
            ("noise", noise_hbm, noise_ref),
            ("atoms", single_hbm, single_ref),
            ("coord", w_coord_hbm, w_coord_ref),
            ("qkv", w_qkv_hbm, w_qkv_ref),
            ("pair", pair_hbm, pair_own),
            ("atom_token", atom_token_hbm, atom_token_ref),
            ("edges", edges_hbm, edges_ref),
            ("bias", bias_hbm, bias_ref),
            ("out", w_out_hbm, w_out_ref),
            ("up", w_up_hbm, w_up_ref),
            ("down", w_down_hbm, w_down_ref),
            ("pool", w_pool_hbm, w_pool_ref),
            ("single", token_single_hbm, token_single_ref),
            ("tqkv", w_tqkv_hbm, w_tqkv),
            ("back", w_back_hbm, w_back_ref),
            ("tout", w_tout_hbm, w_tout),
            ("final", w_final_hbm, w_final_ref),
        )
    ):
        loads[name] = pltpu.make_async_copy(src, dst, load_sem.at[slot])
        loads[name].start()
        if name == "qkv":
            signal(barrier, 1)

    upper_root = 160.0 ** (1.0 / 7.0)
    lower_root = 0.0004 ** (1.0 / 7.0)

    def sigma_of(s):
        level = jnp.full((1, atom_rows), level_ref[s], jnp.int32).astype(F32)
        base = upper_root + level / (LEVELS - 1) * (lower_root - upper_root)
        square = base * base
        sigma = SIGMA_DATA * (square * square * square * base)
        return sigma, sigma * sigma + SIGMA_DATA * SIGMA_DATA

    def noisy_of(s, sigma):
        noise = jnp.concatenate([noise_ref[c, pl.ds(s, 1), :] for c in range(3)], axis=0)
        return x_true_ref[...] + sigma * noise

    for name in ("level", "x_true", "noise"):
        loads[name].wait()
    scaled = []
    for s in range(samples):
        sigma, total = sigma_of(s)
        scaled.append(noisy_of(s, sigma) * lax.rsqrt(total))
    spare = atom_rows - 3 * samples
    columns = jnp.transpose(
        jnp.concatenate(scaled + [jnp.zeros((spare, atom_rows), F32)], axis=0)
    )
    loads["atoms"].wait()
    loads["coord"].wait()
    single = single_ref[...].astype(F32)
    for s in range(samples):
        value = single
        for c in range(3):
            at = 3 * s + c
            value = value + columns[:, at : at + 1] * w_coord_ref[c : c + 1, :]
        stream[s // gs, s % gs] = value

    def exchange(to_right, to_left, begin):
        if begin:

            @pl.when(has_right)
            def _():
                to_right.start()

            @pl.when(has_left)
            def _():
                to_left.start()

        else:

            @pl.when(has_left)
            def _():
                to_right.wait_recv()

            @pl.when(has_right)
            def _():
                to_left.wait_recv()

    def sent(to_right, to_left):
        @pl.when(has_right)
        def _():
            to_right.wait_send()

        @pl.when(has_left)
        def _():
            to_left.wait_send()

    def halo(layer, g):
        return (
            remote(
                kv.at[layer, g, :, pl.ds(atom_rows, RIM), :],
                kv.at[layer, g, :, pl.ds(0, RIM), :],
                halo_send.at[0],
                halo_recv.at[layer, g, 0],
                right,
            ),
            remote(
                kv.at[layer, g, :, pl.ds(RIM, RIM), :],
                kv.at[layer, g, :, pl.ds(RIM + atom_rows, RIM), :],
                halo_send.at[1],
                halo_recv.at[layer, g, 1],
                left,
            ),
        )

    def project(layer, g):
        normal_in = normed(stream[g].reshape(gs * atom_rows, width)).astype(BF16)
        key_value = dot(normal_in, w_qkv_ref[layer, :, width:]).astype(BF16)
        for i in range(gs):
            kv[layer, g, i, RIM : RIM + atom_rows, :] = key_value[
                i * atom_rows : (i + 1) * atom_rows
            ]
        queries[g] = dot(normal_in, w_qkv_ref[layer, :, :width]).astype(BF16)

    def send_halo(layer, g):
        exchange(*halo(layer, g), True)

    stacked = atom_heads * QUERY_BLOCK
    row_head = lax.broadcasted_iota(jnp.int32, (stacked, width), 0) // QUERY_BLOCK
    lane_head = lax.broadcasted_iota(jnp.int32, (stacked, width), 1) // atom_head
    own_lanes = row_head == lane_head
    few_lanes = lane_head[:QUERY_BLOCK]
    scale = atom_head ** (-0.5)
    ones = jnp.ones((KEY_WINDOW, width), BF16)

    def attend(layer, g):
        if layer != ENC_LAYERS:
            exchange(*halo(layer, g), False)
        mixed = []
        pairs = [(i, b) for i in range(gs) for b in range(blocks)]
        for start in range(0, len(pairs), 8):
            part = pairs[start : start + 8]
            scores = []
            for i, b in part:
                q = queries[g, pl.ds(i * atom_rows + b * QUERY_BLOCK, QUERY_BLOCK), :]
                q = jnp.concatenate([q] * atom_heads, axis=0)
                q = jnp.where(own_lanes, q, jnp.zeros_like(q))
                key_win = kv[layer, g, i, QUERY_BLOCK * b : QUERY_BLOCK * b + KEY_WINDOW, :width]
                score = lax.dot_general(q, key_win, LAST, preferred_element_type=F32)
                scores.append(score * scale + masked_bias[b])
            tops = [jnp.max(score, -1, keepdims=True) for score in scores]
            expos = [jnp.exp(score - top).astype(BF16) for score, top in zip(scores, tops)]
            sums = []
            for (i, b), expo in zip(part, expos):
                value_win = kv[layer, g, i, QUERY_BLOCK * b : QUERY_BLOCK * b + KEY_WINDOW, width:]
                sums.append(dot(expo, jnp.concatenate([value_win, ones], axis=1)))
            for both in sums:
                picked = both[:QUERY_BLOCK]
                number, below = picked[:, :width], picked[:, width:]
                for h in range(1, atom_heads):
                    rows = both[h * QUERY_BLOCK : (h + 1) * QUERY_BLOCK]
                    number = jnp.where(few_lanes == h, rows[:, :width], number)
                    below = jnp.where(few_lanes == h, rows[:, width:], below)
                mixed.append((number / below).astype(BF16))
        mixed = jnp.concatenate(mixed, axis=0)
        value = stream[g].reshape(gs * atom_rows, width) + dot(mixed, w_out_ref[layer])
        normal_mid = normed(value).astype(BF16)
        gated = dot(normal_mid, w_up_ref[layer])
        gate = gated[:, : 2 * width]
        hidden = (gate / (1.0 + jnp.exp(-gate)) * gated[:, 2 * width :]).astype(BF16)
        value = value + dot(hidden, w_down_ref[layer])
        stream[g] = value.reshape(gs, atom_rows, width)
        return value

    def pool_copy(g):
        return (
            remote(
                psend.at[g, 1], precv.at[g, 0], pool_send.at[0], pool_recv.at[g, 0], right
            ),
            remote(psend.at[g, 0], precv.at[g, 1], pool_send.at[1], pool_recv.at[g, 1], left),
        )

    def count_copy():
        return (
            remote(counts.at[2], counts.at[3], count_send.at[0], count_recv.at[0], right),
            remote(counts.at[0], counts.at[4], count_send.at[1], count_recv.at[1], left),
        )

    def edge_copy(g):
        return (
            remote(
                stream.at[g, :, pl.ds(atom_rows - RIM, RIM), :],
                edge.at[0, g],
                edge_send.at[0],
                edge_recv.at[g, 0],
                right,
            ),
            remote(
                stream.at[g, :, pl.ds(0, RIM), :],
                edge.at[1, g],
                edge_send.at[1],
                edge_recv.at[g, 1],
                left,
            ),
        )

    def token_copy():
        return (
            remote(atom_token_ref, near_token.at[0], token_send.at[0], token_recv.at[0], right),
            remote(atom_token_ref, near_token.at[1], token_send.at[1], token_recv.at[1], left),
        )

    def selects(row):
        spot = row - (me - 1) * token_rows
        return (
            lax.broadcasted_iota(jnp.int32, (3 * token_rows, atom_rows), 0) == spot
        ).astype(F32)

    def back_copy(t):
        return (
            remote(back.at[t, 1], back.at[t, 0], back_send.at[0], back_recv.at[t, 0], right),
            remote(back.at[t, 1], back.at[t, 2], back_send.at[1], back_recv.at[t, 1], left),
        )

    def take_back(g):
        t, base = (g, 0) if waves == GROUPS else (0, g * gs * token_rows)
        if waves == GROUPS:
            exchange(*back_copy(t), False)
        else:

            @pl.when(g == 0)
            def _():
                exchange(*back_copy(0), False)

        exchange(*edge_copy(g), False)
        beyond = []
        for i in range(gs):
            span = pl.ds(pl.multiple_of(base + i * token_rows, token_rows), token_rows)
            near = jnp.concatenate([back[t, j, span, :] for j in range(3)], axis=0)
            stream[g, i] += lax.dot_general(sel, near, FIRST, preferred_element_type=F32)
            for side, rows in ((0, slice(atom_rows - RIM, atom_rows)), (1, slice(0, RIM))):
                picked = lax.dot_general(
                    near_sel[side], near, FIRST, preferred_element_type=F32
                )
                beyond.append(edge[side, g, i] + picked[rows])
        project(ENC_LAYERS, g)
        normal = normed(jnp.concatenate(beyond, axis=0)).astype(BF16)
        key_value = dot(normal, w_qkv_ref[ENC_LAYERS, :, width:]).astype(BF16)
        for i in range(gs):
            at = 2 * i * RIM
            kv[ENC_LAYERS, g, i, 0:RIM, :] = key_value[at : at + RIM]
            kv[ENC_LAYERS, g, i, RIM + atom_rows :, :] = key_value[at + RIM : at + 2 * RIM]

    def run_pair(first, finish):
        def step(g, c):
            if first == ENC_LAYERS:
                take_back(g)
            attend(first, g)
            project(first + 1, g)
            send_halo(first + 1, g)
            if first == 0:
                for group in range(GROUPS):

                    @pl.when(g == group)
                    def _():
                        met(2 + group)

            return c

        lax.fori_loop(0, GROUPS, step, 0)
        if first == 0:
            for number in range(2 + GROUPS, rounds):
                met(number)
            lax.fori_loop(1, n, pair_start, 0)

        def last(g, c):
            finish(g, attend(first + 1, g))
            return c

        lax.fori_loop(0, GROUPS, last, 0)

    loads["qkv"].wait()
    project(0, 0)
    await_signals(barrier, 1)
    signal(ready.at[0], 1)
    send_halo(0, 0)
    project(0, 1)
    send_halo(0, 1)
    met(0)
    loads["atom_token"].wait()
    selector = selects(atom_token_ref[...])
    sel = selector.astype(BF16)
    counted = jnp.broadcast_to(jnp.sum(selector, 1, keepdims=True), (3 * token_rows, 128))
    for j in range(3):
        counts[j] = counted[j * token_rows : (j + 1) * token_rows].astype(BF16)

    exchange(*count_copy(), True)
    exchange(*token_copy(), True)

    def pair_copy(target, slot):
        return remote(
            pair_out.at[(target * per) // samples],
            pair_buf.at[slot],
            pair_send,
            pair_recv,
            target,
        )

    def pair_start(k, c):
        pair_copy(lax.rem(me + k, n), me).start()
        return c

    loads["pair"].wait()
    rows = pair_own[...]
    pair_out[...] = (rows - jnp.max(rows, -1, keepdims=True)).astype(BF16)
    pair_buf[me] = pair_out[own_head]

    def pool(g, value):
        pooled = jnp.maximum(dot(normed(value).astype(BF16), w_pool_ref[...]), 0.0)
        high = pooled.astype(BF16)
        low = (pooled - high.astype(F32)).astype(BF16)
        for i in range(gs):
            at = slice(i * atom_rows, (i + 1) * atom_rows)
            part = dot(sel, high[at]) + dot(sel, low[at])
            psend[g, 0, i] = part[:token_rows].astype(BF16)
            own_sum[g, i] = part[token_rows : 2 * token_rows]
            psend[g, 1, i] = part[2 * token_rows :].astype(BF16)
        exchange(*pool_copy(g), True)
        exchange(*edge_copy(g), True)

    loads["bias"].wait()
    loads["edges"].wait()
    place = lax.broadcasted_iota(jnp.int32, (1, KEY_WINDOW), 1)
    for b in range(blocks):
        position = me * atom_rows - RIM + QUERY_BLOCK * b + place
        allowed = (position >= edges_ref[0, b]) & (position < edges_ref[1, b])
        masked_bias[b] = jnp.where(
            allowed, bias_ref[b].reshape(atom_heads * QUERY_BLOCK, KEY_WINDOW), -1e30
        )

    @pl.when(jnp.logical_not(has_left))
    def _():
        for layer in range(LAYERS):
            for g in range(GROUPS):
                kv[layer, g, :, 0:RIM, :] = jnp.zeros((gs, RIM, 2 * width), BF16)
        for g in range(GROUPS):
            precv[g, 0] = jnp.zeros(precv.shape[2:], BF16)
        for t in range(waves):
            back[t, 0] = jnp.zeros(back.shape[2:], BF16)
        counts[3] = jnp.zeros(counts.shape[1:], BF16)
        edge[0] = jnp.zeros(edge.shape[1:], F32)
        near_token[0] = jnp.full((1, atom_rows), -tokens, jnp.int32)

    @pl.when(jnp.logical_not(has_right))
    def _():
        for layer in range(LAYERS):
            for g in range(GROUPS):
                kv[layer, g, :, RIM + atom_rows :, :] = jnp.zeros((gs, RIM, 2 * width), BF16)
        for g in range(GROUPS):
            precv[g, 1] = jnp.zeros(precv.shape[2:], BF16)
        for t in range(waves):
            back[t, 2] = jnp.zeros(back.shape[2:], BF16)
        counts[4] = jnp.zeros(counts.shape[1:], BF16)
        edge[1] = jnp.zeros(edge.shape[1:], F32)
        near_token[1] = jnp.full((1, atom_rows), -tokens, jnp.int32)

    for name in ("out", "up", "down", "pool"):
        loads[name].wait()
    met(1)
    run_pair(0, pool)
    loads["single"].wait()
    loads["back"].wait()

    exchange(*count_copy(), False)
    number_of = (
        counts[1].astype(F32)[:, :1] + counts[3].astype(F32)[:, :1] + counts[4].astype(F32)[:, :1]
    )
    lanes = 128
    half = lanes // 2
    main = lanes - 2 * head_size
    rest = head_size - main
    lane = lax.broadcasted_iota(jnp.int32, (token_rows, lanes), 1)

    def moved(block, start, to, size=head_size):
        tile, off = start // lanes, start % lanes
        shift = (to - off) % lanes

        def turned(t):
            part = block[:, t * lanes : (t + 1) * lanes]
            return part if shift == 0 else pltpu.roll(part, shift, 1)

        if off + size <= lanes:
            return turned(tile)
        return jnp.where(lane < to + lanes - off, turned(tile), turned(tile + 1))

    def spread(copy_of):
        def step(k, c):
            turn = lax.rem(k + n // 2 - 1, n - 1) + 1
            copy_of(lax.rem(me + turn, n), me).start()
            return c

        lax.fori_loop(1, n, step, 0)

    others = pl.ds(0, n - 1)

    def every_pair():
        return remote(
            pair_buf.at[others], pair_buf.at[others], pair_send, pair_recv, right
        )

    rows_of = item_rows(token_rows, pack, waves)
    starts = (0, rows_of[0])

    def item_copy(t):
        span = pl.ds(starts[t], rows_of[t])
        return lambda target, slot: remote(
            items.at[target, :, span], got.at[slot, :, span], item_send, item_recv.at[t], target
        )

    def every_item(t):
        span = pl.ds(starts[t], rows_of[t])
        return remote(
            items.at[others, :, span], got.at[others, :, span], item_send, item_recv.at[t], right
        )

    def out_copy(t):
        return lambda target, slot: remote(
            outs.at[t, target], returned.at[t, slot], out_send, out_recv.at[t], target
        )

    def every_out(t):
        return remote(
            outs.at[t, others], returned.at[t, others], out_send, out_recv.at[t], right
        )

    def token_project(t):
        for g in range(GROUPS) if waves == 1 else (t,):
            exchange(*pool_copy(g), False)
        for a in range(wave_samples):
            s = t * wave_samples + a
            g, i = s // gs, s % gs
            sums = own_sum[g, i] + precv[g, 0, i].astype(F32) + precv[g, 1, i].astype(F32)
            token_in[s * token_rows : (s + 1) * token_rows, :] = (
                sums / number_of + token_single_ref[...]
            )
        normal_tok = normed(token_in[t * wave_rows : (t + 1) * wave_rows, :]).astype(BF16)
        parts = [
            dot(normal_tok, w_tqkv[:, j * channels : (j + 1) * channels]) for j in range(3)
        ]
        for h in range(heads) if waves == 1 else ():
            start = h * head_size
            for a in range(0, wave_samples, pack):
                keys = []
                for p in range(pack):
                    item = h * samples + a + p
                    owner, unit = item // per, item % per // pack
                    at = slice((a + p) * token_rows, (a + p + 1) * token_rows)
                    v = moved(parts[2][at], start, half * p)
                    q = moved(parts[0][at], start, half * (1 - p))
                    keys.append(moved(parts[1][at], start, half * (1 - p)))
                    low, high = (v, q) if p == 0 else (q, v)
                    tile = jnp.where(lane < head_size, low, jnp.where(lane < half, 1.0, high))
                    items[owner, unit, p * token_rows : (p + 1) * token_rows, :] = tile.astype(
                        BF16
                    )
                key = keys[0] if pack == 1 else jnp.where(lane < half, keys[1], keys[0])
                items[owner, unit, pack * token_rows :, :] = key.astype(BF16)
        if waves == 2:
            one, two = slice(0, token_rows), slice(token_rows, 2 * token_rows)
            for h in range(heads):
                start = h * head_size
                mixed = []
                for upper, lower, at in ((0, 1, one), (1, 0, two)):
                    low = moved(parts[upper][one], start, 0)
                    mid = moved(parts[lower][two], start, head_size)
                    high = moved(parts[2][at], start, 2 * head_size, main)
                    tile = jnp.where(lane < head_size, low, jnp.where(lane < 2 * head_size, mid, high))
                    mixed.append(tile)
                at = starts[t]
                items[h, 0, at : at + 2 * token_rows, :] = jnp.concatenate(mixed, axis=0).astype(BF16)
                tail = jnp.where(
                    lane < rest,
                    moved(parts[2][one], start + main, 0, rest),
                    moved(parts[2][two], start + main, half - rest, rest),
                )
                near, far = tail[: token_rows // 2], tail[token_rows // 2 :]
                tail = jnp.where(lane[: token_rows // 2] < half, near, pltpu.roll(far, half, 1))
                items[h, 0, at + 2 * token_rows : at + rows_of[t], :] = tail.astype(BF16)
        spread(item_copy(t))
        span = pl.ds(starts[t], rows_of[t])
        got[me, :, span] = items[me, :, span]

    token_scale = head_size ** (-0.5)
    tile = 16
    key_lane = lax.broadcasted_iota(jnp.int32, (tokens, lanes), 1)
    out_lane = lax.broadcasted_iota(jnp.int32, (tile * token_rows, lanes), 1)

    def token_attend(t):
        every_item(t).wait_recv()
        for unit in range(units):
            packed = got[:, unit, pack * token_rows :, :].reshape(tokens, lanes)

            def one(block, c):
                span = pl.ds(block * tile, tile)
                ratios = []
                for p in range(pack):
                    at = slice(p * token_rows, (p + 1) * token_rows)
                    mine = key_lane < head_size
                    if p == 0:
                        mine = (key_lane >= half) & (key_lane < half + head_size)
                    keys = jnp.where(mine, packed, jnp.zeros_like(packed))
                    values = got[:, unit, at, :].reshape(tokens, lanes)
                    q = got[span, unit, at, :].reshape(tile * token_rows, lanes)
                    scores = lax.dot_general(q, keys, LAST, preferred_element_type=F32)
                    scores = scores * token_scale + pair_buf[span].astype(F32).reshape(
                        tile * token_rows, tokens
                    )
                    expo = jnp.exp(scores - jnp.max(scores, -1, keepdims=True)).astype(BF16)
                    both = dot(expo, values)
                    ratios.append(both / both[:, head_size : head_size + 1])
                ratio = ratios[0] if pack == 1 else jnp.where(out_lane < half, *ratios)
                outs[t, span, unit, :, :] = ratio.astype(BF16).reshape(tile, token_rows, lanes)
                return c

            if n == tile:
                one(0, 0)
            else:
                lax.fori_loop(0, n // tile, one, 0)
        spread(out_copy(t))
        returned[t, me] = outs[t, me]

    all_lane = lax.broadcasted_iota(jnp.int32, (tokens, lanes), 1)

    def token_pair(t):
        every_item(t).wait_recv()
        at = starts[t]
        one = got[:, 0, at : at + token_rows, :].reshape(tokens, lanes)
        two = got[:, 0, at + token_rows : at + 2 * token_rows, :].reshape(tokens, lanes)
        tail = got[:, 0, at + 2 * token_rows : at + rows_of[t], :].astype(F32)
        flat = tail.reshape(n * token_rows // 2, lanes)
        tail = jnp.concatenate(
            [tail, pltpu.roll(flat, half, 1).reshape(tail.shape)], axis=1
        ).reshape(tokens, lanes)
        tail = jnp.where(all_lane < half, tail, 1.0).astype(BF16)
        bias = pair_buf[...].astype(F32).reshape(tokens, tokens)
        ratios = []
        for a, (q, k) in enumerate(((one, two), (two, one))):
            mine = (all_lane >= a * head_size) & (all_lane < (a + 1) * head_size)
            keys = jnp.where(mine, k, jnp.zeros_like(k))
            scores = lax.dot_general(q, keys, LAST, preferred_element_type=F32)
            scores = scores * token_scale + bias
            expo = jnp.exp(scores - jnp.max(scores, -1, keepdims=True)).astype(BF16)
            both = dot(expo, jnp.concatenate([q, tail], axis=1))
            ratios.append(both / both[:, lanes + half : lanes + half + 1])
        first, second = ratios
        out = jnp.where(
            all_lane >= lanes - main,
            first[:, :lanes],
            jnp.where(
                all_lane < rest,
                first[:, lanes:],
                jnp.where(
                    all_lane < half - rest,
                    pltpu.roll(second[:, :lanes], half - rest, 1),
                    second[:, lanes:],
                ),
            ),
        )
        outs[t, :, 0, :, :] = out.astype(BF16).reshape(n, token_rows, lanes)
        spread(out_copy(t))
        returned[t, me] = outs[t, me]

    def token_finish(t):
        every_out(t).wait_recv()
        state = token_in[t * wave_rows : (t + 1) * wave_rows, :]
        for h in range(heads):
            mix = []
            for a in range(wave_samples):
                item = h * samples + t * wave_samples + a
                owner, unit, p = item // per, item % per // pack - t * units, item % per % pack
                block = returned[t, owner, unit]
                if waves == 2:
                    shift = lanes - rest if a else main
                    block = pltpu.roll(block.astype(F32), shift, 1).astype(BF16)
                elif p == 1:
                    block = pltpu.roll(block.astype(F32), half, 1).astype(BF16)
                mix.append(block[:, :head_size])
            state = state + dot(
                jnp.concatenate(mix, axis=0), w_tout[h * head_size : (h + 1) * head_size, :]
            )
        for a in range(wave_samples):
            state_ref[t * wave_samples + a] = state[a * token_rows : (a + 1) * token_rows]
        back[t, 1] = dot(normed(state).astype(BF16), w_back_ref[...]).astype(BF16)
        exchange(*back_copy(t), True)

    loads["tqkv"].wait()
    for t in range(waves):
        token_project(t)
    every_pair().wait_recv()
    if waves == 1:
        token_attend(0)
    else:
        for t in range(waves):
            token_pair(t)
    loads["tout"].wait()
    for t in range(waves):
        token_finish(t)
    first = ENC_LAYERS

    def finish(g, value):
        normal = normed(value).astype(BF16)
        for i in range(gs):
            s = g * gs + i
            update = lax.dot_general(
                w_final_ref[...],
                normal[i * atom_rows : (i + 1) * atom_rows],
                LAST,
                preferred_element_type=F32,
            )
            sigma, total = sigma_of(s)
            result = (
                SIGMA_DATA * SIGMA_DATA / total * noisy_of(s, sigma)
                + sigma * SIGMA_DATA * lax.rsqrt(total) * update
            ) / SIGMA_DATA
            for c in range(3):
                denoised_ref[c, pl.ds(s, 1), :] = result[c : c + 1]

    loads["final"].wait()
    exchange(*token_copy(), False)
    sent(
        remote(
            stream.at[:, :, pl.ds(0, RIM), :], edge.at[0], edge_send.at[0], edge_recv.at[0, 0], right
        ),
        remote(
            stream.at[:, :, pl.ds(0, RIM), :], edge.at[1], edge_send.at[1], edge_recv.at[0, 1], left
        ),
    )
    near_sel = [selects(near_token[side]).astype(BF16) for side in range(2)]
    run_pair(first, finish)

    sent(
        remote(
            kv.at[pl.ds(0, LAYERS - 1), :, :, pl.ds(0, RIM), :],
            kv.at[pl.ds(0, LAYERS - 1), :, :, pl.ds(0, RIM), :],
            halo_send.at[0],
            halo_recv.at[0, 0, 0],
            right,
        ),
        remote(
            kv.at[pl.ds(0, LAYERS - 1), :, :, pl.ds(0, RIM), :],
            kv.at[pl.ds(0, LAYERS - 1), :, :, pl.ds(0, RIM), :],
            halo_send.at[1],
            halo_recv.at[0, 0, 1],
            left,
        ),
    )
    sent(*count_copy())
    sent(*token_copy())
    sent(
        remote(psend.at[:, 1], precv.at[:, 0], pool_send.at[0], pool_recv.at[0, 0], right),
        remote(psend.at[:, 0], precv.at[:, 1], pool_send.at[1], pool_recv.at[0, 1], left),
    )
    sent(
        remote(back.at[:, 1], back.at[:, 0], back_send.at[0], back_recv.at[0, 0], right),
        remote(back.at[:, 1], back.at[:, 2], back_send.at[1], back_recv.at[0, 1], left),
    )
    every_pair().wait_send()
    for t in range(waves):
        every_item(t).wait_send()
        every_out(t).wait_send()


def store(denoised_ref, state_ref, denoised_out, state_out, sem):
    copies = (
        pltpu.make_async_copy(state_ref, state_out, sem.at[0]),
        pltpu.make_async_copy(denoised_ref, denoised_out, sem.at[1]),
    )
    for copy in copies:
        copy.start()
    for copy in copies:
        copy.wait()


def shards(
    n,
    x_true,
    noise,
    noise_level,
    atom_single,
    atom_token,
    window_edges,
    atom_pair_bias,
    token_single,
    pair_bias,
    w_coord,
    w_atom_qkv,
    w_atom_out,
    w_atom_up,
    w_atom_down,
    w_pool,
    w_token_qkv,
    w_token_out,
    w_back,
    w_final,
):
    samples = noise.shape[0]
    atom_rows, width = atom_single.shape
    token_rows, channels = token_single.shape
    blocks, atom_heads = atom_pair_bias.shape[:2]
    heads = pair_bias.shape[0]
    gs = samples // GROUPS
    per, pack, waves, units = plan(n, heads, samples)
    vmem = pl.BlockSpec(memory_space=pltpu.VMEM)
    anywhere = pl.BlockSpec(memory_space=pl.ANY)
    dma = pltpu.SemaphoreType.DMA
    held = pl.pallas_call(
        functools.partial(kernel, n),
        name="denoise",
        out_shape=(
            pltpu.VMEM((3, samples, atom_rows), F32),
            pltpu.VMEM((samples, token_rows, channels), F32),
        ),
        in_specs=[anywhere] * 19,
        out_specs=(vmem, vmem),
        scratch_shapes=[
            pltpu.SMEM((samples,), jnp.int32),
            pltpu.SMEM((2, blocks), jnp.int32),
            pltpu.VMEM(x_true.shape, F32),
            pltpu.VMEM((3, samples, atom_rows), F32),
            pltpu.VMEM(atom_single.shape, BF16),
            pltpu.VMEM((1, atom_rows), jnp.int32),
            pltpu.VMEM(w_coord.shape, F32),
            pltpu.VMEM(w_final.shape, BF16),
            pltpu.VMEM((GROUPS, gs, atom_rows, width), F32),
            pltpu.VMEM((2, GROUPS, gs, RIM, width), F32),
            pltpu.VMEM((2, 1, atom_rows), jnp.int32),
            pltpu.VMEM((LAYERS, GROUPS, gs, atom_rows + 2 * RIM, 2 * width), BF16),
            pltpu.VMEM((GROUPS, gs * atom_rows, width), BF16),
            pltpu.VMEM((blocks, atom_heads * QUERY_BLOCK, KEY_WINDOW), F32),
            pltpu.VMEM((5, token_rows, 128), BF16),
            pltpu.VMEM((GROUPS, gs, token_rows, channels), F32),
            pltpu.VMEM((GROUPS, 2, gs, token_rows, channels), BF16),
            pltpu.VMEM((GROUPS, 2, gs, token_rows, channels), BF16),
            pltpu.VMEM((samples * token_rows, channels), F32),
            pltpu.VMEM((n, units, sum(item_rows(token_rows, pack, waves)), 128), BF16),
            pltpu.VMEM((n, units, sum(item_rows(token_rows, pack, waves)), 128), BF16),
            pltpu.VMEM(pair_bias.shape, F32),
            pltpu.VMEM(pair_bias.shape, BF16),
            pltpu.VMEM((n, token_rows, n * token_rows), BF16),
            pltpu.VMEM((waves, n, units, token_rows, 128), BF16),
            pltpu.VMEM((waves, n, units, token_rows, 128), BF16),
            pltpu.VMEM((waves, 3, samples // waves * token_rows, width), BF16),
            pltpu.VMEM(w_token_qkv.shape, BF16),
            pltpu.VMEM(w_token_out.shape, BF16),
            pltpu.VMEM(atom_pair_bias.shape, F32),
            pltpu.VMEM(token_single.shape, F32),
            pltpu.VMEM(w_atom_qkv.shape, BF16),
            pltpu.VMEM(w_atom_out.shape, BF16),
            pltpu.VMEM(w_atom_up.shape, BF16),
            pltpu.VMEM(w_atom_down.shape, BF16),
            pltpu.VMEM(w_pool.shape, BF16),
            pltpu.VMEM(w_back.shape, BF16),
            dma((19,)),
            pltpu.SemaphoreType.REGULAR((reach_rounds(n),)),
            dma((2,)),
            dma((LAYERS, GROUPS, 2)),
            dma((2,)),
            dma((2,)),
            dma((2,)),
            dma((GROUPS, 2)),
            dma(()),
            dma(()),
            dma(()),
            dma((waves,)),
            dma(()),
            dma((waves,)),
            dma((2,)),
            dma((waves, 2)),
            dma((2,)),
            dma((GROUPS, 2)),
            dma((2,)),
            dma((2,)),
        ],
        compiler_params=pltpu.CompilerParams(
            collective_id=0, has_side_effects=True, vmem_limit_bytes=56 * 1024 * 1024
        ),
    )(
        noise_level,
        window_edges.T,
        x_true,
        noise.transpose(1, 0, 2),
        atom_single,
        atom_token.reshape(1, atom_rows),
        atom_pair_bias,
        token_single,
        pair_bias,
        w_coord,
        w_atom_qkv,
        w_atom_out,
        w_atom_up,
        w_atom_down,
        w_pool,
        w_token_qkv,
        w_token_out,
        w_back,
        w_final,
    )
    denoised, state = pl.pallas_call(
        store,
        name="store",
        out_shape=(
            jax.ShapeDtypeStruct((3, samples, atom_rows), F32),
            jax.ShapeDtypeStruct((samples, token_rows, channels), F32),
        ),
        in_specs=[vmem] * 2,
        out_specs=(anywhere, anywhere),
        scratch_shapes=[dma((2,))],
    )(*[pltpu.with_memory_space_constraint(x, pltpu.VMEM) for x in held])
    return denoised.transpose(1, 0, 2), state


def solution(mesh):
    in_specs = (
        P(None, ("groups", "seq")),
        P("groups", None, "seq"),
        P("groups"),
        P(("groups", "seq"), None),
        P(("groups", "seq")),
        P(("groups", "seq"), None),
        P(("groups", "seq"), None, None, None),
        P(("groups", "seq"), None),
        P("groups", "seq", None),
    ) + (P(),) * 10
    out_specs = (P("groups", None, "seq"), P("groups", "seq", None))
    return jax.shard_map(
        functools.partial(shards, mesh.shape["seq"]),
        mesh=mesh,
        in_specs=in_specs,
        out_specs=out_specs,
        check_vma=False,
    )
```

```python
import functools

import jax
import jax.numpy as jnp
from jax import lax
from jax.experimental import pallas as pl
from jax.experimental.pallas import tpu as pltpu
from jax.sharding import PartitionSpec as P

QUERY_BLOCK = 32
KEY_WINDOW = 128
ENC_LAYERS = 2
LEVELS = 200
RIM = 48
LAYERS = 4
GROUPS = 2

EPS = 1e-05
SIGMA_DATA = 16.0
MESH = pl.DeviceIdType.MESH
F32 = jnp.float32
BF16 = jnp.bfloat16
LAST = (((1,), (1,)), ((), ()))
FIRST = (((0,), (0,)), ((), ()))


def normed(values):
    centred = values - jnp.mean(values, -1, keepdims=True)
    spread = jnp.mean(centred * centred, -1, keepdims=True)
    return centred * lax.rsqrt(spread + EPS)


def dot(a, b):
    return jnp.dot(a, b, preferred_element_type=F32)


def remote(src, dst, send, recv, target):
    return pltpu.make_async_remote_copy(
        src_ref=src,
        dst_ref=dst,
        send_sem=send,
        recv_sem=recv,
        device_id={"seq": target},
        device_id_type=MESH,
    )


def plan(n, heads, samples):
    per = heads * samples // n
    gs = samples // GROUPS
    pack = 2 if per % 2 == 0 else 1
    waves = GROUPS if per == samples and gs == pack else 1
    return per, pack, waves, per // pack // waves


def reach_rounds(n):
    rounds, known = 0, 1
    while known < n - 1:
        rounds, known = rounds + 1, 2 * known
    return rounds


def item_rows(token_rows, pack, waves):
    if waves == 1:
        return ((pack + 1) * token_rows,)
    return (2 * token_rows + token_rows // 2,) * 2


def kernel(
    n,
    level_hbm,
    edges_hbm,
    x_true_hbm,
    noise_hbm,
    single_hbm,
    atom_token_hbm,
    bias_hbm,
    token_single_hbm,
    pair_hbm,
    w_coord_hbm,
    w_qkv_hbm,
    w_out_hbm,
    w_up_hbm,
    w_down_hbm,
    w_pool_hbm,
    w_tqkv_hbm,
    w_tout_hbm,
    w_back_hbm,
    w_final_hbm,
    denoised_ref,
    state_ref,
    level_ref,
    edges_ref,
    x_true_ref,
    noise_ref,
    single_ref,
    atom_token_ref,
    w_coord_ref,
    w_final_ref,
    stream,
    edge,
    near_token,
    kv,
    queries,
    masked_bias,
    counts,
    own_sum,
    psend,
    precv,
    token_in,
    items,
    got,
    pair_own,
    pair_out,
    pair_buf,
    outs,
    returned,
    back,
    w_tqkv,
    w_tout,
    bias_ref,
    token_single_ref,
    w_qkv_ref,
    w_out_ref,
    w_up_ref,
    w_down_ref,
    w_pool_ref,
    w_back_ref,
    load_sem,
    ready,
    halo_send,
    halo_recv,
    count_send,
    count_recv,
    pool_send,
    pool_recv,
    pair_send,
    pair_recv,
    item_send,
    item_recv,
    out_send,
    out_recv,
    back_send,
    back_recv,
    edge_send,
    edge_recv,
    token_send,
    token_recv,
):
    samples = noise_ref.shape[1]
    atom_rows, width = single_ref.shape
    token_rows, channels = token_single_ref.shape
    blocks, atom_heads = bias_ref.shape[:2]
    atom_head = width // atom_heads
    heads = pair_hbm.shape[0]
    head_size = channels // heads
    tokens = n * token_rows
    gs = samples // GROUPS
    per, pack, waves, units = plan(n, heads, samples)
    wave_samples = samples // waves
    wave_rows = wave_samples * token_rows

    me = lax.axis_index("seq")
    right = lax.rem(me + 1, n)
    left = lax.rem(me + n - 1, n)
    has_left = me > 0
    has_right = me < n - 1

    barrier = pltpu.get_barrier_semaphore()

    def signal(semaphore, reach):
        for there, target in ((me >= reach, me - reach), (me + reach < n, me + reach)):

            @pl.when(there)
            def _():
                pl.semaphore_signal(
                    semaphore, inc=1, device_id={"seq": target}, device_id_type=MESH
                )

    def await_signals(semaphore, reach):
        count = (me >= reach).astype(jnp.int32) + (me + reach < n).astype(jnp.int32)
        pl.semaphore_wait(semaphore, count)

    rounds = reach_rounds(n)
    side = 4 if n % 4 == 0 else 1

    def far_first(k):
        plane = k // side
        plane = lax.rem(me // side + (n // side) // 2 + plane, n // side)
        return plane * side + lax.rem(me + k, side)

    def met(number):
        if number < rounds:
            await_signals(ready.at[number], 2**number)
        if number + 1 < rounds:
            signal(ready.at[number + 1], 2 ** (number + 1))

    own_head = (me * per) // samples
    loads = {}
    for slot, (name, src, dst) in enumerate(
        (
            ("level", level_hbm, level_ref),
            ("x_true", x_true_hbm, x_true_ref),
            ("noise", noise_hbm, noise_ref),
            ("atoms", single_hbm, single_ref),
            ("coord", w_coord_hbm, w_coord_ref),
            ("qkv", w_qkv_hbm, w_qkv_ref),
            ("pair", pair_hbm, pair_own),
            ("atom_token", atom_token_hbm, atom_token_ref),
            ("edges", edges_hbm, edges_ref),
            ("bias", bias_hbm, bias_ref),
            ("out", w_out_hbm, w_out_ref),
            ("up", w_up_hbm, w_up_ref),
            ("down", w_down_hbm, w_down_ref),
            ("pool", w_pool_hbm, w_pool_ref),
            ("single", token_single_hbm, token_single_ref),
            ("tqkv", w_tqkv_hbm, w_tqkv),
            ("back", w_back_hbm, w_back_ref),
            ("tout", w_tout_hbm, w_tout),
            ("final", w_final_hbm, w_final_ref),
        )
    ):
        loads[name] = pltpu.make_async_copy(src, dst, load_sem.at[slot])
        loads[name].start()
        if name == "qkv":
            signal(barrier, 1)

    upper_root = 160.0 ** (1.0 / 7.0)
    lower_root = 0.0004 ** (1.0 / 7.0)

    def sigma_of(s):
        level = jnp.full((1, atom_rows), level_ref[s], jnp.int32).astype(F32)
        base = upper_root + level / (LEVELS - 1) * (lower_root - upper_root)
        square = base * base
        sigma = SIGMA_DATA * (square * square * square * base)
        return sigma, sigma * sigma + SIGMA_DATA * SIGMA_DATA

    def noisy_of(s, sigma):
        noise = jnp.concatenate([noise_ref[c, pl.ds(s, 1), :] for c in range(3)], axis=0)
        return x_true_ref[...] + sigma * noise

    for name in ("level", "x_true", "noise"):
        loads[name].wait()
    scaled = []
    for s in range(samples):
        sigma, total = sigma_of(s)
        scaled.append(noisy_of(s, sigma) * lax.rsqrt(total))
    spare = atom_rows - 3 * samples
    columns = jnp.transpose(
        jnp.concatenate(scaled + [jnp.zeros((spare, atom_rows), F32)], axis=0)
    )
    loads["atoms"].wait()
    loads["coord"].wait()
    single = single_ref[...].astype(F32)
    for s in range(samples):
        value = single
        for c in range(3):
            at = 3 * s + c
            value = value + columns[:, at : at + 1] * w_coord_ref[c : c + 1, :]
        stream[s // gs, s % gs] = value

    def exchange(to_right, to_left, begin):
        if begin:

            @pl.when(has_right)
            def _():
                to_right.start()

            @pl.when(has_left)
            def _():
                to_left.start()

        else:

            @pl.when(has_left)
            def _():
                to_right.wait_recv()

            @pl.when(has_right)
            def _():
                to_left.wait_recv()

    def sent(to_right, to_left):
        @pl.when(has_right)
        def _():
            to_right.wait_send()

        @pl.when(has_left)
        def _():
            to_left.wait_send()

    def halo(layer, g):
        return (
            remote(
                kv.at[layer, g, :, pl.ds(atom_rows, RIM), :],
                kv.at[layer, g, :, pl.ds(0, RIM), :],
                halo_send.at[0],
                halo_recv.at[layer, g, 0],
                right,
            ),
            remote(
                kv.at[layer, g, :, pl.ds(RIM, RIM), :],
                kv.at[layer, g, :, pl.ds(RIM + atom_rows, RIM), :],
                halo_send.at[1],
                halo_recv.at[layer, g, 1],
                left,
            ),
        )

    def project(layer, g):
        normal_in = normed(stream[g].reshape(gs * atom_rows, width)).astype(BF16)
        key_value = dot(normal_in, w_qkv_ref[layer, :, width:]).astype(BF16)
        for i in range(gs):
            kv[layer, g, i, RIM : RIM + atom_rows, :] = key_value[
                i * atom_rows : (i + 1) * atom_rows
            ]
        queries[g] = dot(normal_in, w_qkv_ref[layer, :, :width]).astype(BF16)

    def send_halo(layer, g):
        exchange(*halo(layer, g), True)

    stacked = atom_heads * QUERY_BLOCK
    row_head = lax.broadcasted_iota(jnp.int32, (stacked, width), 0) // QUERY_BLOCK
    lane_head = lax.broadcasted_iota(jnp.int32, (stacked, width), 1) // atom_head
    own_lanes = row_head == lane_head
    few_lanes = lane_head[:QUERY_BLOCK]
    scale = atom_head ** (-0.5)
    ones = jnp.ones((KEY_WINDOW, width), BF16)

    def attend(layer, g):
        if layer != ENC_LAYERS:
            exchange(*halo(layer, g), False)
        mixed = []
        pairs = [(i, b) for i in range(gs) for b in range(blocks)]
        for start in range(0, len(pairs), 8):
            part = pairs[start : start + 8]
            scores = []
            for i, b in part:
                q = queries[g, pl.ds(i * atom_rows + b * QUERY_BLOCK, QUERY_BLOCK), :]
                q = jnp.concatenate([q] * atom_heads, axis=0)
                q = jnp.where(own_lanes, q, jnp.zeros_like(q))
                key_win = kv[layer, g, i, QUERY_BLOCK * b : QUERY_BLOCK * b + KEY_WINDOW, :width]
                score = lax.dot_general(q, key_win, LAST, preferred_element_type=F32)
                scores.append(score * scale + masked_bias[b])
            tops = [jnp.max(score, -1, keepdims=True) for score in scores]
            expos = [jnp.exp(score - top).astype(BF16) for score, top in zip(scores, tops)]
            sums = []
            for (i, b), expo in zip(part, expos):
                value_win = kv[layer, g, i, QUERY_BLOCK * b : QUERY_BLOCK * b + KEY_WINDOW, width:]
                sums.append(dot(expo, jnp.concatenate([value_win, ones], axis=1)))
            for both in sums:
                picked = both[:QUERY_BLOCK]
                number, below = picked[:, :width], picked[:, width:]
                for h in range(1, atom_heads):
                    rows = both[h * QUERY_BLOCK : (h + 1) * QUERY_BLOCK]
                    number = jnp.where(few_lanes == h, rows[:, :width], number)
                    below = jnp.where(few_lanes == h, rows[:, width:], below)
                mixed.append((number / below).astype(BF16))
        mixed = jnp.concatenate(mixed, axis=0)
        value = stream[g].reshape(gs * atom_rows, width) + dot(mixed, w_out_ref[layer])
        normal_mid = normed(value).astype(BF16)
        gated = dot(normal_mid, w_up_ref[layer])
        gate = gated[:, : 2 * width]
        hidden = (gate / (1.0 + jnp.exp(-gate)) * gated[:, 2 * width :]).astype(BF16)
        value = value + dot(hidden, w_down_ref[layer])
        stream[g] = value.reshape(gs, atom_rows, width)
        return value

    def pool_copy(g):
        return (
            remote(
                psend.at[g, 1], precv.at[g, 0], pool_send.at[0], pool_recv.at[g, 0], right
            ),
            remote(psend.at[g, 0], precv.at[g, 1], pool_send.at[1], pool_recv.at[g, 1], left),
        )

    def count_copy():
        return (
            remote(counts.at[2], counts.at[3], count_send.at[0], count_recv.at[0], right),
            remote(counts.at[0], counts.at[4], count_send.at[1], count_recv.at[1], left),
        )

    def edge_copy(g):
        return (
            remote(
                stream.at[g, :, pl.ds(atom_rows - RIM, RIM), :],
                edge.at[0, g],
                edge_send.at[0],
                edge_recv.at[g, 0],
                right,
            ),
            remote(
                stream.at[g, :, pl.ds(0, RIM), :],
                edge.at[1, g],
                edge_send.at[1],
                edge_recv.at[g, 1],
                left,
            ),
        )

    def token_copy():
        return (
            remote(atom_token_ref, near_token.at[0], token_send.at[0], token_recv.at[0], right),
            remote(atom_token_ref, near_token.at[1], token_send.at[1], token_recv.at[1], left),
        )

    def selects(row):
        spot = row - (me - 1) * token_rows
        return (
            lax.broadcasted_iota(jnp.int32, (3 * token_rows, atom_rows), 0) == spot
        ).astype(F32)

    def back_copy(t):
        return (
            remote(back.at[t, 1], back.at[t, 0], back_send.at[0], back_recv.at[t, 0], right),
            remote(back.at[t, 1], back.at[t, 2], back_send.at[1], back_recv.at[t, 1], left),
        )

    def take_back(g):
        t, base = (g, 0) if waves == GROUPS else (0, g * gs * token_rows)
        if waves == GROUPS:
            exchange(*back_copy(t), False)
        else:

            @pl.when(g == 0)
            def _():
                exchange(*back_copy(0), False)

        exchange(*edge_copy(g), False)
        beyond = []
        for i in range(gs):
            span = pl.ds(pl.multiple_of(base + i * token_rows, token_rows), token_rows)
            near = jnp.concatenate([back[t, j, span, :] for j in range(3)], axis=0)
            stream[g, i] += lax.dot_general(sel, near, FIRST, preferred_element_type=F32)
            for side, rows in ((0, slice(atom_rows - RIM, atom_rows)), (1, slice(0, RIM))):
                picked = lax.dot_general(
                    near_sel[side], near, FIRST, preferred_element_type=F32
                )
                beyond.append(edge[side, g, i] + picked[rows])
        project(ENC_LAYERS, g)
        normal = normed(jnp.concatenate(beyond, axis=0)).astype(BF16)
        key_value = dot(normal, w_qkv_ref[ENC_LAYERS, :, width:]).astype(BF16)
        for i in range(gs):
            at = 2 * i * RIM
            kv[ENC_LAYERS, g, i, 0:RIM, :] = key_value[at : at + RIM]
            kv[ENC_LAYERS, g, i, RIM + atom_rows :, :] = key_value[at + RIM : at + 2 * RIM]

    def run_pair(first, finish):
        def step(g, c):
            if first == ENC_LAYERS:
                take_back(g)
            attend(first, g)
            project(first + 1, g)
            send_halo(first + 1, g)
            if first == 0:
                for group in range(GROUPS):

                    @pl.when(g == group)
                    def _():
                        met(2 + group)

            return c

        lax.fori_loop(0, GROUPS, step, 0)
        if first == 0:
            for number in range(2 + GROUPS, rounds):
                met(number)
            lax.fori_loop(1, n, pair_start, 0)

        def last(g, c):
            finish(g, attend(first + 1, g))
            return c

        lax.fori_loop(0, GROUPS, last, 0)

    loads["qkv"].wait()
    project(0, 0)
    await_signals(barrier, 1)
    signal(ready.at[0], 1)
    send_halo(0, 0)
    project(0, 1)
    send_halo(0, 1)
    met(0)
    loads["atom_token"].wait()
    selector = selects(atom_token_ref[...])
    sel = selector.astype(BF16)
    counted = jnp.broadcast_to(jnp.sum(selector, 1, keepdims=True), (3 * token_rows, 128))
    for j in range(3):
        counts[j] = counted[j * token_rows : (j + 1) * token_rows].astype(BF16)

    exchange(*count_copy(), True)
    exchange(*token_copy(), True)

    def pair_copy(target, slot):
        return remote(
            pair_out.at[(target * per) // samples],
            pair_buf.at[slot],
            pair_send,
            pair_recv,
            target,
        )

    def pair_start(k, c):
        pair_copy(lax.rem(me + k, n), me).start()
        return c

    loads["pair"].wait()
    rows = pair_own[...]
    pair_out[...] = (rows - jnp.max(rows, -1, keepdims=True)).astype(BF16)
    pair_buf[me] = pair_out[own_head]

    def pool(g, value):
        pooled = jnp.maximum(dot(normed(value).astype(BF16), w_pool_ref[...]), 0.0)
        high = pooled.astype(BF16)
        low = (pooled - high.astype(F32)).astype(BF16)
        for i in range(gs):
            at = slice(i * atom_rows, (i + 1) * atom_rows)
            part = dot(sel, high[at]) + dot(sel, low[at])
            psend[g, 0, i] = part[:token_rows].astype(BF16)
            own_sum[g, i] = part[token_rows : 2 * token_rows]
            psend[g, 1, i] = part[2 * token_rows :].astype(BF16)
        exchange(*pool_copy(g), True)
        exchange(*edge_copy(g), True)

    loads["bias"].wait()
    loads["edges"].wait()
    place = lax.broadcasted_iota(jnp.int32, (1, KEY_WINDOW), 1)
    for b in range(blocks):
        position = me * atom_rows - RIM + QUERY_BLOCK * b + place
        allowed = (position >= edges_ref[0, b]) & (position < edges_ref[1, b])
        masked_bias[b] = jnp.where(
            allowed, bias_ref[b].reshape(atom_heads * QUERY_BLOCK, KEY_WINDOW), -1e30
        )

    @pl.when(jnp.logical_not(has_left))
    def _():
        for layer in range(LAYERS):
            for g in range(GROUPS):
                kv[layer, g, :, 0:RIM, :] = jnp.zeros((gs, RIM, 2 * width), BF16)
        for g in range(GROUPS):
            precv[g, 0] = jnp.zeros(precv.shape[2:], BF16)
        for t in range(waves):
            back[t, 0] = jnp.zeros(back.shape[2:], BF16)
        counts[3] = jnp.zeros(counts.shape[1:], BF16)
        edge[0] = jnp.zeros(edge.shape[1:], F32)
        near_token[0] = jnp.full((1, atom_rows), -tokens, jnp.int32)

    @pl.when(jnp.logical_not(has_right))
    def _():
        for layer in range(LAYERS):
            for g in range(GROUPS):
                kv[layer, g, :, RIM + atom_rows :, :] = jnp.zeros((gs, RIM, 2 * width), BF16)
        for g in range(GROUPS):
            precv[g, 1] = jnp.zeros(precv.shape[2:], BF16)
        for t in range(waves):
            back[t, 2] = jnp.zeros(back.shape[2:], BF16)
        counts[4] = jnp.zeros(counts.shape[1:], BF16)
        edge[1] = jnp.zeros(edge.shape[1:], F32)
        near_token[1] = jnp.full((1, atom_rows), -tokens, jnp.int32)

    for name in ("out", "up", "down", "pool"):
        loads[name].wait()
    met(1)
    run_pair(0, pool)
    loads["single"].wait()
    loads["back"].wait()

    exchange(*count_copy(), False)
    number_of = (
        counts[1].astype(F32)[:, :1] + counts[3].astype(F32)[:, :1] + counts[4].astype(F32)[:, :1]
    )
    lanes = 128
    half = lanes // 2
    main = lanes - 2 * head_size
    rest = head_size - main
    lane = lax.broadcasted_iota(jnp.int32, (token_rows, lanes), 1)

    def moved(block, start, to, size=head_size):
        tile, off = start // lanes, start % lanes
        shift = (to - off) % lanes

        def turned(t):
            part = block[:, t * lanes : (t + 1) * lanes]
            return part if shift == 0 else pltpu.roll(part, shift, 1)

        if off + size <= lanes:
            return turned(tile)
        return jnp.where(lane < to + lanes - off, turned(tile), turned(tile + 1))

    def spread(copy_of):
        def step(k, c):
            target = far_first(k)

            @pl.when(target != me)
            def _():
                copy_of(target, me).start()

            return c

        lax.fori_loop(0, n, step, 0)

    others = pl.ds(0, n - 1)

    def every_pair():
        return remote(
            pair_buf.at[others], pair_buf.at[others], pair_send, pair_recv, right
        )

    rows_of = item_rows(token_rows, pack, waves)
    starts = (0, rows_of[0])

    def item_copy(t):
        span = pl.ds(starts[t], rows_of[t])
        return lambda target, slot: remote(
            items.at[target, :, span], got.at[slot, :, span], item_send, item_recv.at[t], target
        )

    def every_item(t):
        span = pl.ds(starts[t], rows_of[t])
        return remote(
            items.at[others, :, span], got.at[others, :, span], item_send, item_recv.at[t], right
        )

    def out_copy(t):
        return lambda target, slot: remote(
            outs.at[t, target], returned.at[t, slot], out_send, out_recv.at[t], target
        )

    def every_out(t):
        return remote(
            outs.at[t, others], returned.at[t, others], out_send, out_recv.at[t], right
        )

    def token_project(t):
        for g in range(GROUPS) if waves == 1 else (t,):
            exchange(*pool_copy(g), False)
        for a in range(wave_samples):
            s = t * wave_samples + a
            g, i = s // gs, s % gs
            sums = own_sum[g, i] + precv[g, 0, i].astype(F32) + precv[g, 1, i].astype(F32)
            token_in[s * token_rows : (s + 1) * token_rows, :] = (
                sums / number_of + token_single_ref[...]
            )
        normal_tok = normed(token_in[t * wave_rows : (t + 1) * wave_rows, :]).astype(BF16)
        parts = [
            dot(normal_tok, w_tqkv[:, j * channels : (j + 1) * channels]) for j in range(3)
        ]
        for h in range(heads) if waves == 1 else ():
            start = h * head_size
            for a in range(0, wave_samples, pack):
                keys = []
                for p in range(pack):
                    item = h * samples + a + p
                    owner, unit = item // per, item % per // pack
                    at = slice((a + p) * token_rows, (a + p + 1) * token_rows)
                    v = moved(parts[2][at], start, half * p)
                    q = moved(parts[0][at], start, half * (1 - p))
                    keys.append(moved(parts[1][at], start, half * (1 - p)))
                    low, high = (v, q) if p == 0 else (q, v)
                    tile = jnp.where(lane < head_size, low, jnp.where(lane < half, 1.0, high))
                    items[owner, unit, p * token_rows : (p + 1) * token_rows, :] = tile.astype(
                        BF16
                    )
                key = keys[0] if pack == 1 else jnp.where(lane < half, keys[1], keys[0])
                items[owner, unit, pack * token_rows :, :] = key.astype(BF16)
        if waves == 2:
            one, two = slice(0, token_rows), slice(token_rows, 2 * token_rows)
            for h in range(heads):
                start = h * head_size
                mixed = []
                for upper, lower, at in ((0, 1, one), (1, 0, two)):
                    low = moved(parts[upper][one], start, 0)
                    mid = moved(parts[lower][two], start, head_size)
                    high = moved(parts[2][at], start, 2 * head_size, main)
                    tile = jnp.where(lane < head_size, low, jnp.where(lane < 2 * head_size, mid, high))
                    mixed.append(tile)
                at = starts[t]
                items[h, 0, at : at + 2 * token_rows, :] = jnp.concatenate(mixed, axis=0).astype(BF16)
                tail = jnp.where(
                    lane < rest,
                    moved(parts[2][one], start + main, 0, rest),
                    moved(parts[2][two], start + main, half - rest, rest),
                )
                near, far = tail[: token_rows // 2], tail[token_rows // 2 :]
                tail = jnp.where(lane[: token_rows // 2] < half, near, pltpu.roll(far, half, 1))
                items[h, 0, at + 2 * token_rows : at + rows_of[t], :] = tail.astype(BF16)
        spread(item_copy(t))
        span = pl.ds(starts[t], rows_of[t])
        got[me, :, span] = items[me, :, span]

    token_scale = head_size ** (-0.5)
    tile = 16
    key_lane = lax.broadcasted_iota(jnp.int32, (tokens, lanes), 1)
    out_lane = lax.broadcasted_iota(jnp.int32, (tile * token_rows, lanes), 1)

    def token_attend(t):
        every_item(t).wait_recv()
        for unit in range(units):
            packed = got[:, unit, pack * token_rows :, :].reshape(tokens, lanes)

            def one(block, c):
                span = pl.ds(block * tile, tile)
                ratios = []
                for p in range(pack):
                    at = slice(p * token_rows, (p + 1) * token_rows)
                    mine = key_lane < head_size
                    if p == 0:
                        mine = (key_lane >= half) & (key_lane < half + head_size)
                    keys = jnp.where(mine, packed, jnp.zeros_like(packed))
                    values = got[:, unit, at, :].reshape(tokens, lanes)
                    q = got[span, unit, at, :].reshape(tile * token_rows, lanes)
                    scores = lax.dot_general(q, keys, LAST, preferred_element_type=F32)
                    scores = scores * token_scale + pair_buf[span].astype(F32).reshape(
                        tile * token_rows, tokens
                    )
                    expo = jnp.exp(scores - jnp.max(scores, -1, keepdims=True)).astype(BF16)
                    both = dot(expo, values)
                    ratios.append(both / both[:, head_size : head_size + 1])
                ratio = ratios[0] if pack == 1 else jnp.where(out_lane < half, *ratios)
                outs[t, span, unit, :, :] = ratio.astype(BF16).reshape(tile, token_rows, lanes)
                return c

            if n == tile:
                one(0, 0)
            else:
                lax.fori_loop(0, n // tile, one, 0)
        spread(out_copy(t))
        returned[t, me] = outs[t, me]

    all_lane = lax.broadcasted_iota(jnp.int32, (tokens, lanes), 1)

    def token_pair(t):
        every_item(t).wait_recv()
        at = starts[t]
        one = got[:, 0, at : at + token_rows, :].reshape(tokens, lanes)
        two = got[:, 0, at + token_rows : at + 2 * token_rows, :].reshape(tokens, lanes)
        tail = got[:, 0, at + 2 * token_rows : at + rows_of[t], :].astype(F32)
        flat = tail.reshape(n * token_rows // 2, lanes)
        tail = jnp.concatenate(
            [tail, pltpu.roll(flat, half, 1).reshape(tail.shape)], axis=1
        ).reshape(tokens, lanes)
        tail = jnp.where(all_lane < half, tail, 1.0).astype(BF16)
        bias = pair_buf[...].astype(F32).reshape(tokens, tokens)
        ratios = []
        for a, (q, k) in enumerate(((one, two), (two, one))):
            mine = (all_lane >= a * head_size) & (all_lane < (a + 1) * head_size)
            keys = jnp.where(mine, k, jnp.zeros_like(k))
            scores = lax.dot_general(q, keys, LAST, preferred_element_type=F32)
            scores = scores * token_scale + bias
            expo = jnp.exp(scores - jnp.max(scores, -1, keepdims=True)).astype(BF16)
            both = dot(expo, jnp.concatenate([q, tail], axis=1))
            ratios.append(both / both[:, lanes + half : lanes + half + 1])
        first, second = ratios
        out = jnp.where(
            all_lane >= lanes - main,
            first[:, :lanes],
            jnp.where(
                all_lane < rest,
                first[:, lanes:],
                jnp.where(
                    all_lane < half - rest,
                    pltpu.roll(second[:, :lanes], half - rest, 1),
                    second[:, lanes:],
                ),
            ),
        )
        outs[t, :, 0, :, :] = out.astype(BF16).reshape(n, token_rows, lanes)
        spread(out_copy(t))
        returned[t, me] = outs[t, me]

    def token_finish(t):
        every_out(t).wait_recv()
        state = token_in[t * wave_rows : (t + 1) * wave_rows, :]
        if waves == 2:
            samples_mixed = []
            for a in range(wave_samples):
                begin = half - main - rest if a else lanes - main
                tiles = [None] * (channels // lanes)
                for h in range(heads):
                    low = h * head_size
                    block = returned[t, h, 0].astype(F32)
                    turned = pltpu.roll(block, (low - begin) % lanes, 1)
                    for j in range(low // lanes, (low + head_size - 1) // lanes + 1):
                        above = lane + j * lanes >= low
                        tiles[j] = turned if tiles[j] is None else jnp.where(above, turned, tiles[j])
                samples_mixed.append(jnp.concatenate(tiles, axis=1))
            mixed = jnp.concatenate(samples_mixed, axis=0).astype(BF16)
            state = state + dot(mixed, w_tout[...])
        for h in range(heads) if waves == 1 else ():
            mix = []
            for a in range(wave_samples):
                item = h * samples + t * wave_samples + a
                owner, unit, p = item // per, item % per // pack - t * units, item % per % pack
                block = returned[t, owner, unit]
                if p == 1:
                    block = pltpu.roll(block.astype(F32), half, 1).astype(BF16)
                mix.append(block[:, :head_size])
            state = state + dot(
                jnp.concatenate(mix, axis=0), w_tout[h * head_size : (h + 1) * head_size, :]
            )
        for a in range(wave_samples):
            state_ref[t * wave_samples + a] = state[a * token_rows : (a + 1) * token_rows]
        back[t, 1] = dot(normed(state).astype(BF16), w_back_ref[...]).astype(BF16)
        exchange(*back_copy(t), True)

    loads["tqkv"].wait()
    for t in range(waves):
        token_project(t)
    every_pair().wait_recv()
    if waves == 1:
        token_attend(0)
    else:
        for t in range(waves):
            token_pair(t)
    loads["tout"].wait()
    for t in range(waves):
        token_finish(t)
    first = ENC_LAYERS

    def finish(g, value):
        normal = normed(value).astype(BF16)
        for i in range(gs):
            s = g * gs + i
            update = lax.dot_general(
                w_final_ref[...],
                normal[i * atom_rows : (i + 1) * atom_rows],
                LAST,
                preferred_element_type=F32,
            )
            sigma, total = sigma_of(s)
            result = (
                SIGMA_DATA * SIGMA_DATA / total * noisy_of(s, sigma)
                + sigma * SIGMA_DATA * lax.rsqrt(total) * update
            ) / SIGMA_DATA
            for c in range(3):
                denoised_ref[c, pl.ds(s, 1), :] = result[c : c + 1]

    loads["final"].wait()
    exchange(*token_copy(), False)
    sent(
        remote(
            stream.at[:, :, pl.ds(0, RIM), :], edge.at[0], edge_send.at[0], edge_recv.at[0, 0], right
        ),
        remote(
            stream.at[:, :, pl.ds(0, RIM), :], edge.at[1], edge_send.at[1], edge_recv.at[0, 1], left
        ),
    )
    near_sel = [selects(near_token[side]).astype(BF16) for side in range(2)]
    run_pair(first, finish)

    sent(
        remote(
            kv.at[pl.ds(0, LAYERS - 1), :, :, pl.ds(0, RIM), :],
            kv.at[pl.ds(0, LAYERS - 1), :, :, pl.ds(0, RIM), :],
            halo_send.at[0],
            halo_recv.at[0, 0, 0],
            right,
        ),
        remote(
            kv.at[pl.ds(0, LAYERS - 1), :, :, pl.ds(0, RIM), :],
            kv.at[pl.ds(0, LAYERS - 1), :, :, pl.ds(0, RIM), :],
            halo_send.at[1],
            halo_recv.at[0, 0, 1],
            left,
        ),
    )
    sent(*count_copy())
    sent(*token_copy())
    sent(
        remote(psend.at[:, 1], precv.at[:, 0], pool_send.at[0], pool_recv.at[0, 0], right),
        remote(psend.at[:, 0], precv.at[:, 1], pool_send.at[1], pool_recv.at[0, 1], left),
    )
    sent(
        remote(back.at[:, 1], back.at[:, 0], back_send.at[0], back_recv.at[0, 0], right),
        remote(back.at[:, 1], back.at[:, 2], back_send.at[1], back_recv.at[0, 1], left),
    )
    every_pair().wait_send()
    for t in range(waves):
        every_item(t).wait_send()
        every_out(t).wait_send()


def store(denoised_ref, state_ref, denoised_out, state_out, sem):
    copies = (
        pltpu.make_async_copy(state_ref, state_out, sem.at[0]),
        pltpu.make_async_copy(denoised_ref, denoised_out, sem.at[1]),
    )
    for copy in copies:
        copy.start()
    for copy in copies:
        copy.wait()


def shards(
    n,
    x_true,
    noise,
    noise_level,
    atom_single,
    atom_token,
    window_edges,
    atom_pair_bias,
    token_single,
    pair_bias,
    w_coord,
    w_atom_qkv,
    w_atom_out,
    w_atom_up,
    w_atom_down,
    w_pool,
    w_token_qkv,
    w_token_out,
    w_back,
    w_final,
):
    samples = noise.shape[0]
    atom_rows, width = atom_single.shape
    token_rows, channels = token_single.shape
    blocks, atom_heads = atom_pair_bias.shape[:2]
    heads = pair_bias.shape[0]
    gs = samples // GROUPS
    per, pack, waves, units = plan(n, heads, samples)
    vmem = pl.BlockSpec(memory_space=pltpu.VMEM)
    anywhere = pl.BlockSpec(memory_space=pl.ANY)
    dma = pltpu.SemaphoreType.DMA
    held = pl.pallas_call(
        functools.partial(kernel, n),
        name="denoise",
        out_shape=(
            pltpu.VMEM((3, samples, atom_rows), F32),
            pltpu.VMEM((samples, token_rows, channels), F32),
        ),
        in_specs=[anywhere] * 19,
        out_specs=(vmem, vmem),
        scratch_shapes=[
            pltpu.SMEM((samples,), jnp.int32),
            pltpu.SMEM((2, blocks), jnp.int32),
            pltpu.VMEM(x_true.shape, F32),
            pltpu.VMEM((3, samples, atom_rows), F32),
            pltpu.VMEM(atom_single.shape, BF16),
            pltpu.VMEM((1, atom_rows), jnp.int32),
            pltpu.VMEM(w_coord.shape, F32),
            pltpu.VMEM(w_final.shape, BF16),
            pltpu.VMEM((GROUPS, gs, atom_rows, width), F32),
            pltpu.VMEM((2, GROUPS, gs, RIM, width), F32),
            pltpu.VMEM((2, 1, atom_rows), jnp.int32),
            pltpu.VMEM((LAYERS, GROUPS, gs, atom_rows + 2 * RIM, 2 * width), BF16),
            pltpu.VMEM((GROUPS, gs * atom_rows, width), BF16),
            pltpu.VMEM((blocks, atom_heads * QUERY_BLOCK, KEY_WINDOW), F32),
            pltpu.VMEM((5, token_rows, 128), BF16),
            pltpu.VMEM((GROUPS, gs, token_rows, channels), F32),
            pltpu.VMEM((GROUPS, 2, gs, token_rows, channels), BF16),
            pltpu.VMEM((GROUPS, 2, gs, token_rows, channels), BF16),
            pltpu.VMEM((samples * token_rows, channels), F32),
            pltpu.VMEM((n, units, sum(item_rows(token_rows, pack, waves)), 128), BF16),
            pltpu.VMEM((n, units, sum(item_rows(token_rows, pack, waves)), 128), BF16),
            pltpu.VMEM(pair_bias.shape, F32),
            pltpu.VMEM(pair_bias.shape, BF16),
            pltpu.VMEM((n, token_rows, n * token_rows), BF16),
            pltpu.VMEM((waves, n, units, token_rows, 128), BF16),
            pltpu.VMEM((waves, n, units, token_rows, 128), BF16),
            pltpu.VMEM((waves, 3, samples // waves * token_rows, width), BF16),
            pltpu.VMEM(w_token_qkv.shape, BF16),
            pltpu.VMEM(w_token_out.shape, BF16),
            pltpu.VMEM(atom_pair_bias.shape, F32),
            pltpu.VMEM(token_single.shape, F32),
            pltpu.VMEM(w_atom_qkv.shape, BF16),
            pltpu.VMEM(w_atom_out.shape, BF16),
            pltpu.VMEM(w_atom_up.shape, BF16),
            pltpu.VMEM(w_atom_down.shape, BF16),
            pltpu.VMEM(w_pool.shape, BF16),
            pltpu.VMEM(w_back.shape, BF16),
            dma((19,)),
            pltpu.SemaphoreType.REGULAR((reach_rounds(n),)),
            dma((2,)),
            dma((LAYERS, GROUPS, 2)),
            dma((2,)),
            dma((2,)),
            dma((2,)),
            dma((GROUPS, 2)),
            dma(()),
            dma(()),
            dma(()),
            dma((waves,)),
            dma(()),
            dma((waves,)),
            dma((2,)),
            dma((waves, 2)),
            dma((2,)),
            dma((GROUPS, 2)),
            dma((2,)),
            dma((2,)),
        ],
        compiler_params=pltpu.CompilerParams(
            collective_id=0, has_side_effects=True, vmem_limit_bytes=56 * 1024 * 1024
        ),
    )(
        noise_level,
        window_edges.T,
        x_true,
        noise.transpose(1, 0, 2),
        atom_single,
        atom_token.reshape(1, atom_rows),
        atom_pair_bias,
        token_single,
        pair_bias,
        w_coord,
        w_atom_qkv,
        w_atom_out,
        w_atom_up,
        w_atom_down,
        w_pool,
        w_token_qkv,
        w_token_out,
        w_back,
        w_final,
    )
    denoised, state = pl.pallas_call(
        store,
        name="store",
        out_shape=(
            jax.ShapeDtypeStruct((3, samples, atom_rows), F32),
            jax.ShapeDtypeStruct((samples, token_rows, channels), F32),
        ),
        in_specs=[vmem] * 2,
        out_specs=(anywhere, anywhere),
        scratch_shapes=[dma((2,))],
    )(*[pltpu.with_memory_space_constraint(x, pltpu.VMEM) for x in held])
    return denoised.transpose(1, 0, 2), state


def solution(mesh):
    in_specs = (
        P(None, ("groups", "seq")),
        P("groups", None, "seq"),
        P("groups"),
        P(("groups", "seq"), None),
        P(("groups", "seq")),
        P(("groups", "seq"), None),
        P(("groups", "seq"), None, None, None),
        P(("groups", "seq"), None),
        P("groups", "seq", None),
    ) + (P(),) * 10
    out_specs = (P("groups", None, "seq"), P("groups", "seq", None))
    return jax.shard_map(
        functools.partial(shards, mesh.shape["seq"]),
        mesh=mesh,
        in_specs=in_specs,
        out_specs=out_specs,
        check_vma=False,
    )
```

```python
import functools

import jax
import jax.numpy as jnp
from jax import lax
from jax.experimental import pallas as pl
from jax.experimental.pallas import tpu as pltpu
from jax.sharding import PartitionSpec as P

QUERY_BLOCK = 32
KEY_WINDOW = 128
ENC_LAYERS = 2
LEVELS = 200
RIM = 48
LAYERS = 4
GROUPS = 2

EPS = 1e-05
SIGMA_DATA = 16.0
MESH = pl.DeviceIdType.MESH
F32 = jnp.float32
BF16 = jnp.bfloat16
LAST = (((1,), (1,)), ((), ()))
FIRST = (((0,), (0,)), ((), ()))


def normed(values):
    centred = values - jnp.mean(values, -1, keepdims=True)
    spread = jnp.mean(centred * centred, -1, keepdims=True)
    return centred * lax.rsqrt(spread + EPS)


def dot(a, b):
    return jnp.dot(a, b, preferred_element_type=F32)


def remote(src, dst, send, recv, target):
    return pltpu.make_async_remote_copy(
        src_ref=src,
        dst_ref=dst,
        send_sem=send,
        recv_sem=recv,
        device_id={"seq": target},
        device_id_type=MESH,
    )


def plan(n, heads, samples):
    per = heads * samples // n
    gs = samples // GROUPS
    pack = 2 if per % 2 == 0 else 1
    waves = GROUPS if per == samples and gs == pack else 1
    return per, pack, waves, per // pack // waves


def reach_rounds(n):
    rounds, known = 0, 1
    while known < n - 1:
        rounds, known = rounds + 1, 2 * known
    return rounds


def item_rows(token_rows, pack, waves):
    if waves == 1:
        return ((pack + 1) * token_rows,)
    return (2 * token_rows + token_rows // 2,) * 2


def kernel(
    n,
    level_hbm,
    edges_hbm,
    x_true_hbm,
    noise_hbm,
    single_hbm,
    atom_token_hbm,
    bias_hbm,
    token_single_hbm,
    pair_hbm,
    w_coord_hbm,
    w_qkv_hbm,
    w_out_hbm,
    w_up_hbm,
    w_down_hbm,
    w_pool_hbm,
    w_tqkv_hbm,
    w_tout_hbm,
    w_back_hbm,
    w_final_hbm,
    denoised_ref,
    state_ref,
    level_ref,
    edges_ref,
    x_true_ref,
    noise_ref,
    single_ref,
    atom_token_ref,
    w_coord_ref,
    w_final_ref,
    stream,
    edge,
    rim,
    near_token,
    kv,
    queries,
    masked_bias,
    counts,
    own_sum,
    psend,
    precv,
    token_in,
    items,
    got,
    pair_own,
    pair_out,
    pair_buf,
    outs,
    returned,
    back,
    w_tqkv,
    w_tout,
    bias_ref,
    token_single_ref,
    w_qkv_ref,
    w_out_ref,
    w_up_ref,
    w_down_ref,
    w_pool_ref,
    w_back_ref,
    load_sem,
    ready,
    halo_send,
    halo_recv,
    count_send,
    count_recv,
    pool_send,
    pool_recv,
    pair_send,
    pair_recv,
    item_send,
    item_recv,
    out_send,
    out_recv,
    back_send,
    back_recv,
    edge_send,
    edge_recv,
    token_send,
    token_recv,
):
    samples = noise_ref.shape[1]
    atom_rows, width = single_ref.shape
    token_rows, channels = token_single_ref.shape
    blocks, atom_heads = bias_ref.shape[:2]
    atom_head = width // atom_heads
    heads = pair_hbm.shape[0]
    head_size = channels // heads
    tokens = n * token_rows
    gs = samples // GROUPS
    per, pack, waves, units = plan(n, heads, samples)
    wave_samples = samples // waves
    wave_rows = wave_samples * token_rows

    me = lax.axis_index("seq")
    right = lax.rem(me + 1, n)
    left = lax.rem(me + n - 1, n)
    has_left = me > 0
    has_right = me < n - 1

    barrier = pltpu.get_barrier_semaphore()

    def signal(semaphore, reach):
        for there, target in ((me >= reach, me - reach), (me + reach < n, me + reach)):

            @pl.when(there)
            def _():
                pl.semaphore_signal(
                    semaphore, inc=1, device_id={"seq": target}, device_id_type=MESH
                )

    def await_signals(semaphore, reach):
        count = (me >= reach).astype(jnp.int32) + (me + reach < n).astype(jnp.int32)
        pl.semaphore_wait(semaphore, count)

    rounds = reach_rounds(n)
    side = 4 if n % 4 == 0 else 1

    planes = n // side

    def far_first():
        for k in range(n):
            offset = (planes // 2 + k // side) % planes
            if offset or k % side:
                plane = lax.rem(me // side + offset, planes)
                yield plane * side + lax.rem(me + k, side)

    def met(number):
        if number < rounds:
            await_signals(ready.at[number], 2**number)
        if number + 1 < rounds:
            signal(ready.at[number + 1], 2 ** (number + 1))

    own_head = (me * per) // samples
    loads = {}
    for slot, (name, src, dst) in enumerate(
        (
            ("level", level_hbm, level_ref),
            ("x_true", x_true_hbm, x_true_ref),
            ("noise", noise_hbm, noise_ref),
            ("atoms", single_hbm, single_ref),
            ("coord", w_coord_hbm, w_coord_ref),
            ("qkv", w_qkv_hbm, w_qkv_ref),
            ("pair", pair_hbm, pair_own),
            ("atom_token", atom_token_hbm, atom_token_ref),
            ("edges", edges_hbm, edges_ref),
            ("bias", bias_hbm, bias_ref),
            ("out", w_out_hbm, w_out_ref),
            ("up", w_up_hbm, w_up_ref),
            ("down", w_down_hbm, w_down_ref),
            ("pool", w_pool_hbm, w_pool_ref),
            ("single", token_single_hbm, token_single_ref),
            ("tqkv", w_tqkv_hbm, w_tqkv),
            ("back", w_back_hbm, w_back_ref),
            ("tout", w_tout_hbm, w_tout),
            ("final", w_final_hbm, w_final_ref),
        )
    ):
        loads[name] = pltpu.make_async_copy(src, dst, load_sem.at[slot])
        loads[name].start()
        if name == "qkv":
            signal(barrier, 1)

    upper_root = 160.0 ** (1.0 / 7.0)
    lower_root = 0.0004 ** (1.0 / 7.0)

    def sigma_of(s):
        level = jnp.full((1, atom_rows), level_ref[s], jnp.int32).astype(F32)
        base = upper_root + level / (LEVELS - 1) * (lower_root - upper_root)
        square = base * base
        sigma = SIGMA_DATA * (square * square * square * base)
        return sigma, sigma * sigma + SIGMA_DATA * SIGMA_DATA

    def noisy_of(s, sigma):
        noise = jnp.concatenate([noise_ref[c, pl.ds(s, 1), :] for c in range(3)], axis=0)
        return x_true_ref[...] + sigma * noise

    for name in ("level", "x_true", "noise"):
        loads[name].wait()
    scaled = []
    for s in range(samples):
        sigma, total = sigma_of(s)
        scaled.append(noisy_of(s, sigma) * lax.rsqrt(total))
    spare = atom_rows - 3 * samples
    columns = jnp.transpose(
        jnp.concatenate(scaled + [jnp.zeros((spare, atom_rows), F32)], axis=0)
    )
    loads["atoms"].wait()
    loads["coord"].wait()
    single = single_ref[...].astype(F32)
    def embed(s):
        value = single
        for c in range(3):
            at = 3 * s + c
            value = value + columns[:, at : at + 1] * w_coord_ref[c : c + 1, :]
        stream[s // gs, s % gs] = value

    def exchange(to_right, to_left, begin):
        if begin:

            @pl.when(has_right)
            def _():
                to_right.start()

            @pl.when(has_left)
            def _():
                to_left.start()

        else:

            @pl.when(has_left)
            def _():
                to_right.wait_recv()

            @pl.when(has_right)
            def _():
                to_left.wait_recv()

    def sent(to_right, to_left):
        @pl.when(has_right)
        def _():
            to_right.wait_send()

        @pl.when(has_left)
        def _():
            to_left.wait_send()

    def halo(layer, g):
        return (
            remote(
                kv.at[layer, g, :, pl.ds(atom_rows, RIM), :],
                kv.at[layer, g, :, pl.ds(0, RIM), :],
                halo_send.at[0],
                halo_recv.at[layer, g, 0],
                right,
            ),
            remote(
                kv.at[layer, g, :, pl.ds(RIM, RIM), :],
                kv.at[layer, g, :, pl.ds(RIM + atom_rows, RIM), :],
                halo_send.at[1],
                halo_recv.at[layer, g, 1],
                left,
            ),
        )

    def project(layer, g):
        normal_in = normed(stream[g].reshape(gs * atom_rows, width)).astype(BF16)
        key_value = dot(normal_in, w_qkv_ref[layer, :, width:]).astype(BF16)
        for i in range(gs):
            kv[layer, g, i, RIM : RIM + atom_rows, :] = key_value[
                i * atom_rows : (i + 1) * atom_rows
            ]
        queries[g] = dot(normal_in, w_qkv_ref[layer, :, :width]).astype(BF16)

    def send_halo(layer, g):
        exchange(*halo(layer, g), True)

    stacked = atom_heads * QUERY_BLOCK
    row_head = lax.broadcasted_iota(jnp.int32, (stacked, width), 0) // QUERY_BLOCK
    lane_head = lax.broadcasted_iota(jnp.int32, (stacked, width), 1) // atom_head
    own_lanes = row_head == lane_head
    few_lanes = lane_head[:QUERY_BLOCK]
    scale = atom_head ** (-0.5)
    ones = jnp.ones((KEY_WINDOW, width), BF16)

    def attend(layer, g):
        if layer != ENC_LAYERS:
            exchange(*halo(layer, g), False)
        mixed = []
        pairs = [(i, b) for i in range(gs) for b in range(blocks)]
        for start in range(0, len(pairs), 8):
            part = pairs[start : start + 8]
            scores = []
            for i, b in part:
                q = queries[g, pl.ds(i * atom_rows + b * QUERY_BLOCK, QUERY_BLOCK), :]
                q = jnp.concatenate([q] * atom_heads, axis=0)
                q = jnp.where(own_lanes, q, jnp.zeros_like(q))
                key_win = kv[layer, g, i, QUERY_BLOCK * b : QUERY_BLOCK * b + KEY_WINDOW, :width]
                score = lax.dot_general(q, key_win, LAST, preferred_element_type=F32)
                scores.append(score * scale + masked_bias[b])
            tops = [jnp.max(score, -1, keepdims=True) for score in scores]
            expos = [jnp.exp(score - top).astype(BF16) for score, top in zip(scores, tops)]
            sums = []
            for (i, b), expo in zip(part, expos):
                value_win = kv[layer, g, i, QUERY_BLOCK * b : QUERY_BLOCK * b + KEY_WINDOW, width:]
                sums.append(dot(expo, jnp.concatenate([value_win, ones], axis=1)))
            for both in sums:
                picked = both[:QUERY_BLOCK]
                number, below = picked[:, :width], picked[:, width:]
                for h in range(1, atom_heads):
                    rows = both[h * QUERY_BLOCK : (h + 1) * QUERY_BLOCK]
                    number = jnp.where(few_lanes == h, rows[:, :width], number)
                    below = jnp.where(few_lanes == h, rows[:, width:], below)
                mixed.append((number / below).astype(BF16))
        mixed = jnp.concatenate(mixed, axis=0)
        value = stream[g].reshape(gs * atom_rows, width) + dot(mixed, w_out_ref[layer])
        normal_mid = normed(value).astype(BF16)
        gated = dot(normal_mid, w_up_ref[layer])
        gate = gated[:, : 2 * width]
        hidden = (gate / (1.0 + jnp.exp(-gate)) * gated[:, 2 * width :]).astype(BF16)
        value = value + dot(hidden, w_down_ref[layer])
        stream[g] = value.reshape(gs, atom_rows, width)
        return value

    def pool_copy(g):
        return (
            remote(
                psend.at[g, 1], precv.at[g, 0], pool_send.at[0], pool_recv.at[g, 0], right
            ),
            remote(psend.at[g, 0], precv.at[g, 1], pool_send.at[1], pool_recv.at[g, 1], left),
        )

    def count_copy():
        return (
            remote(counts.at[2], counts.at[3], count_send.at[0], count_recv.at[0], right),
            remote(counts.at[0], counts.at[4], count_send.at[1], count_recv.at[1], left),
        )

    def edge_copy(g):
        return (
            remote(
                rim.at[0, g],
                edge.at[0, g],
                edge_send.at[0],
                edge_recv.at[g, 0],
                right,
            ),
            remote(
                rim.at[1, g],
                edge.at[1, g],
                edge_send.at[1],
                edge_recv.at[g, 1],
                left,
            ),
        )

    def token_copy():
        return (
            remote(atom_token_ref, near_token.at[0], token_send.at[0], token_recv.at[0], right),
            remote(atom_token_ref, near_token.at[1], token_send.at[1], token_recv.at[1], left),
        )

    def selects(row):
        spot = row - (me - 1) * token_rows
        return (
            lax.broadcasted_iota(jnp.int32, (3 * token_rows, atom_rows), 0) == spot
        ).astype(F32)

    def back_copy(t):
        return (
            remote(back.at[t, 1], back.at[t, 0], back_send.at[0], back_recv.at[t, 0], right),
            remote(back.at[t, 1], back.at[t, 2], back_send.at[1], back_recv.at[t, 1], left),
        )

    def take_back(g):
        t, base = (g, 0) if waves == GROUPS else (0, g * gs * token_rows)
        if waves == GROUPS:
            exchange(*back_copy(t), False)
        else:

            @pl.when(g == 0)
            def _():
                exchange(*back_copy(0), False)

        exchange(*edge_copy(g), False)
        beyond = []
        for i in range(gs):
            span = pl.ds(pl.multiple_of(base + i * token_rows, token_rows), token_rows)
            near = jnp.concatenate([back[t, j, span, :] for j in range(3)], axis=0)
            stream[g, i] += lax.dot_general(sel, near, FIRST, preferred_element_type=F32)
            for side, rows in ((0, slice(atom_rows - RIM, atom_rows)), (1, slice(0, RIM))):
                picked = lax.dot_general(
                    near_sel[side], near, FIRST, preferred_element_type=F32
                )
                beyond.append(edge[side, g, i].astype(F32) + picked[rows])
        project(ENC_LAYERS, g)
        normal = normed(jnp.concatenate(beyond, axis=0)).astype(BF16)
        key_value = dot(normal, w_qkv_ref[ENC_LAYERS, :, width:]).astype(BF16)
        for i in range(gs):
            at = 2 * i * RIM
            kv[ENC_LAYERS, g, i, 0:RIM, :] = key_value[at : at + RIM]
            kv[ENC_LAYERS, g, i, RIM + atom_rows :, :] = key_value[at + RIM : at + 2 * RIM]

    def run_pair(first, finish):
        def step(g, c):
            if first == ENC_LAYERS:
                take_back(g)
            attend(first, g)
            project(first + 1, g)
            send_halo(first + 1, g)
            if first == 0:
                for group in range(GROUPS):

                    @pl.when(g == group)
                    def _():
                        met(2 + group)

            return c

        lax.fori_loop(0, GROUPS, step, 0)
        if first == 0:
            for number in range(2 + GROUPS, rounds):
                met(number)
            lax.fori_loop(1, n, pair_start, 0)

        def last(g, c):
            finish(g, attend(first + 1, g))
            return c

        lax.fori_loop(0, GROUPS, last, 0)

    for s in range(gs):
        embed(s)
    loads["qkv"].wait()
    project(0, 0)
    await_signals(barrier, 1)
    signal(ready.at[0], 1)
    send_halo(0, 0)
    for s in range(gs, samples):
        embed(s)
    project(0, 1)
    send_halo(0, 1)
    met(0)
    loads["atom_token"].wait()
    selector = selects(atom_token_ref[...])
    sel = selector.astype(BF16)
    counted = jnp.broadcast_to(jnp.sum(selector, 1, keepdims=True), (3 * token_rows, 128))
    for j in range(3):
        counts[j] = counted[j * token_rows : (j + 1) * token_rows].astype(BF16)

    exchange(*count_copy(), True)
    exchange(*token_copy(), True)

    def pair_copy(target, slot):
        return remote(
            pair_out.at[(target * per) // samples],
            pair_buf.at[slot],
            pair_send,
            pair_recv,
            target,
        )

    def pair_start(k, c):
        pair_copy(lax.rem(me + k, n), me).start()
        return c

    loads["pair"].wait()
    rows = pair_own[...]
    pair_out[...] = (rows - jnp.max(rows, -1, keepdims=True)).astype(BF16)
    pair_buf[me] = pair_out[own_head]

    def pool(g, value):
        pooled = jnp.maximum(dot(normed(value).astype(BF16), w_pool_ref[...]), 0.0)
        high = pooled.astype(BF16)
        low = (pooled - high.astype(F32)).astype(BF16)
        for i in range(gs):
            at = slice(i * atom_rows, (i + 1) * atom_rows)
            part = dot(sel, high[at]) + dot(sel, low[at])
            psend[g, 0, i] = part[:token_rows].astype(BF16)
            own_sum[g, i] = part[token_rows : 2 * token_rows]
            psend[g, 1, i] = part[2 * token_rows :].astype(BF16)
        exchange(*pool_copy(g), True)
        for i in range(gs):
            rim[0, g, i] = stream[g, i, atom_rows - RIM :, :].astype(BF16)
            rim[1, g, i] = stream[g, i, :RIM, :].astype(BF16)
        exchange(*edge_copy(g), True)

    loads["bias"].wait()
    loads["edges"].wait()
    place = lax.broadcasted_iota(jnp.int32, (1, KEY_WINDOW), 1)
    for b in range(blocks):
        position = me * atom_rows - RIM + QUERY_BLOCK * b + place
        allowed = (position >= edges_ref[0, b]) & (position < edges_ref[1, b])
        masked_bias[b] = jnp.where(
            allowed, bias_ref[b].reshape(atom_heads * QUERY_BLOCK, KEY_WINDOW), -1e30
        )

    @pl.when(jnp.logical_not(has_left))
    def _():
        for layer in range(LAYERS):
            for g in range(GROUPS):
                kv[layer, g, :, 0:RIM, :] = jnp.zeros((gs, RIM, 2 * width), BF16)
        for g in range(GROUPS):
            precv[g, 0] = jnp.zeros(precv.shape[2:], BF16)
        for t in range(waves):
            back[t, 0] = jnp.zeros(back.shape[2:], BF16)
        counts[3] = jnp.zeros(counts.shape[1:], BF16)
        edge[0] = jnp.zeros(edge.shape[1:], BF16)
        near_token[0] = jnp.full((1, atom_rows), -tokens, jnp.int32)

    @pl.when(jnp.logical_not(has_right))
    def _():
        for layer in range(LAYERS):
            for g in range(GROUPS):
                kv[layer, g, :, RIM + atom_rows :, :] = jnp.zeros((gs, RIM, 2 * width), BF16)
        for g in range(GROUPS):
            precv[g, 1] = jnp.zeros(precv.shape[2:], BF16)
        for t in range(waves):
            back[t, 2] = jnp.zeros(back.shape[2:], BF16)
        counts[4] = jnp.zeros(counts.shape[1:], BF16)
        edge[1] = jnp.zeros(edge.shape[1:], BF16)
        near_token[1] = jnp.full((1, atom_rows), -tokens, jnp.int32)

    for name in ("out", "up", "down", "pool"):
        loads[name].wait()
    met(1)
    run_pair(0, pool)
    loads["single"].wait()
    loads["back"].wait()

    exchange(*count_copy(), False)
    number_of = (
        counts[1].astype(F32)[:, :1] + counts[3].astype(F32)[:, :1] + counts[4].astype(F32)[:, :1]
    )
    lanes = 128
    half = lanes // 2
    main = lanes - 2 * head_size
    rest = head_size - main
    lane = lax.broadcasted_iota(jnp.int32, (token_rows, lanes), 1)

    def moved(block, start, to, size=head_size):
        tile, off = start // lanes, start % lanes
        shift = (to - off) % lanes

        def turned(t):
            part = block[:, t * lanes : (t + 1) * lanes]
            return part if shift == 0 else pltpu.roll(part, shift, 1)

        if off + size <= lanes:
            return turned(tile)
        return jnp.where(lane < to + lanes - off, turned(tile), turned(tile + 1))

    def spread(copy_of):
        for target in far_first():
            copy_of(target, me).start()

    others = pl.ds(0, n - 1)

    def every_pair():
        return remote(
            pair_buf.at[others], pair_buf.at[others], pair_send, pair_recv, right
        )

    rows_of = item_rows(token_rows, pack, waves)
    starts = (0, rows_of[0])

    def item_copy(t):
        span = pl.ds(starts[t], rows_of[t])
        return lambda target, slot: remote(
            items.at[target, :, span], got.at[slot, :, span], item_send, item_recv.at[t], target
        )

    def every_item(t):
        span = pl.ds(starts[t], rows_of[t])
        return remote(
            items.at[others, :, span], got.at[others, :, span], item_send, item_recv.at[t], right
        )

    def out_copy(t):
        return lambda target, slot: remote(
            outs.at[t, target], returned.at[t, slot], out_send, out_recv.at[t], target
        )

    def every_out(t):
        return remote(
            outs.at[t, others], returned.at[t, others], out_send, out_recv.at[t], right
        )

    def token_project(t):
        for g in range(GROUPS) if waves == 1 else (t,):
            exchange(*pool_copy(g), False)
        for a in range(wave_samples):
            s = t * wave_samples + a
            g, i = s // gs, s % gs
            sums = own_sum[g, i] + precv[g, 0, i].astype(F32) + precv[g, 1, i].astype(F32)
            token_in[s * token_rows : (s + 1) * token_rows, :] = (
                sums / number_of + token_single_ref[...]
            )
        normal_tok = normed(token_in[t * wave_rows : (t + 1) * wave_rows, :]).astype(BF16)
        parts = [
            dot(normal_tok, w_tqkv[:, j * channels : (j + 1) * channels]) for j in range(3)
        ]
        for h in range(heads) if waves == 1 else ():
            start = h * head_size
            for a in range(0, wave_samples, pack):
                keys = []
                for p in range(pack):
                    item = h * samples + a + p
                    owner, unit = item // per, item % per // pack
                    at = slice((a + p) * token_rows, (a + p + 1) * token_rows)
                    v = moved(parts[2][at], start, half * p)
                    q = moved(parts[0][at], start, half * (1 - p))
                    keys.append(moved(parts[1][at], start, half * (1 - p)))
                    low, high = (v, q) if p == 0 else (q, v)
                    tile = jnp.where(lane < head_size, low, jnp.where(lane < half, 1.0, high))
                    items[owner, unit, p * token_rows : (p + 1) * token_rows, :] = tile.astype(
                        BF16
                    )
                key = keys[0] if pack == 1 else jnp.where(lane < half, keys[1], keys[0])
                items[owner, unit, pack * token_rows :, :] = key.astype(BF16)
        if waves == 2:
            one, two = slice(0, token_rows), slice(token_rows, 2 * token_rows)
            for h in range(heads):
                start = h * head_size
                mixed = []
                for upper, lower, at in ((0, 1, one), (1, 0, two)):
                    low = moved(parts[upper][one], start, 0)
                    mid = moved(parts[lower][two], start, head_size)
                    high = moved(parts[2][at], start, 2 * head_size, main)
                    tile = jnp.where(lane < head_size, low, jnp.where(lane < 2 * head_size, mid, high))
                    mixed.append(tile)
                at = starts[t]
                items[h, 0, at : at + 2 * token_rows, :] = jnp.concatenate(mixed, axis=0).astype(BF16)
                tail = jnp.where(
                    lane < rest,
                    moved(parts[2][one], start + main, 0, rest),
                    moved(parts[2][two], start + main, half - rest, rest),
                )
                near, far = tail[: token_rows // 2], tail[token_rows // 2 :]
                tail = jnp.where(lane[: token_rows // 2] < half, near, pltpu.roll(far, half, 1))
                items[h, 0, at + 2 * token_rows : at + rows_of[t], :] = tail.astype(BF16)
        spread(item_copy(t))
        span = pl.ds(starts[t], rows_of[t])
        got[me, :, span] = items[me, :, span]

    token_scale = head_size ** (-0.5)
    tile = 16
    key_lane = lax.broadcasted_iota(jnp.int32, (tokens, lanes), 1)
    out_lane = lax.broadcasted_iota(jnp.int32, (tile * token_rows, lanes), 1)

    def token_attend(t):
        every_item(t).wait_recv()
        for unit in range(units):
            packed = got[:, unit, pack * token_rows :, :].reshape(tokens, lanes)

            def one(block, c):
                span = pl.ds(block * tile, tile)
                ratios = []
                for p in range(pack):
                    at = slice(p * token_rows, (p + 1) * token_rows)
                    mine = key_lane < head_size
                    if p == 0:
                        mine = (key_lane >= half) & (key_lane < half + head_size)
                    keys = jnp.where(mine, packed, jnp.zeros_like(packed))
                    values = got[:, unit, at, :].reshape(tokens, lanes)
                    q = got[span, unit, at, :].reshape(tile * token_rows, lanes)
                    scores = lax.dot_general(q, keys, LAST, preferred_element_type=F32)
                    scores = scores * token_scale + pair_buf[span].astype(F32).reshape(
                        tile * token_rows, tokens
                    )
                    expo = jnp.exp(scores - jnp.max(scores, -1, keepdims=True)).astype(BF16)
                    both = dot(expo, values)
                    ratios.append(both / both[:, head_size : head_size + 1])
                ratio = ratios[0] if pack == 1 else jnp.where(out_lane < half, *ratios)
                outs[t, span, unit, :, :] = ratio.astype(BF16).reshape(tile, token_rows, lanes)
                return c

            if n == tile:
                one(0, 0)
            else:
                lax.fori_loop(0, n // tile, one, 0)
        spread(out_copy(t))
        returned[t, me] = outs[t, me]

    all_lane = lax.broadcasted_iota(jnp.int32, (tokens, lanes), 1)

    def token_pair(t):
        every_item(t).wait_recv()
        at = starts[t]
        one = got[:, 0, at : at + token_rows, :].reshape(tokens, lanes)
        two = got[:, 0, at + token_rows : at + 2 * token_rows, :].reshape(tokens, lanes)
        tail = got[:, 0, at + 2 * token_rows : at + rows_of[t], :].astype(F32)
        flat = tail.reshape(n * token_rows // 2, lanes)
        tail = jnp.concatenate(
            [tail, pltpu.roll(flat, half, 1).reshape(tail.shape)], axis=1
        ).reshape(tokens, lanes)
        tail = jnp.where(all_lane < half, tail, 1.0).astype(BF16)
        bias = pair_buf[...].astype(F32).reshape(tokens, tokens)
        ratios = []
        for a, (q, k) in enumerate(((one, two), (two, one))):
            mine = (all_lane >= a * head_size) & (all_lane < (a + 1) * head_size)
            keys = jnp.where(mine, k, jnp.zeros_like(k))
            scores = lax.dot_general(q, keys, LAST, preferred_element_type=F32)
            scores = scores * token_scale + bias
            expo = jnp.exp(scores - jnp.max(scores, -1, keepdims=True)).astype(BF16)
            both = dot(expo, jnp.concatenate([q, tail], axis=1))
            ratios.append(both / both[:, lanes + half : lanes + half + 1])
        first, second = ratios
        out = jnp.where(
            all_lane >= lanes - main,
            first[:, :lanes],
            jnp.where(
                all_lane < rest,
                first[:, lanes:],
                jnp.where(
                    all_lane < half - rest,
                    pltpu.roll(second[:, :lanes], half - rest, 1),
                    second[:, lanes:],
                ),
            ),
        )
        outs[t, :, 0, :, :] = out.astype(BF16).reshape(n, token_rows, lanes)
        spread(out_copy(t))
        returned[t, me] = outs[t, me]

    def token_finish(t):
        every_out(t).wait_recv()
        state = token_in[t * wave_rows : (t + 1) * wave_rows, :]
        if waves == 2:
            samples_mixed = []
            for a in range(wave_samples):
                begin = half - main - rest if a else lanes - main
                tiles = [None] * (channels // lanes)
                for h in range(heads):
                    low = h * head_size
                    block = returned[t, h, 0].astype(F32)
                    turned = pltpu.roll(block, (low - begin) % lanes, 1)
                    for j in range(low // lanes, (low + head_size - 1) // lanes + 1):
                        above = lane + j * lanes >= low
                        tiles[j] = turned if tiles[j] is None else jnp.where(above, turned, tiles[j])
                samples_mixed.append(jnp.concatenate(tiles, axis=1))
            mixed = jnp.concatenate(samples_mixed, axis=0).astype(BF16)
            state = state + dot(mixed, w_tout[...])
        for h in range(heads) if waves == 1 else ():
            mix = []
            for a in range(wave_samples):
                item = h * samples + t * wave_samples + a
                owner, unit, p = item // per, item % per // pack - t * units, item % per % pack
                block = returned[t, owner, unit]
                if p == 1:
                    block = pltpu.roll(block.astype(F32), half, 1).astype(BF16)
                mix.append(block[:, :head_size])
            state = state + dot(
                jnp.concatenate(mix, axis=0), w_tout[h * head_size : (h + 1) * head_size, :]
            )
        for a in range(wave_samples):
            state_ref[t * wave_samples + a] = state[a * token_rows : (a + 1) * token_rows]
        back[t, 1] = dot(normed(state).astype(BF16), w_back_ref[...]).astype(BF16)
        exchange(*back_copy(t), True)

    loads["tqkv"].wait()
    for t in range(waves):
        token_project(t)
    every_pair().wait_recv()
    if waves == 1:
        token_attend(0)
    else:
        for t in range(waves):
            token_pair(t)
    loads["tout"].wait()
    for t in range(waves):
        token_finish(t)
    first = ENC_LAYERS

    def finish(g, value):
        normal = normed(value).astype(BF16)
        for i in range(gs):
            s = g * gs + i
            update = lax.dot_general(
                w_final_ref[...],
                normal[i * atom_rows : (i + 1) * atom_rows],
                LAST,
                preferred_element_type=F32,
            )
            sigma, total = sigma_of(s)
            result = (
                SIGMA_DATA * SIGMA_DATA / total * noisy_of(s, sigma)
                + sigma * SIGMA_DATA * lax.rsqrt(total) * update
            ) / SIGMA_DATA
            for c in range(3):
                denoised_ref[c, pl.ds(s, 1), :] = result[c : c + 1]

    loads["final"].wait()
    exchange(*token_copy(), False)
    sent(
        remote(
            rim.at[0], edge.at[0], edge_send.at[0], edge_recv.at[0, 0], right
        ),
        remote(
            rim.at[1], edge.at[1], edge_send.at[1], edge_recv.at[0, 1], left
        ),
    )
    near_sel = [selects(near_token[side]).astype(BF16) for side in range(2)]
    run_pair(first, finish)

    sent(
        remote(
            kv.at[pl.ds(0, LAYERS - 1), :, :, pl.ds(0, RIM), :],
            kv.at[pl.ds(0, LAYERS - 1), :, :, pl.ds(0, RIM), :],
            halo_send.at[0],
            halo_recv.at[0, 0, 0],
            right,
        ),
        remote(
            kv.at[pl.ds(0, LAYERS - 1), :, :, pl.ds(0, RIM), :],
            kv.at[pl.ds(0, LAYERS - 1), :, :, pl.ds(0, RIM), :],
            halo_send.at[1],
            halo_recv.at[0, 0, 1],
            left,
        ),
    )
    sent(*count_copy())
    sent(*token_copy())
    sent(
        remote(psend.at[:, 1], precv.at[:, 0], pool_send.at[0], pool_recv.at[0, 0], right),
        remote(psend.at[:, 0], precv.at[:, 1], pool_send.at[1], pool_recv.at[0, 1], left),
    )
    sent(
        remote(back.at[:, 1], back.at[:, 0], back_send.at[0], back_recv.at[0, 0], right),
        remote(back.at[:, 1], back.at[:, 2], back_send.at[1], back_recv.at[0, 1], left),
    )
    every_pair().wait_send()
    for t in range(waves):
        every_item(t).wait_send()
        every_out(t).wait_send()


def store(denoised_ref, state_ref, denoised_out, state_out, sem):
    copies = (
        pltpu.make_async_copy(state_ref, state_out, sem.at[0]),
        pltpu.make_async_copy(denoised_ref, denoised_out, sem.at[1]),
    )
    for copy in copies:
        copy.start()
    for copy in copies:
        copy.wait()


def shards(
    n,
    x_true,
    noise,
    noise_level,
    atom_single,
    atom_token,
    window_edges,
    atom_pair_bias,
    token_single,
    pair_bias,
    w_coord,
    w_atom_qkv,
    w_atom_out,
    w_atom_up,
    w_atom_down,
    w_pool,
    w_token_qkv,
    w_token_out,
    w_back,
    w_final,
):
    samples = noise.shape[0]
    atom_rows, width = atom_single.shape
    token_rows, channels = token_single.shape
    blocks, atom_heads = atom_pair_bias.shape[:2]
    heads = pair_bias.shape[0]
    gs = samples // GROUPS
    per, pack, waves, units = plan(n, heads, samples)
    vmem = pl.BlockSpec(memory_space=pltpu.VMEM)
    anywhere = pl.BlockSpec(memory_space=pl.ANY)
    dma = pltpu.SemaphoreType.DMA
    held = pl.pallas_call(
        functools.partial(kernel, n),
        name="denoise",
        out_shape=(
            pltpu.VMEM((3, samples, atom_rows), F32),
            pltpu.VMEM((samples, token_rows, channels), F32),
        ),
        in_specs=[anywhere] * 19,
        out_specs=(vmem, vmem),
        scratch_shapes=[
            pltpu.SMEM((samples,), jnp.int32),
            pltpu.SMEM((2, blocks), jnp.int32),
            pltpu.VMEM(x_true.shape, F32),
            pltpu.VMEM((3, samples, atom_rows), F32),
            pltpu.VMEM(atom_single.shape, BF16),
            pltpu.VMEM((1, atom_rows), jnp.int32),
            pltpu.VMEM(w_coord.shape, F32),
            pltpu.VMEM(w_final.shape, BF16),
            pltpu.VMEM((GROUPS, gs, atom_rows, width), F32),
            pltpu.VMEM((2, GROUPS, gs, RIM, width), BF16),
            pltpu.VMEM((2, GROUPS, gs, RIM, width), BF16),
            pltpu.VMEM((2, 1, atom_rows), jnp.int32),
            pltpu.VMEM((LAYERS, GROUPS, gs, atom_rows + 2 * RIM, 2 * width), BF16),
            pltpu.VMEM((GROUPS, gs * atom_rows, width), BF16),
            pltpu.VMEM((blocks, atom_heads * QUERY_BLOCK, KEY_WINDOW), F32),
            pltpu.VMEM((5, token_rows, 128), BF16),
            pltpu.VMEM((GROUPS, gs, token_rows, channels), F32),
            pltpu.VMEM((GROUPS, 2, gs, token_rows, channels), BF16),
            pltpu.VMEM((GROUPS, 2, gs, token_rows, channels), BF16),
            pltpu.VMEM((samples * token_rows, channels), F32),
            pltpu.VMEM((n, units, sum(item_rows(token_rows, pack, waves)), 128), BF16),
            pltpu.VMEM((n, units, sum(item_rows(token_rows, pack, waves)), 128), BF16),
            pltpu.VMEM(pair_bias.shape, F32),
            pltpu.VMEM(pair_bias.shape, BF16),
            pltpu.VMEM((n, token_rows, n * token_rows), BF16),
            pltpu.VMEM((waves, n, units, token_rows, 128), BF16),
            pltpu.VMEM((waves, n, units, token_rows, 128), BF16),
            pltpu.VMEM((waves, 3, samples // waves * token_rows, width), BF16),
            pltpu.VMEM(w_token_qkv.shape, BF16),
            pltpu.VMEM(w_token_out.shape, BF16),
            pltpu.VMEM(atom_pair_bias.shape, F32),
            pltpu.VMEM(token_single.shape, F32),
            pltpu.VMEM(w_atom_qkv.shape, BF16),
            pltpu.VMEM(w_atom_out.shape, BF16),
            pltpu.VMEM(w_atom_up.shape, BF16),
            pltpu.VMEM(w_atom_down.shape, BF16),
            pltpu.VMEM(w_pool.shape, BF16),
            pltpu.VMEM(w_back.shape, BF16),
            dma((19,)),
            pltpu.SemaphoreType.REGULAR((reach_rounds(n),)),
            dma((2,)),
            dma((LAYERS, GROUPS, 2)),
            dma((2,)),
            dma((2,)),
            dma((2,)),
            dma((GROUPS, 2)),
            dma(()),
            dma(()),
            dma(()),
            dma((waves,)),
            dma(()),
            dma((waves,)),
            dma((2,)),
            dma((waves, 2)),
            dma((2,)),
            dma((GROUPS, 2)),
            dma((2,)),
            dma((2,)),
        ],
        compiler_params=pltpu.CompilerParams(
            collective_id=0,
            has_side_effects=True,
            vmem_limit_bytes=56 * 1024 * 1024,
        ),
    )(
        noise_level,
        window_edges.T,
        x_true,
        noise.transpose(1, 0, 2),
        atom_single,
        atom_token.reshape(1, atom_rows),
        atom_pair_bias,
        token_single,
        pair_bias,
        w_coord,
        w_atom_qkv,
        w_atom_out,
        w_atom_up,
        w_atom_down,
        w_pool,
        w_token_qkv,
        w_token_out,
        w_back,
        w_final,
    )
    denoised, state = pl.pallas_call(
        store,
        name="store",
        out_shape=(
            jax.ShapeDtypeStruct((3, samples, atom_rows), F32),
            jax.ShapeDtypeStruct((samples, token_rows, channels), F32),
        ),
        in_specs=[vmem] * 2,
        out_specs=(anywhere, anywhere),
        scratch_shapes=[dma((2,))],
    )(*[pltpu.with_memory_space_constraint(x, pltpu.VMEM) for x in held])
    return denoised.transpose(1, 0, 2), state


def solution(mesh):
    in_specs = (
        P(None, ("groups", "seq")),
        P("groups", None, "seq"),
        P("groups"),
        P(("groups", "seq"), None),
        P(("groups", "seq")),
        P(("groups", "seq"), None),
        P(("groups", "seq"), None, None, None),
        P(("groups", "seq"), None),
        P("groups", "seq", None),
    ) + (P(),) * 10
    out_specs = (P("groups", None, "seq"), P("groups", "seq", None))
    return jax.shard_map(
        functools.partial(shards, mesh.shape["seq"]),
        mesh=mesh,
        in_specs=in_specs,
        out_specs=out_specs,
        check_vma=False,
    )
```

```python
import functools

import jax
import jax.numpy as jnp
from jax import lax
from jax.experimental import pallas as pl
from jax.experimental.pallas import tpu as pltpu
from jax.sharding import PartitionSpec as P

QUERY_BLOCK = 32
KEY_WINDOW = 128
ENC_LAYERS = 2
LEVELS = 200
RIM = 48
LAYERS = 4
GROUPS = 2

EPS = 1e-05
SIGMA_DATA = 16.0
MESH = pl.DeviceIdType.MESH
F32 = jnp.float32
BF16 = jnp.bfloat16
LAST = (((1,), (1,)), ((), ()))
FIRST = (((0,), (0,)), ((), ()))


def normed(values):
    centred = values - jnp.mean(values, -1, keepdims=True)
    spread = jnp.mean(centred * centred, -1, keepdims=True)
    return centred * lax.rsqrt(spread + EPS)


def dot(a, b):
    return jnp.dot(a, b, preferred_element_type=F32)


def remote(src, dst, send, recv, target):
    return pltpu.make_async_remote_copy(
        src_ref=src,
        dst_ref=dst,
        send_sem=send,
        recv_sem=recv,
        device_id={"seq": target},
        device_id_type=MESH,
    )


def plan(n, heads, samples):
    per = heads * samples // n
    gs = samples // GROUPS
    pack = 2 if per % 2 == 0 else 1
    waves = GROUPS if per == samples and gs == pack else 1
    return per, pack, waves, per // pack // waves


def reach_rounds(n):
    rounds, known = 0, 1
    while known < n - 1:
        rounds, known = rounds + 1, 2 * known
    return rounds


def item_rows(token_rows, pack, waves):
    if waves == 1:
        return ((pack + 1) * token_rows,)
    return (2 * token_rows + token_rows // 2,) * 2


def kernel(
    n,
    level_hbm,
    edges_hbm,
    x_true_hbm,
    noise_hbm,
    single_hbm,
    atom_token_hbm,
    bias_hbm,
    token_single_hbm,
    pair_hbm,
    w_coord_hbm,
    w_qkv_hbm,
    w_out_hbm,
    w_up_hbm,
    w_down_hbm,
    w_pool_hbm,
    w_tqkv_hbm,
    w_tout_hbm,
    w_back_hbm,
    w_final_hbm,
    denoised_ref,
    state_ref,
    level_ref,
    edges_ref,
    x_true_ref,
    noise_ref,
    single_ref,
    atom_token_ref,
    w_coord_ref,
    w_final_ref,
    stream,
    edge,
    rim,
    near_token,
    kv,
    queries,
    masked_bias,
    counts,
    own_sum,
    psend,
    precv,
    token_in,
    items,
    got,
    pair_own,
    pair_out,
    pair_buf,
    outs,
    returned,
    back,
    w_tqkv,
    w_tout,
    bias_ref,
    token_single_ref,
    w_qkv_ref,
    w_out_ref,
    w_up_ref,
    w_down_ref,
    w_pool_ref,
    w_back_ref,
    load_sem,
    ready,
    halo_send,
    halo_recv,
    count_send,
    count_recv,
    pool_send,
    pool_recv,
    pair_send,
    pair_recv,
    item_send,
    item_recv,
    out_send,
    out_recv,
    back_send,
    back_recv,
    edge_send,
    edge_recv,
    token_send,
    token_recv,
):
    samples = noise_ref.shape[1]
    atom_rows, width = single_ref.shape
    token_rows, channels = token_single_ref.shape
    blocks, atom_heads = bias_ref.shape[:2]
    atom_head = width // atom_heads
    heads = pair_hbm.shape[0]
    head_size = channels // heads
    tokens = n * token_rows
    gs = samples // GROUPS
    per, pack, waves, units = plan(n, heads, samples)
    wave_samples = samples // waves
    wave_rows = wave_samples * token_rows

    me = lax.axis_index("seq")
    right = lax.rem(me + 1, n)
    left = lax.rem(me + n - 1, n)
    has_left = me > 0
    has_right = me < n - 1

    barrier = pltpu.get_barrier_semaphore()

    def signal(semaphore, reach):
        for there, target in ((me >= reach, me - reach), (me + reach < n, me + reach)):

            @pl.when(there)
            def _():
                pl.semaphore_signal(
                    semaphore, inc=1, device_id={"seq": target}, device_id_type=MESH
                )

    def await_signals(semaphore, reach):
        count = (me >= reach).astype(jnp.int32) + (me + reach < n).astype(jnp.int32)
        pl.semaphore_wait(semaphore, count)

    rounds = reach_rounds(n)
    side = 4 if n % 4 == 0 else 1

    planes = n // side

    def far_first():
        for k in range(n):
            offset = (planes // 2 + k // side) % planes
            if offset or k % side:
                plane = lax.rem(me // side + offset, planes)
                yield plane * side + lax.rem(me + k, side)

    def met(number):
        if number < rounds:
            await_signals(ready.at[number], 2**number)
        if number + 1 < rounds:
            signal(ready.at[number + 1], 2 ** (number + 1))

    own_head = (me * per) // samples
    loads = {}
    for slot, (name, src, dst) in enumerate(
        (
            ("level", level_hbm, level_ref),
            ("x_true", x_true_hbm, x_true_ref),
            ("noise", noise_hbm, noise_ref),
            ("atoms", single_hbm, single_ref),
            ("coord", w_coord_hbm, w_coord_ref),
            ("qkv", w_qkv_hbm, w_qkv_ref),
            ("pair", pair_hbm, pair_own),
            ("atom_token", atom_token_hbm, atom_token_ref),
            ("edges", edges_hbm, edges_ref),
            ("bias", bias_hbm, bias_ref),
            ("out", w_out_hbm, w_out_ref),
            ("up", w_up_hbm, w_up_ref),
            ("down", w_down_hbm, w_down_ref),
            ("pool", w_pool_hbm, w_pool_ref),
            ("single", token_single_hbm, token_single_ref),
            ("tqkv", w_tqkv_hbm, w_tqkv),
            ("back", w_back_hbm, w_back_ref),
            ("tout", w_tout_hbm, w_tout),
            ("final", w_final_hbm, w_final_ref),
        )
    ):
        loads[name] = pltpu.make_async_copy(src, dst, load_sem.at[slot])
        loads[name].start()
        if name == "qkv":
            signal(barrier, 1)

    upper_root = 160.0 ** (1.0 / 7.0)
    lower_root = 0.0004 ** (1.0 / 7.0)

    def sigma_of(s):
        level = jnp.full((1, atom_rows), level_ref[s], jnp.int32).astype(F32)
        base = upper_root + level / (LEVELS - 1) * (lower_root - upper_root)
        square = base * base
        sigma = SIGMA_DATA * (square * square * square * base)
        return sigma, sigma * sigma + SIGMA_DATA * SIGMA_DATA

    def noisy_of(s, sigma):
        noise = jnp.concatenate([noise_ref[c, pl.ds(s, 1), :] for c in range(3)], axis=0)
        return x_true_ref[...] + sigma * noise

    for name in ("level", "x_true", "noise"):
        loads[name].wait()
    scaled = []
    for s in range(samples):
        sigma, total = sigma_of(s)
        scaled.append(noisy_of(s, sigma) * lax.rsqrt(total))
    spare = atom_rows - 3 * samples
    columns = jnp.transpose(
        jnp.concatenate(scaled + [jnp.zeros((spare, atom_rows), F32)], axis=0)
    )
    loads["atoms"].wait()
    loads["coord"].wait()
    single = single_ref[...].astype(F32)
    def embed(s):
        value = single
        for c in range(3):
            at = 3 * s + c
            value = value + columns[:, at : at + 1] * w_coord_ref[c : c + 1, :]
        stream[s // gs, s % gs] = value

    def exchange(to_right, to_left, begin):
        if begin:

            @pl.when(has_right)
            def _():
                to_right.start()

            @pl.when(has_left)
            def _():
                to_left.start()

        else:

            @pl.when(has_left)
            def _():
                to_right.wait_recv()

            @pl.when(has_right)
            def _():
                to_left.wait_recv()

    def sent(to_right, to_left):
        @pl.when(has_right)
        def _():
            to_right.wait_send()

        @pl.when(has_left)
        def _():
            to_left.wait_send()

    def halo(layer, g):
        return (
            remote(
                kv.at[layer, g, :, pl.ds(atom_rows, RIM), :],
                kv.at[layer, g, :, pl.ds(0, RIM), :],
                halo_send.at[0],
                halo_recv.at[min(layer, LAYERS - 2), g, 0],
                right,
            ),
            remote(
                kv.at[layer, g, :, pl.ds(RIM, RIM), :],
                kv.at[layer, g, :, pl.ds(RIM + atom_rows, RIM), :],
                halo_send.at[1],
                halo_recv.at[min(layer, LAYERS - 2), g, 1],
                left,
            ),
        )

    def project(layer, g):
        normal_in = normed(stream[g].reshape(gs * atom_rows, width)).astype(BF16)
        key_value = dot(normal_in, w_qkv_ref[layer, :, width:]).astype(BF16)
        for i in range(gs):
            kv[layer, g, i, RIM : RIM + atom_rows, :] = key_value[
                i * atom_rows : (i + 1) * atom_rows
            ]
        queries[g] = dot(normal_in, w_qkv_ref[layer, :, :width]).astype(BF16)

    def send_halo(layer, g):
        exchange(*halo(layer, g), True)

    stacked = atom_heads * QUERY_BLOCK
    row_head = lax.broadcasted_iota(jnp.int32, (stacked, width), 0) // QUERY_BLOCK
    lane_head = lax.broadcasted_iota(jnp.int32, (stacked, width), 1) // atom_head
    own_lanes = row_head == lane_head
    few_lanes = lane_head[:QUERY_BLOCK]
    scale = atom_head ** (-0.5)
    ones = jnp.ones((KEY_WINDOW, width), BF16)

    def attend(layer, g):
        if layer != ENC_LAYERS:
            exchange(*halo(layer, g), False)
        mixed = []
        pairs = [(i, b) for i in range(gs) for b in range(blocks)]
        for start in range(0, len(pairs), 8):
            part = pairs[start : start + 8]
            scores = []
            for i, b in part:
                q = queries[g, pl.ds(i * atom_rows + b * QUERY_BLOCK, QUERY_BLOCK), :]
                q = jnp.concatenate([q] * atom_heads, axis=0)
                q = jnp.where(own_lanes, q, jnp.zeros_like(q))
                key_win = kv[layer, g, i, QUERY_BLOCK * b : QUERY_BLOCK * b + KEY_WINDOW, :width]
                score = lax.dot_general(q, key_win, LAST, preferred_element_type=F32)
                scores.append(score * scale + masked_bias[b])
            tops = [jnp.max(score, -1, keepdims=True) for score in scores]
            expos = [jnp.exp(score - top).astype(BF16) for score, top in zip(scores, tops)]
            sums = []
            for (i, b), expo in zip(part, expos):
                value_win = kv[layer, g, i, QUERY_BLOCK * b : QUERY_BLOCK * b + KEY_WINDOW, width:]
                sums.append(dot(expo, jnp.concatenate([value_win, ones], axis=1)))
            for both in sums:
                picked = both[:QUERY_BLOCK]
                number, below = picked[:, :width], picked[:, width:]
                for h in range(1, atom_heads):
                    rows = both[h * QUERY_BLOCK : (h + 1) * QUERY_BLOCK]
                    number = jnp.where(few_lanes == h, rows[:, :width], number)
                    below = jnp.where(few_lanes == h, rows[:, width:], below)
                mixed.append((number / below).astype(BF16))
        mixed = jnp.concatenate(mixed, axis=0)
        value = stream[g].reshape(gs * atom_rows, width) + dot(mixed, w_out_ref[layer])
        normal_mid = normed(value).astype(BF16)
        gated = dot(normal_mid, w_up_ref[layer])
        gate = gated[:, : 2 * width]
        hidden = (gate / (1.0 + jnp.exp(-gate)) * gated[:, 2 * width :]).astype(BF16)
        value = value + dot(hidden, w_down_ref[layer])
        stream[g] = value.reshape(gs, atom_rows, width)
        return value

    def pool_copy(g):
        return (
            remote(
                psend.at[g, 1], precv.at[g, 0], pool_send.at[0], pool_recv.at[g, 0], right
            ),
            remote(psend.at[g, 0], precv.at[g, 1], pool_send.at[1], pool_recv.at[g, 1], left),
        )

    def count_copy():
        return (
            remote(counts.at[2], counts.at[3], count_send.at[0], count_recv.at[0], right),
            remote(counts.at[0], counts.at[4], count_send.at[1], count_recv.at[1], left),
        )

    def edge_copy(g):
        return (
            remote(
                rim.at[0, g],
                edge.at[0, g],
                edge_send.at[0],
                edge_recv.at[g, 0],
                right,
            ),
            remote(
                rim.at[1, g],
                edge.at[1, g],
                edge_send.at[1],
                edge_recv.at[g, 1],
                left,
            ),
        )

    def token_copy():
        return (
            remote(atom_token_ref, near_token.at[0], token_send.at[0], token_recv.at[0], right),
            remote(atom_token_ref, near_token.at[1], token_send.at[1], token_recv.at[1], left),
        )

    def selects(row):
        spot = row - (me - 1) * token_rows
        return (
            lax.broadcasted_iota(jnp.int32, (3 * token_rows, atom_rows), 0) == spot
        ).astype(F32)

    def back_copy(t):
        return (
            remote(back.at[t, 1], back.at[t, 0], back_send.at[0], back_recv.at[t, 0], right),
            remote(back.at[t, 1], back.at[t, 2], back_send.at[1], back_recv.at[t, 1], left),
        )

    def take_back(g):
        t, base = (g, 0) if waves == GROUPS else (0, g * gs * token_rows)
        if waves == GROUPS:
            exchange(*back_copy(t), False)
        else:

            @pl.when(g == 0)
            def _():
                exchange(*back_copy(0), False)

        exchange(*edge_copy(g), False)
        beyond = []
        for i in range(gs):
            span = pl.ds(pl.multiple_of(base + i * token_rows, token_rows), token_rows)
            near = jnp.concatenate([back[t, j, span, :] for j in range(3)], axis=0)
            stream[g, i] += lax.dot_general(sel, near, FIRST, preferred_element_type=F32)
            for side, rows in ((0, slice(atom_rows - RIM, atom_rows)), (1, slice(0, RIM))):
                picked = lax.dot_general(
                    near_sel[side], near, FIRST, preferred_element_type=F32
                )
                beyond.append(edge[side, g, i].astype(F32) + picked[rows])
        project(ENC_LAYERS, g)
        normal = normed(jnp.concatenate(beyond, axis=0)).astype(BF16)
        key_value = dot(normal, w_qkv_ref[ENC_LAYERS, :, width:]).astype(BF16)
        for i in range(gs):
            at = 2 * i * RIM
            kv[ENC_LAYERS, g, i, 0:RIM, :] = key_value[at : at + RIM]
            kv[ENC_LAYERS, g, i, RIM + atom_rows :, :] = key_value[at + RIM : at + 2 * RIM]

    def run_pair(first, finish):
        def step(g, c):
            if first == ENC_LAYERS:
                take_back(g)
            attend(first, g)
            project(first + 1, g)
            send_halo(first + 1, g)
            if first == 0:
                for group in range(GROUPS):

                    @pl.when(g == group)
                    def _():
                        met(2 + group)

            return c

        lax.fori_loop(0, GROUPS, step, 0)
        if first == 0:
            for number in range(2 + GROUPS, rounds):
                met(number)
            lax.fori_loop(1, n, pair_start, 0)

        def last(g, c):
            finish(g, attend(first + 1, g))
            return c

        lax.fori_loop(0, GROUPS, last, 0)

    for s in range(gs):
        embed(s)
    loads["qkv"].wait()
    project(0, 0)
    await_signals(barrier, 1)
    signal(ready.at[0], 1)
    send_halo(0, 0)
    for s in range(gs, samples):
        embed(s)
    project(0, 1)
    send_halo(0, 1)
    met(0)
    loads["atom_token"].wait()
    selector = selects(atom_token_ref[...])
    sel = selector.astype(BF16)
    counted = jnp.broadcast_to(jnp.sum(selector, 1, keepdims=True), (3 * token_rows, 128))
    for j in range(3):
        counts[j] = counted[j * token_rows : (j + 1) * token_rows].astype(BF16)

    exchange(*count_copy(), True)
    exchange(*token_copy(), True)

    def pair_copy(target, slot):
        return remote(
            pair_out.at[(target * per) // samples],
            pair_buf.at[slot],
            pair_send,
            pair_recv,
            target,
        )

    def pair_start(k, c):
        pair_copy(lax.rem(me + k, n), me).start()
        return c

    loads["pair"].wait()
    rows = pair_own[...]
    pair_out[...] = (rows - jnp.max(rows, -1, keepdims=True)).astype(BF16)
    pair_buf[me] = pair_out[own_head]

    def pool(g, value):
        pooled = jnp.maximum(dot(normed(value).astype(BF16), w_pool_ref[...]), 0.0)
        high = pooled.astype(BF16)
        low = (pooled - high.astype(F32)).astype(BF16)
        for i in range(gs):
            at = slice(i * atom_rows, (i + 1) * atom_rows)
            part = dot(sel, high[at]) + dot(sel, low[at])
            psend[g, 0, i] = part[:token_rows].astype(BF16)
            own_sum[g, i] = part[token_rows : 2 * token_rows]
            psend[g, 1, i] = part[2 * token_rows :].astype(BF16)
        exchange(*pool_copy(g), True)
        for i in range(gs):
            rim[0, g, i] = stream[g, i, atom_rows - RIM :, :].astype(BF16)
            rim[1, g, i] = stream[g, i, :RIM, :].astype(BF16)
        exchange(*edge_copy(g), True)

    loads["bias"].wait()
    loads["edges"].wait()
    place = lax.broadcasted_iota(jnp.int32, (1, KEY_WINDOW), 1)
    for b in range(blocks):
        position = me * atom_rows - RIM + QUERY_BLOCK * b + place
        allowed = (position >= edges_ref[0, b]) & (position < edges_ref[1, b])
        masked_bias[b] = jnp.where(
            allowed, bias_ref[b].reshape(atom_heads * QUERY_BLOCK, KEY_WINDOW), -1e30
        )

    @pl.when(jnp.logical_not(has_left))
    def _():
        for layer in range(LAYERS):
            for g in range(GROUPS):
                kv[layer, g, :, 0:RIM, :] = jnp.zeros((gs, RIM, 2 * width), BF16)
        for g in range(GROUPS):
            precv[g, 0] = jnp.zeros(precv.shape[2:], BF16)
        for t in range(waves):
            back[t, 0] = jnp.zeros(back.shape[2:], BF16)
        counts[3] = jnp.zeros(counts.shape[1:], BF16)
        edge[0] = jnp.zeros(edge.shape[1:], BF16)
        near_token[0] = jnp.full((1, atom_rows), -tokens, jnp.int32)

    @pl.when(jnp.logical_not(has_right))
    def _():
        for layer in range(LAYERS):
            for g in range(GROUPS):
                kv[layer, g, :, RIM + atom_rows :, :] = jnp.zeros((gs, RIM, 2 * width), BF16)
        for g in range(GROUPS):
            precv[g, 1] = jnp.zeros(precv.shape[2:], BF16)
        for t in range(waves):
            back[t, 2] = jnp.zeros(back.shape[2:], BF16)
        counts[4] = jnp.zeros(counts.shape[1:], BF16)
        edge[1] = jnp.zeros(edge.shape[1:], BF16)
        near_token[1] = jnp.full((1, atom_rows), -tokens, jnp.int32)

    for name in ("out", "up", "down", "pool"):
        loads[name].wait()
    met(1)
    run_pair(0, pool)
    loads["single"].wait()
    loads["back"].wait()

    exchange(*count_copy(), False)
    number_of = (
        counts[1].astype(F32)[:, :1] + counts[3].astype(F32)[:, :1] + counts[4].astype(F32)[:, :1]
    )
    lanes = 128
    half = lanes // 2
    main = lanes - 2 * head_size
    rest = head_size - main
    lane = lax.broadcasted_iota(jnp.int32, (token_rows, lanes), 1)

    def moved(block, start, to, size=head_size):
        tile, off = start // lanes, start % lanes
        shift = (to - off) % lanes

        def turned(t):
            part = block[:, t * lanes : (t + 1) * lanes]
            return part if shift == 0 else pltpu.roll(part, shift, 1)

        if off + size <= lanes:
            return turned(tile)
        return jnp.where(lane < to + lanes - off, turned(tile), turned(tile + 1))

    def spread(copy_of):
        for target in far_first():
            copy_of(target, me).start()

    others = pl.ds(0, n - 1)

    def every_pair():
        return remote(
            pair_buf.at[others], pair_buf.at[others], pair_send, pair_recv, right
        )

    rows_of = item_rows(token_rows, pack, waves)
    starts = (0, rows_of[0])

    def item_copy(t):
        span = pl.ds(starts[t], rows_of[t])
        return lambda target, slot: remote(
            items.at[target, :, span], got.at[slot, :, span], item_send, item_recv.at[t], target
        )

    def every_item(t):
        span = pl.ds(starts[t], rows_of[t])
        return remote(
            items.at[others, :, span], got.at[others, :, span], item_send, item_recv.at[t], right
        )

    def out_copy(t):
        return lambda target, slot: remote(
            outs.at[t, target], returned.at[t, slot], out_send, out_recv.at[t], target
        )

    def every_out(t):
        return remote(
            outs.at[t, others], returned.at[t, others], out_send, out_recv.at[t], right
        )

    def token_project(t):
        for g in range(GROUPS) if waves == 1 else (t,):
            exchange(*pool_copy(g), False)
        for a in range(wave_samples):
            s = t * wave_samples + a
            g, i = s // gs, s % gs
            sums = own_sum[g, i] + precv[g, 0, i].astype(F32) + precv[g, 1, i].astype(F32)
            token_in[s * token_rows : (s + 1) * token_rows, :] = (
                sums / number_of + token_single_ref[...]
            )
        normal_tok = normed(token_in[t * wave_rows : (t + 1) * wave_rows, :]).astype(BF16)
        parts = [
            dot(normal_tok, w_tqkv[:, j * channels : (j + 1) * channels]) for j in range(3)
        ]
        for h in range(heads) if waves == 1 else ():
            start = h * head_size
            for a in range(0, wave_samples, pack):
                keys = []
                for p in range(pack):
                    item = h * samples + a + p
                    owner, unit = item // per, item % per // pack
                    at = slice((a + p) * token_rows, (a + p + 1) * token_rows)
                    v = moved(parts[2][at], start, half * p)
                    q = moved(parts[0][at], start, half * (1 - p))
                    keys.append(moved(parts[1][at], start, half * (1 - p)))
                    low, high = (v, q) if p == 0 else (q, v)
                    tile = jnp.where(lane < head_size, low, jnp.where(lane < half, 1.0, high))
                    items[owner, unit, p * token_rows : (p + 1) * token_rows, :] = tile.astype(
                        BF16
                    )
                key = keys[0] if pack == 1 else jnp.where(lane < half, keys[1], keys[0])
                items[owner, unit, pack * token_rows :, :] = key.astype(BF16)
        if waves == 2:
            one, two = slice(0, token_rows), slice(token_rows, 2 * token_rows)
            for h in range(heads):
                start = h * head_size
                mixed = []
                for upper, lower, at in ((0, 1, one), (1, 0, two)):
                    low = moved(parts[upper][one], start, 0)
                    mid = moved(parts[lower][two], start, head_size)
                    high = moved(parts[2][at], start, 2 * head_size, main)
                    tile = jnp.where(lane < head_size, low, jnp.where(lane < 2 * head_size, mid, high))
                    mixed.append(tile)
                at = starts[t]
                items[h, 0, at : at + 2 * token_rows, :] = jnp.concatenate(mixed, axis=0).astype(BF16)
                tail = jnp.where(
                    lane < rest,
                    moved(parts[2][one], start + main, 0, rest),
                    moved(parts[2][two], start + main, half - rest, rest),
                )
                near, far = tail[: token_rows // 2], tail[token_rows // 2 :]
                tail = jnp.where(lane[: token_rows // 2] < half, near, pltpu.roll(far, half, 1))
                items[h, 0, at + 2 * token_rows : at + rows_of[t], :] = tail.astype(BF16)
        spread(item_copy(t))
        span = pl.ds(starts[t], rows_of[t])
        got[me, :, span] = items[me, :, span]

    token_scale = head_size ** (-0.5)
    tile = 16
    key_lane = lax.broadcasted_iota(jnp.int32, (tokens, lanes), 1)
    out_lane = lax.broadcasted_iota(jnp.int32, (tile * token_rows, lanes), 1)

    def token_attend(t):
        every_item(t).wait_recv()
        for unit in range(units):
            packed = got[:, unit, pack * token_rows :, :].reshape(tokens, lanes)

            def one(block, c):
                span = pl.ds(block * tile, tile)
                ratios = []
                for p in range(pack):
                    at = slice(p * token_rows, (p + 1) * token_rows)
                    mine = key_lane < head_size
                    if p == 0:
                        mine = (key_lane >= half) & (key_lane < half + head_size)
                    keys = jnp.where(mine, packed, jnp.zeros_like(packed))
                    values = got[:, unit, at, :].reshape(tokens, lanes)
                    q = got[span, unit, at, :].reshape(tile * token_rows, lanes)
                    scores = lax.dot_general(q, keys, LAST, preferred_element_type=F32)
                    scores = scores * token_scale + pair_buf[span].astype(F32).reshape(
                        tile * token_rows, tokens
                    )
                    expo = jnp.exp(scores - jnp.max(scores, -1, keepdims=True)).astype(BF16)
                    both = dot(expo, values)
                    ratios.append(both / both[:, head_size : head_size + 1])
                ratio = ratios[0] if pack == 1 else jnp.where(out_lane < half, *ratios)
                outs[t, span, unit, :, :] = ratio.astype(BF16).reshape(tile, token_rows, lanes)
                return c

            if n == tile:
                one(0, 0)
            else:
                lax.fori_loop(0, n // tile, one, 0)
        spread(out_copy(t))
        returned[t, me] = outs[t, me]

    all_lane = lax.broadcasted_iota(jnp.int32, (tokens, lanes), 1)

    def token_pair(t):
        every_item(t).wait_recv()
        at = starts[t]
        one = got[:, 0, at : at + token_rows, :].reshape(tokens, lanes)
        two = got[:, 0, at + token_rows : at + 2 * token_rows, :].reshape(tokens, lanes)
        tail = got[:, 0, at + 2 * token_rows : at + rows_of[t], :].astype(F32)
        flat = tail.reshape(n * token_rows // 2, lanes)
        tail = jnp.concatenate(
            [tail, pltpu.roll(flat, half, 1).reshape(tail.shape)], axis=1
        ).reshape(tokens, lanes)
        tail = jnp.where(all_lane < half, tail, 1.0).astype(BF16)
        bias = pair_buf[...].astype(F32).reshape(tokens, tokens)
        ratios = []
        for a, (q, k) in enumerate(((one, two), (two, one))):
            mine = (all_lane >= a * head_size) & (all_lane < (a + 1) * head_size)
            keys = jnp.where(mine, k, jnp.zeros_like(k))
            scores = lax.dot_general(q, keys, LAST, preferred_element_type=F32)
            scores = scores * token_scale + bias
            expo = jnp.exp(scores - jnp.max(scores, -1, keepdims=True)).astype(BF16)
            both = dot(expo, jnp.concatenate([q, tail], axis=1))
            ratios.append(both / both[:, lanes + half : lanes + half + 1])
        first, second = ratios
        out = jnp.where(
            all_lane >= lanes - main,
            first[:, :lanes],
            jnp.where(
                all_lane < rest,
                first[:, lanes:],
                jnp.where(
                    all_lane < half - rest,
                    pltpu.roll(second[:, :lanes], half - rest, 1),
                    second[:, lanes:],
                ),
            ),
        )
        outs[t, :, 0, :, :] = out.astype(BF16).reshape(n, token_rows, lanes)
        spread(out_copy(t))
        returned[t, me] = outs[t, me]

    def token_finish(t):
        every_out(t).wait_recv()
        state = token_in[t * wave_rows : (t + 1) * wave_rows, :]
        if waves == 2:
            samples_mixed = []
            for a in range(wave_samples):
                begin = half - main - rest if a else lanes - main
                tiles = [None] * (channels // lanes)
                for h in range(heads):
                    low = h * head_size
                    block = returned[t, h, 0].astype(F32)
                    turned = pltpu.roll(block, (low - begin) % lanes, 1)
                    for j in range(low // lanes, (low + head_size - 1) // lanes + 1):
                        above = lane + j * lanes >= low
                        tiles[j] = turned if tiles[j] is None else jnp.where(above, turned, tiles[j])
                samples_mixed.append(jnp.concatenate(tiles, axis=1))
            mixed = jnp.concatenate(samples_mixed, axis=0).astype(BF16)
            state = state + dot(mixed, w_tout[...])
        for h in range(heads) if waves == 1 else ():
            mix = []
            for a in range(wave_samples):
                item = h * samples + t * wave_samples + a
                owner, unit, p = item // per, item % per // pack - t * units, item % per % pack
                block = returned[t, owner, unit]
                if p == 1:
                    block = pltpu.roll(block.astype(F32), half, 1).astype(BF16)
                mix.append(block[:, :head_size])
            state = state + dot(
                jnp.concatenate(mix, axis=0), w_tout[h * head_size : (h + 1) * head_size, :]
            )
        for a in range(wave_samples):
            state_ref[t * wave_samples + a] = state[a * token_rows : (a + 1) * token_rows]
        back[t, 1] = dot(normed(state).astype(BF16), w_back_ref[...]).astype(BF16)
        exchange(*back_copy(t), True)

    loads["tqkv"].wait()
    for t in range(waves):
        token_project(t)
    every_pair().wait_recv()
    if waves == 1:
        token_attend(0)
    else:
        for t in range(waves):
            token_pair(t)
    loads["tout"].wait()
    for t in range(waves):
        token_finish(t)
    first = ENC_LAYERS

    def finish(g, value):
        normal = normed(value).astype(BF16)
        for i in range(gs):
            s = g * gs + i
            update = lax.dot_general(
                w_final_ref[...],
                normal[i * atom_rows : (i + 1) * atom_rows],
                LAST,
                preferred_element_type=F32,
            )
            sigma, total = sigma_of(s)
            result = (
                SIGMA_DATA * SIGMA_DATA / total * noisy_of(s, sigma)
                + sigma * SIGMA_DATA * lax.rsqrt(total) * update
            ) / SIGMA_DATA
            for c in range(3):
                denoised_ref[c, pl.ds(s, 1), :] = result[c : c + 1]

    loads["final"].wait()
    exchange(*token_copy(), False)
    sent(
        remote(
            rim.at[0], edge.at[0], edge_send.at[0], edge_recv.at[0, 0], right
        ),
        remote(
            rim.at[1], edge.at[1], edge_send.at[1], edge_recv.at[0, 1], left
        ),
    )
    near_sel = [selects(near_token[side]).astype(BF16) for side in range(2)]
    run_pair(first, finish)

    sent(
        remote(
            kv.at[pl.ds(0, LAYERS - 1), :, :, pl.ds(0, RIM), :],
            kv.at[pl.ds(0, LAYERS - 1), :, :, pl.ds(0, RIM), :],
            halo_send.at[0],
            halo_recv.at[0, 0, 0],
            right,
        ),
        remote(
            kv.at[pl.ds(0, LAYERS - 1), :, :, pl.ds(0, RIM), :],
            kv.at[pl.ds(0, LAYERS - 1), :, :, pl.ds(0, RIM), :],
            halo_send.at[1],
            halo_recv.at[0, 0, 1],
            left,
        ),
    )
    sent(*count_copy())
    sent(*token_copy())
    sent(
        remote(psend.at[:, 1], precv.at[:, 0], pool_send.at[0], pool_recv.at[0, 0], right),
        remote(psend.at[:, 0], precv.at[:, 1], pool_send.at[1], pool_recv.at[0, 1], left),
    )
    sent(
        remote(back.at[:, 1], back.at[:, 0], back_send.at[0], back_recv.at[0, 0], right),
        remote(back.at[:, 1], back.at[:, 2], back_send.at[1], back_recv.at[0, 1], left),
    )
    every_pair().wait_send()
    for t in range(waves):
        every_item(t).wait_send()
        every_out(t).wait_send()


def store(denoised_ref, state_ref, denoised_out, state_out, sem):
    copies = (
        pltpu.make_async_copy(state_ref, state_out, sem.at[0]),
        pltpu.make_async_copy(denoised_ref, denoised_out, sem.at[1]),
    )
    for copy in copies:
        copy.start()
    for copy in copies:
        copy.wait()


def shards(
    n,
    x_true,
    noise,
    noise_level,
    atom_single,
    atom_token,
    window_edges,
    atom_pair_bias,
    token_single,
    pair_bias,
    w_coord,
    w_atom_qkv,
    w_atom_out,
    w_atom_up,
    w_atom_down,
    w_pool,
    w_token_qkv,
    w_token_out,
    w_back,
    w_final,
):
    samples = noise.shape[0]
    atom_rows, width = atom_single.shape
    token_rows, channels = token_single.shape
    blocks, atom_heads = atom_pair_bias.shape[:2]
    heads = pair_bias.shape[0]
    gs = samples // GROUPS
    per, pack, waves, units = plan(n, heads, samples)
    vmem = pl.BlockSpec(memory_space=pltpu.VMEM)
    anywhere = pl.BlockSpec(memory_space=pl.ANY)
    dma = pltpu.SemaphoreType.DMA
    held = pl.pallas_call(
        functools.partial(kernel, n),
        name="denoise",
        out_shape=(
            pltpu.VMEM((3, samples, atom_rows), F32),
            pltpu.VMEM((samples, token_rows, channels), F32),
        ),
        in_specs=[anywhere] * 19,
        out_specs=(vmem, vmem),
        scratch_shapes=[
            pltpu.SMEM((samples,), jnp.int32),
            pltpu.SMEM((2, blocks), jnp.int32),
            pltpu.VMEM(x_true.shape, F32),
            pltpu.VMEM((3, samples, atom_rows), F32),
            pltpu.VMEM(atom_single.shape, BF16),
            pltpu.VMEM((1, atom_rows), jnp.int32),
            pltpu.VMEM(w_coord.shape, F32),
            pltpu.VMEM(w_final.shape, BF16),
            pltpu.VMEM((GROUPS, gs, atom_rows, width), F32),
            pltpu.VMEM((2, GROUPS, gs, RIM, width), BF16),
            pltpu.VMEM((2, GROUPS, gs, RIM, width), BF16),
            pltpu.VMEM((2, 1, atom_rows), jnp.int32),
            pltpu.VMEM((LAYERS, GROUPS, gs, atom_rows + 2 * RIM, 2 * width), BF16),
            pltpu.VMEM((GROUPS, gs * atom_rows, width), BF16),
            pltpu.VMEM((blocks, atom_heads * QUERY_BLOCK, KEY_WINDOW), F32),
            pltpu.VMEM((5, token_rows, 128), BF16),
            pltpu.VMEM((GROUPS, gs, token_rows, channels), F32),
            pltpu.VMEM((GROUPS, 2, gs, token_rows, channels), BF16),
            pltpu.VMEM((GROUPS, 2, gs, token_rows, channels), BF16),
            pltpu.VMEM((samples * token_rows, channels), F32),
            pltpu.VMEM((n, units, sum(item_rows(token_rows, pack, waves)), 128), BF16),
            pltpu.VMEM((n, units, sum(item_rows(token_rows, pack, waves)), 128), BF16),
            pltpu.VMEM(pair_bias.shape, F32),
            pltpu.VMEM(pair_bias.shape, BF16),
            pltpu.VMEM((n, token_rows, n * token_rows), BF16),
            pltpu.VMEM((waves, n, units, token_rows, 128), BF16),
            pltpu.VMEM((waves, n, units, token_rows, 128), BF16),
            pltpu.VMEM((waves, 3, samples // waves * token_rows, width), BF16),
            pltpu.VMEM(w_token_qkv.shape, BF16),
            pltpu.VMEM(w_token_out.shape, BF16),
            pltpu.VMEM(atom_pair_bias.shape, F32),
            pltpu.VMEM(token_single.shape, F32),
            pltpu.VMEM(w_atom_qkv.shape, BF16),
            pltpu.VMEM(w_atom_out.shape, BF16),
            pltpu.VMEM(w_atom_up.shape, BF16),
            pltpu.VMEM(w_atom_down.shape, BF16),
            pltpu.VMEM(w_pool.shape, BF16),
            pltpu.VMEM(w_back.shape, BF16),
            dma((19,)),
            pltpu.SemaphoreType.REGULAR((reach_rounds(n),)),
            dma((2,)),
            dma((LAYERS - 1, GROUPS, 2)),
            dma((2,)),
            dma((2,)),
            dma((2,)),
            dma((GROUPS, 2)),
            dma(()),
            dma(()),
            dma(()),
            dma((waves,)),
            dma(()),
            dma((waves,)),
            dma((2,)),
            dma((waves, 2)),
            dma((2,)),
            dma((GROUPS, 2)),
            dma((2,)),
            dma((2,)),
        ],
        compiler_params=pltpu.CompilerParams(
            collective_id=0,
            has_side_effects=True,
            vmem_limit_bytes=56 * 1024 * 1024,
        ),
    )(
        noise_level,
        window_edges.T,
        x_true,
        noise.transpose(1, 0, 2),
        atom_single,
        atom_token.reshape(1, atom_rows),
        atom_pair_bias,
        token_single,
        pair_bias,
        w_coord,
        w_atom_qkv,
        w_atom_out,
        w_atom_up,
        w_atom_down,
        w_pool,
        w_token_qkv,
        w_token_out,
        w_back,
        w_final,
    )
    denoised, state = pl.pallas_call(
        store,
        name="store",
        out_shape=(
            jax.ShapeDtypeStruct((3, samples, atom_rows), F32),
            jax.ShapeDtypeStruct((samples, token_rows, channels), F32),
        ),
        in_specs=[vmem] * 2,
        out_specs=(anywhere, anywhere),
        scratch_shapes=[dma((2,))],
    )(*[pltpu.with_memory_space_constraint(x, pltpu.VMEM) for x in held])
    return denoised.transpose(1, 0, 2), state


def solution(mesh):
    in_specs = (
        P(None, ("groups", "seq")),
        P("groups", None, "seq"),
        P("groups"),
        P(("groups", "seq"), None),
        P(("groups", "seq")),
        P(("groups", "seq"), None),
        P(("groups", "seq"), None, None, None),
        P(("groups", "seq"), None),
        P("groups", "seq", None),
    ) + (P(),) * 10
    out_specs = (P("groups", None, "seq"), P("groups", "seq", None))
    return jax.shard_map(
        functools.partial(shards, mesh.shape["seq"]),
        mesh=mesh,
        in_specs=in_specs,
        out_specs=out_specs,
        check_vma=False,
    )
```
